32 devices in a mesh: grp: 4 (over y, core), ctx: 2 (over x), tp: 4 (over z).
Axes of the slice: x: 2, y: 2, z: 4, core: 2. Of those that a mesh axis runs over, the one named last changes fastest.
Arguments:
- state: float32 [4, 32, 5120], P(None, 'ctx', ('grp', 'tp')), may hold values from -6 to 6
- clean_tokens: bfloat16 [32, 5120], P('ctx', ('grp', 'tp')), may hold values from -6 to 6
- w_query: bfloat16 [5120, 4096], P('ctx', ('grp', 'tp')), may hold values from -0.078125 to 0.078125
- w_key: bfloat16 [5120, 4096], P('ctx', ('grp', 'tp')), may hold values from -0.078125 to 0.078125
- w_value: bfloat16 [5120, 4096], P('ctx', ('grp', 'tp')), may hold values from -0.078125 to 0.078125
- w_out: bfloat16 [4096, 5120], P(('grp', 'tp'), 'ctx'), may hold values from -0.09375 to 0.09375
- cache_keys: bfloat16 [1024, 4096], P('ctx', ('grp', 'tp')), may hold values from -200 to 200
- cache_values: bfloat16 [1024, 4096], P('ctx', ('grp', 'tp')), may hold values from -6 to 6
- norm_gain: float32 [5120], P(('grp', 'tp')), may hold values from 0.25 to 1.75
- mod_gain: float32 [5120], P(('grp', 'tp')), may hold values from -3 to 3
- out_gain: float32 [5120], P(('grp', 'tp')), may hold values from 0.1 to 1.9
- levels: float32 [50], replicated, may hold values from 0.05 to 1
- noise_index: int32 [4], replicated, may hold values from 0 to 47
- placement: int32 [4], P('ctx'), may hold values from 0 to 3, each once
- group_mask: int32 [4, 4], replicated, may hold values 0 or 1
Outputs:
- new_state: float32 [4, 32, 5120], P(None, 'ctx', ('grp', 'tp'))
- new_keys: bfloat16 [32, 4096], P('ctx', ('grp', 'tp'))
- new_values: bfloat16 [32, 4096], P('ctx', ('grp', 'tp'))
The draws below stay inside these ranges and needn't reach their ends.
All inputs are finite; a program needn't handle non-finite values.
Results may differ from the reference program's by a relative error of at most 0.0062.
The reference program's roundings to bfloat16 on the way count: a program that leaves them out, or rounds other values in their place, can miss the bound.
Values may be sent and summed in bfloat16 or wider, within the bound.
A program may use at most 64 MiB of HBM per device.

```python
import math
import jax
import jax.numpy as jnp
from jax import lax

D = 5120
HEADS = 32
HD = 128
FLIGHT = 4
STEPS = 1
LEVELS = 50
SLOT = 256
GROUP = 32
CACHE = 1024
CACHE_GROUPS = 4


def draw_cache_keys(key, part):
    width = HEADS * HD
    base_key = jax.random.fold_in(jax.random.fold_in(key, 11), 0)
    values = jnp.clip(jax.random.normal(base_key, (CACHE, width), jnp.float32), -6.0, 6.0)
    return values.astype(jnp.bfloat16)


def touch_ends(array, stream_key, least, top_value):
    extent = array.shape
    place = [jax.random.randint(jax.random.fold_in(stream_key, axis), (), 0, extent[axis]) for axis in range(len(extent))]
    array = array.at[tuple(place)].set(least)
    longest = extent.index(max(extent))
    place[longest] = (place[longest] + 1) % extent[longest]
    return array.at[tuple(place)].set(top_value)


def block_levels(rng, extent, cuts, low, top_value):
    def one(position, blocks):
        heights = jax.random.uniform(jax.random.fold_in(jax.random.fold_in(rng, 6), position), (blocks,), jnp.float32, low / len(cuts), top_value / len(cuts))
        return jnp.repeat(jnp.exp(heights), extent[position] // blocks).reshape((-1,) + (1,) * (len(extent) - position - 1))

    gain = one(*cuts[0])
    for cut in cuts[1:]:
        gain = gain * one(*cut)
    return gain


def centred(own_key, extent, scale, limit, cuts=(), kind=jnp.bfloat16):
    array = jax.random.normal(own_key, extent, jnp.float32) * scale
    if len(cuts) > 0:
        array = block_levels(own_key, extent, cuts, -0.22, 0.18) * array
    return jnp.clip(array, min=-limit, max=limit).astype(kind)


def setup_inputs(seed: int = 0) -> dict:
    streams_of = jax.random.split(jax.random.key(seed), 16)
    return {
        "state": centred(streams_of[0], (FLIGHT, GROUP, D), 1.0, 6.0, ((1, 2), (2, 16)), jnp.float32),
        "clean_tokens": centred(streams_of[1], (GROUP, D), 1.0, 6.0, ((0, 2), (1, 16))),
        "w_query": centred(streams_of[2], (D, HEADS * HD), D ** -0.5, 0.078125, ((0, 2), (1, 16))),
        "w_key": centred(streams_of[3], (D, HEADS * HD), D ** -0.5, 0.078125, ((0, 2), (1, 16))),
        "w_value": centred(streams_of[4], (D, HEADS * HD), D ** -0.5, 0.078125, ((0, 2), (1, 16))),
        "w_out": centred(streams_of[5], (HEADS * HD, D), (HEADS * HD) ** -0.5, 0.09375, ((0, 16), (1, 2))),
        "cache_keys": draw_cache_keys(jax.random.fold_in(streams_of[15], 71), 0),
        "cache_values": centred(streams_of[7], (CACHE, HEADS * HD), 1.0, 6.0, ((0, 2), (1, 16))),
        "norm_gain": jnp.clip(1.0 + 0.15 * jax.random.normal(streams_of[8], (D,), jnp.float32), 0.25, 1.75),
        "mod_gain": centred(streams_of[9], (D,), 1.0, 3.0, ((0, 16),), jnp.float32),
        "out_gain": jnp.clip(1.0 + 0.18 * jax.random.normal(streams_of[10], (D,), jnp.float32), 0.1, 1.9),
        "levels": jnp.clip(jax.random.uniform(streams_of[11], (LEVELS,), jnp.float32, 0.05, 1.0), 0.05, 1.0),
        "noise_index": touch_ends(jax.random.randint(streams_of[12], (FLIGHT,), 0, LEVELS - 2), jax.random.fold_in(streams_of[12], 1), 0, (LEVELS - 2) - 1).astype(jnp.int32),
        "placement": jax.random.permutation(streams_of[13], CACHE_GROUPS).astype(jnp.int32),
        "group_mask": touch_ends((jax.random.randint(streams_of[14], (FLIGHT, CACHE_GROUPS), 0, 4) < 3).astype(jnp.int32), jax.random.fold_in(streams_of[14], 1), 0, 1),
    }


epsilon = 1e-06

def normalize(rows, sigma_rows, norm_gain, mod_gain):
    mean_square = lax.optimization_barrier(jnp.mean(rows * rows, axis=1))
    inverse = lax.rsqrt(mean_square + epsilon)
    scaled = rows * inverse[:, None] * norm_gain[None, :] * (1.0 + sigma_rows[:, None] * mod_gain[None, :])
    return scaled.astype(jnp.bfloat16)

def attend(queries, keys, values, seen):
    scale = 1.0 / math.sqrt(HD)

    def one_head(operands):
        query_head, key_head, value_head = operands
        scores = jnp.dot(query_head, key_head.T, preferred_element_type=jnp.float32) * scale
        masked = jnp.where(seen, scores, -jnp.inf)
        peak = lax.optimization_barrier(jnp.max(masked, axis=1, keepdims=True))
        weights = jnp.where(seen, jnp.exp(scores - peak), 0.0).astype(jnp.bfloat16)
        numer = jnp.dot(weights, value_head, preferred_element_type=jnp.float32)
        denom = lax.optimization_barrier(jnp.sum(weights.astype(jnp.float32), axis=1, keepdims=True))
        return (numer / denom).astype(jnp.bfloat16)
    outputs = lax.map(one_head, (queries, keys, values))
    return jnp.transpose(outputs, (1, 0, 2)).reshape(queries.shape[1], HEADS * HD)

def by_heads(matrix):
    return jnp.transpose(matrix.reshape(matrix.shape[0], HEADS, HD), (1, 0, 2))

def reference(state, clean_tokens, w_query, w_key, w_value, w_out, cache_keys, cache_values, norm_gain, mod_gain, out_gain, levels, noise_index, placement, group_mask):
    rows_count = FLIGHT * GROUP
    clean_h = normalize(clean_tokens.astype(jnp.float32), jnp.zeros((GROUP,), jnp.float32), norm_gain, mod_gain)
    new_keys = jnp.dot(clean_h, w_key, preferred_element_type=jnp.float32).astype(jnp.bfloat16)
    new_values = jnp.dot(clean_h, w_value, preferred_element_type=jnp.float32).astype(jnp.bfloat16)
    slot_time = placement[jnp.arange(CACHE, dtype=jnp.int32) // SLOT]
    cache_seen = group_mask[:, slot_time] != 0
    finished_seen = jnp.ones((FLIGHT, GROUP), dtype=bool)
    key_group = jnp.arange(rows_count, dtype=jnp.int32) // GROUP
    own_group = jnp.arange(FLIGHT, dtype=jnp.int32)
    flight_seen = key_group[None, :] <= own_group[:, None]
    seen = jnp.concatenate([cache_seen, finished_seen, flight_seen], axis=1)
    row_seen = jnp.repeat(seen, GROUP, axis=0)
    x = state.reshape(rows_count, D)
    for step in range(STEPS):
        current = levels[noise_index + step]
        following = levels[noise_index + step + 1]
        h = normalize(x, jnp.repeat(current, GROUP), norm_gain, mod_gain)
        q = jnp.dot(h, w_query, preferred_element_type=jnp.float32).astype(jnp.bfloat16)
        k = jnp.dot(h, w_key, preferred_element_type=jnp.float32).astype(jnp.bfloat16)
        v = jnp.dot(h, w_value, preferred_element_type=jnp.float32).astype(jnp.bfloat16)
        all_keys = jnp.concatenate([cache_keys, new_keys, k], axis=0)
        all_values = jnp.concatenate([cache_values, new_values, v], axis=0)
        attention = attend(by_heads(q), by_heads(all_keys), by_heads(all_values), row_seen)
        y = jnp.dot(attention, w_out, preferred_element_type=jnp.float32)
        velocity = y * lax.rsqrt(lax.optimization_barrier(jnp.mean(y * y, axis=1, keepdims=True)) + epsilon) * out_gain[None, :]
        x = x + jnp.repeat(following - current, GROUP)[:, None] * velocity
    return (x.reshape(FLIGHT, GROUP, D), new_keys, new_values)
```

```python
import functools
import math

import jax
import jax.numpy as jnp
from jax import lax
from jax.experimental import pallas as pl
from jax.experimental.pallas import tpu as pltpu
from jax.sharding import PartitionSpec as P

D = 5120
HD = 128
SLOT = 256


epsilon = 1e-06


def level_lookup(levels, indices):
    table = jnp.arange(levels.shape[0], dtype=jnp.int32)
    picked = (indices[:, None] == table[None, :]).astype(jnp.float32)
    return jnp.sum(picked * levels[None, :], axis=1)


def normalize_rows(rows, sigma_rows, norm_gain, mod_gain):
    squares = lax.psum(jnp.sum(rows * rows, axis=1), ("grp", "tp"))
    inverse = lax.rsqrt(squares / D + epsilon)
    scaled = (
        rows
        * inverse[:, None]
        * norm_gain[None, :]
        * (1.0 + sigma_rows[:, None] * mod_gain[None, :])
    )
    return lax.all_gather(scaled.astype(jnp.bfloat16), ("grp", "tp"), axis=1, tiled=True)


def local(
    state,
    clean_tokens,
    w_query,
    w_key,
    w_value,
    w_out,
    cache_keys,
    cache_values,
    norm_gain,
    mod_gain,
    out_gain,
    levels,
    noise_index,
    placement,
    group_mask,
):
    flight, ch_dev, local_width = state.shape
    ctx_count = lax.axis_size("ctx")
    group = ch_dev * ctx_count
    cache_dev = cache_keys.shape[0]
    slots_dev = cache_dev // SLOT
    heads_dev = cache_keys.shape[1] // HD
    rows_count = flight * ch_dev
    scale = 1.0 / math.sqrt(HD)
    wk_full, wv_full, wo_full = (
        lax.all_gather(w_key, "ctx", axis=0, tiled=True),
        lax.all_gather(w_value, "ctx", axis=0, tiled=True),
        lax.all_gather(w_out, "ctx", axis=1, tiled=True),
    )
    group_table = jnp.arange(group_mask.shape[1], dtype=jnp.int32)
    slot_onehot = (placement[:, None] == group_table[None, :]).astype(jnp.int32)
    slot_seen = jnp.sum(slot_onehot[None, :, :] * group_mask[:, None, :], axis=2) > 0
    cache_seen = slot_seen[:, None, None, :, None]
    own_group = jnp.arange(flight, dtype=jnp.int32)
    flight_seen = (own_group[None, :] <= own_group[:, None])[:, None, None, :, None]
    cache_k = cache_keys.reshape(slots_dev, SLOT, heads_dev, HD)
    cache_v = cache_values.reshape(slots_dev, SLOT, heads_dev, HD)
    finished_keys = None
    finished_values = None
    current = level_lookup(levels, noise_index + 0)
    following = level_lookup(levels, noise_index + 0 + 1)
    rows = state.reshape(rows_count, local_width)
    sigma_rows = jnp.repeat(current, ch_dev)
    rows = jnp.concatenate([rows, clean_tokens.astype(jnp.float32)], axis=0)
    sigma_rows = jnp.concatenate([sigma_rows, jnp.zeros((ch_dev,), jnp.float32)])
    features = normalize_rows(rows, sigma_rows, norm_gain, mod_gain)
    keys_new = jnp.dot(features, wk_full, preferred_element_type=jnp.float32).astype(jnp.bfloat16)
    values_new = jnp.dot(features, wv_full, preferred_element_type=jnp.float32).astype(jnp.bfloat16)
    finished_keys = keys_new[rows_count:]
    finished_values = values_new[rows_count:]
    keys_new = keys_new[:rows_count]
    values_new = values_new[:rows_count]
    noisy = features[:rows_count]
    pieces = lax.all_to_all(
        noisy.reshape(flight, ch_dev, -1), "ctx", split_axis=2, concat_axis=1, tiled=True
    )
    partial_q = jnp.einsum("fqd,de->fqe", pieces, w_query, preferred_element_type=jnp.float32)
    queries = lax.psum(partial_q, "ctx").astype(jnp.bfloat16)
    query_heads = queries.reshape(flight, group, heads_dev, HD)
    finished_k = finished_keys.reshape(ch_dev, heads_dev, HD)
    finished_v = finished_values.reshape(ch_dev, heads_dev, HD)
    flight_k = keys_new.reshape(flight, ch_dev, heads_dev, HD)
    flight_v = values_new.reshape(flight, ch_dev, heads_dev, HD)
    cache_scores = (
        jnp.einsum("fqhd,sthd->fqhst", query_heads, cache_k, preferred_element_type=jnp.float32)
        * scale
    )
    finished_scores = (
        jnp.einsum("fqhd,thd->fqht", query_heads, finished_k, preferred_element_type=jnp.float32)
        * scale
    )
    flight_scores = (
        jnp.einsum("fqhd,gthd->fqhgt", query_heads, flight_k, preferred_element_type=jnp.float32)
        * scale
    )
    peak = jnp.max(finished_scores, axis=3)
    peak = jnp.maximum(peak, jnp.max(jnp.where(cache_seen, cache_scores, -jnp.inf), axis=(3, 4)))
    peak = jnp.maximum(peak, jnp.max(jnp.where(flight_seen, flight_scores, -jnp.inf), axis=(3, 4)))
    peak = lax.pmax(peak, "ctx")
    cache_p = jnp.where(cache_seen, jnp.exp(cache_scores - peak[..., None, None]), 0.0).astype(
        jnp.bfloat16
    )
    finished_p = jnp.exp(finished_scores - peak[..., None]).astype(jnp.bfloat16)
    flight_p = jnp.where(flight_seen, jnp.exp(flight_scores - peak[..., None, None]), 0.0).astype(
        jnp.bfloat16
    )
    numer = jnp.einsum("fqhst,sthd->fqhd", cache_p, cache_v, preferred_element_type=jnp.float32)
    numer = numer + jnp.einsum(
        "fqht,thd->fqhd", finished_p, finished_v, preferred_element_type=jnp.float32
    )
    numer = numer + jnp.einsum(
        "fqhgt,gthd->fqhd", flight_p, flight_v, preferred_element_type=jnp.float32
    )
    denom = jnp.sum(cache_p, axis=(3, 4), dtype=jnp.float32)
    denom = denom + jnp.sum(finished_p, axis=3, dtype=jnp.float32)
    denom = denom + jnp.sum(flight_p, axis=(3, 4), dtype=jnp.float32)
    numer, denom = (
        lax.psum_scatter(
            numer.reshape(flight, group, heads_dev * HD), "ctx", scatter_dimension=1, tiled=True
        ),
        lax.psum_scatter(denom, "ctx", scatter_dimension=1, tiled=True),
    )
    attention = numer.reshape(flight, ch_dev, heads_dev, HD) / denom[..., None]
    attention = attention.astype(jnp.bfloat16).reshape(rows_count, heads_dev * HD)
    partial_y = jnp.dot(attention, wo_full, preferred_element_type=jnp.float32)
    y_rows = lax.psum_scatter(partial_y, ("grp", "tp"), scatter_dimension=1, tiled=True)
    y_squares = lax.psum(jnp.sum(y_rows * y_rows, axis=1), ("grp", "tp"))
    velocity = y_rows * lax.rsqrt(y_squares / D + epsilon)[:, None] * out_gain[None, :]
    state = state + (following - current)[:, None, None] * velocity.reshape(
        flight, ch_dev, local_width
    )
    return (state, finished_keys, finished_values)


MESH = pl.DeviceIdType.MESH
VMEM_LIMIT = 62 * 1024 * 1024


def remote(src, dst, send, recv, device):
    return pltpu.make_async_remote_copy(
        src_ref=src,
        dst_ref=dst,
        send_sem=send,
        recv_sem=recv,
        device_id=device,
        device_id_type=MESH,
    )


def row_squares(rows, lanes):
    squares = rows * rows
    count = squares.shape[0]
    if count < lanes:
        squares = jnp.concatenate(
            [squares, jnp.zeros((lanes - count, squares.shape[1]), jnp.float32)], axis=0
        )
    ones = jnp.ones((8, squares.shape[1]), jnp.float32)
    return lax.dot_general(
        ones,
        squares,
        (((1,), (1,)), ((), ())),
        precision=lax.Precision.HIGHEST,
        preferred_element_type=jnp.float32,
    )


def kernel(
    dims,
    state_hbm,
    clean_hbm,
    wq_hbm,
    wk_hbm,
    wv_hbm,
    wo_hbm,
    ck_hbm,
    cv_hbm,
    ng_hbm,
    mg_hbm,
    og_hbm,
    levels_hbm,
    noise_hbm,
    place_hbm,
    mask_hbm,
    out_ref,
    nk_ref,
    nv_ref,
    state_ref,
    clean_ref,
    ng_ref,
    mg_ref,
    og_ref,
    levels_ref,
    noise_ref,
    place_ref,
    mask_ref,
    w_buf,
    wo_buf,
    cache_buf,
    seen_buf,
    ssq_buf,
    ssy_buf,
    h_own,
    h_buf,
    acc,
    part,
    part_in,
    kv_buf,
    fin_in,
    att_buf,
    y_part,
    y_send,
    y_in1,
    v_send,
    v_in,
    z_send,
    z_in,
    local_sem,
    cache_s,
    cache_r,
    ssq_s,
    ssq_r,
    a_s,
    a_r,
    b_s,
    b_r,
    n_s,
    n_r,
    c_s,
    c_r,
    p_s,
    p_r,
    f_s,
    f_r,
    t_s,
    t_r,
    y1_s,
    y1_r,
    yv_s,
    yv_r,
    y2_s,
    y2_r,
    ssy_s,
    ssy_r,
):
    n_grp, n_ctx, n_tp = dims
    per = n_grp // n_ctx
    members = n_grp * n_tp
    flight, ch, width = state_hbm.shape
    rows_count = flight * ch
    all_rows = rows_count + ch
    cache_dev = ck_hbm.shape[0]
    lanes = ssq_buf.shape[2]
    total_rows = n_ctx * all_rows
    g, c, t = lax.axis_index("grp"), lax.axis_index("ctx"), lax.axis_index("tp")
    u, k = g // per, g % per
    j = g * n_tp + t
    other = 1 - c
    partner = (g, other, t)
    sibling = (u * per + (1 - k), c, t)
    beside = ((1 - u) * per + k, c, t)
    held = 1 - u
    at_home = u == c
    cross = ((1 - u) * per + k, other, t)

    def member(index):
        return (index // n_tp, c, index % n_tp)

    def zpeer(d):
        return (g, c, (t + d) % n_tp)

    barrier = pltpu.get_barrier_semaphore()
    for d in range(1, members):
        pl.semaphore_signal(barrier, inc=1, device_id=member((j + d) % members), device_id_type=MESH)
    pl.semaphore_signal(barrier, inc=1, device_id=partner, device_id_type=MESH)
    pl.semaphore_signal(barrier, inc=1, device_id=cross, device_id_type=MESH)

    loads = [
        pltpu.make_async_copy(wq_hbm, w_buf.at[0], local_sem.at[0]),
        pltpu.make_async_copy(wk_hbm, w_buf.at[1], local_sem.at[1]),
        pltpu.make_async_copy(wv_hbm, w_buf.at[2], local_sem.at[2]),
        pltpu.make_async_copy(wo_hbm, wo_buf, local_sem.at[3]),
    ]
    own_lanes = pl.ds(pl.multiple_of(c * HD, HD), HD)
    other_lanes = pl.ds(pl.multiple_of(other * HD, HD), HD)
    cache_loads = [
        pltpu.make_async_copy(ck_hbm.at[:, own_lanes], cache_buf.at[0, c], local_sem.at[4]),
        pltpu.make_async_copy(cv_hbm.at[:, own_lanes], cache_buf.at[1, c], local_sem.at[5]),
    ]
    small = [
        pltpu.make_async_copy(src, dst, local_sem.at[6 + i])
        for i, (src, dst) in enumerate(
            [
                (state_hbm, state_ref),
                (clean_hbm, clean_ref),
                (ng_hbm, ng_ref),
                (mg_hbm, mg_ref),
                (og_hbm, og_ref),
                (levels_hbm, levels_ref),
                (noise_hbm, noise_ref),
                (place_hbm, place_ref),
                (mask_hbm, mask_ref),
            ]
        )
    ]
    for copy in small + loads + cache_loads:
        copy.start()
    for copy in small:
        copy.wait()

    rows = jnp.concatenate(
        [state_ref[...].reshape(rows_count, width), clean_ref[...].astype(jnp.float32)], axis=0
    )
    ssq_buf[0] = row_squares(rows, lanes)[0:1]
    line = lax.broadcasted_iota(jnp.int32, (8, SLOT), 0)
    for s in range(cache_dev // SLOT):
        block = jnp.zeros((8, SLOT), jnp.float32)
        for f in range(flight):
            shown = jnp.where(mask_ref[f, place_ref[s]] != 0, 1.0, 0.0)
            block = jnp.where(line == f, shown, block)
        seen_buf[c, :, s * SLOT : (s + 1) * SLOT] = block
    pl.semaphore_wait(barrier, members + 1)

    def exchange(buf, send, recv):
        copies = [
            remote(
                buf.at[0], buf.at[d], send.at[d - 1], recv.at[d - 1], member((j + d) % members)
            )
            for d in range(1, members)
        ]
        for copy in copies:
            copy.start()
        return copies

    ssq_copies = exchange(ssq_buf, ssq_s, ssq_r)
    cache_copies = [
        remote(seen_buf.at[c], seen_buf.at[c], cache_s.at[0], cache_r.at[0], partner),
        remote(
            ck_hbm.at[:, other_lanes], cache_buf.at[0, c], cache_s.at[1], cache_r.at[1], partner
        ),
        remote(
            cv_hbm.at[:, other_lanes], cache_buf.at[1, c], cache_s.at[2], cache_r.at[2], partner
        ),
    ]
    for copy in cache_copies[:2]:
        copy.start()
    for copy in ssq_copies:
        copy.wait_recv()

    total = ssq_buf[0]
    for d in range(1, members):
        total = total + ssq_buf[d]
    inverse = lax.rsqrt(jnp.transpose(jnp.broadcast_to(total, (8, lanes)))[:all_rows, 0:1] / D + epsilon)
    modulation = mg_ref[...].reshape(1, width)
    scaled = rows * inverse * ng_ref[...].reshape(1, width)
    blocks = []
    for f in range(flight):
        sigma = levels_ref[noise_ref[f]]
        blocks.append(scaled[f * ch : (f + 1) * ch] * (1.0 + sigma * modulation))
    blocks.append(scaled[rows_count:])
    features = jnp.concatenate(blocks, axis=0).astype(jnp.bfloat16)
    h_own[...] = features

    mine = k * n_tp + t
    a_copy = remote(
        h_own, h_buf.at[mine, c], a_s.at[0], a_r.at[0], ((1 - c) * per + k, u, t)
    )
    a_copy.start()
    cache_copies[2].start()
    remote(h_own, h_buf.at[mine, held], a_s.at[0], a_r.at[0], partner).wait_recv()

    stage_b = []

    def forward(x, index, send, recv, where, device):
        copy = remote(h_buf.at[index, x], h_buf.at[index, x], send.at[where], recv.at[where], device)
        copy.start()
        stage_b.append(copy)

    def arrived(x, index, send, recv, where, device):
        remote(
            h_buf.at[index, x], h_buf.at[index, x], send.at[where], recv.at[where], device
        ).wait_recv()

    def slot_of(core, d):
        return core * n_tp + (t + n_tp - d) % n_tp

    for d in range(1, n_tp):
        forward(held, mine, b_s, b_r, d - 1, zpeer(d))
    forward(held, mine, n_s, n_r, 0, beside)
    forward(held, mine, c_s, c_r, 0, sibling)
    for d in range(1, n_tp):
        arrived(held, slot_of(k, d), b_s, b_r, d - 1, zpeer(d))
        forward(held, slot_of(k, d), n_s, n_r, d, beside)
        forward(held, slot_of(k, d), c_s, c_r, d, sibling)

    for copy in loads[:3]:
        copy.wait()

    def project(slot, i):
        lhs = h_buf[slot].reshape(total_rows, width)
        depth = pl.ds(pl.multiple_of(slot * width, 64), width)
        return jnp.dot(lhs, w_buf[i, depth, :], preferred_element_type=jnp.float32)

    for d in range(n_tp):
        slot = slot_of(k, d)
        arrived(u, slot, n_s, n_r, d, beside)
        forward(u, slot, c_s, c_r, n_tp + d, sibling)
        for i in range(3):
            acc[i] = project(slot, i) if d == 0 else acc[i] + project(slot, i)
    part_copies = []
    for d in range(n_tp):
        slot = slot_of(1 - k, d)
        arrived(held, slot, c_s, c_r, d, sibling)
        arrived(u, slot, c_s, c_r, n_tp + d, sibling)
        for i in range(3):
            if d < n_tp - 1:
                acc[i] = acc[i] + project(slot, i)
                continue
            whole = acc[i] + project(slot, i)
            for head in range(n_ctx):
                part[head, i] = whole[:, head * HD : (head + 1) * HD]
            copy = remote(part.at[other, i], part_in.at[i], p_s.at[i], p_r.at[i], partner)
            copy.start()
            part_copies.append(copy)
    for copy in cache_loads:
        copy.wait()
    for i, copy in enumerate(cache_copies):
        copy.wait_recv()
    row_group = (lax.broadcasted_iota(jnp.int32, (total_rows, 8), 0) % all_rows) // ch
    pick = (row_group == lax.broadcasted_iota(jnp.int32, (total_rows, 8), 1)).astype(jnp.bfloat16)
    seen = [
        jnp.dot(pick, seen_buf[x].astype(jnp.bfloat16), preferred_element_type=jnp.float32) > 0.5
        for x in range(n_ctx)
    ]
    query_group = (lax.broadcasted_iota(jnp.int32, (total_rows, total_rows), 0) % all_rows) // ch
    key_group = (lax.broadcasted_iota(jnp.int32, (total_rows, total_rows), 1) % all_rows) // ch
    seen.append(jnp.logical_or(key_group == flight, key_group <= query_group))

    part_copies[0].wait_recv()
    q = (part[c, 0] + part_in[0]).astype(jnp.bfloat16)
    scale = 1.0 / math.sqrt(HD)

    def score(keys):
        return (
            lax.dot_general(q, keys, (((1,), (1,)), ((), ())), preferred_element_type=jnp.float32)
            * scale
        )

    scores = [score(cache_buf[0, x]) for x in range(n_ctx)]
    part_copies[1].wait_recv()
    key = (part[c, 1] + part_in[1]).astype(jnp.bfloat16)
    scores.append(score(key))
    scores = [jnp.where(s, v, -jnp.inf) for s, v in zip(seen, scores)]
    peak = functools.reduce(
        jnp.maximum, [jnp.max(v, axis=1, keepdims=True) for v in scores]
    )
    weights = [
        jnp.where(s, jnp.exp(v - peak), 0.0).astype(jnp.bfloat16) for s, v in zip(seen, scores)
    ]
    denom = sum(jnp.sum(w.astype(jnp.float32), axis=1, keepdims=True) for w in weights)
    part_copies[2].wait_recv()
    value = (part[c, 2] + part_in[2]).astype(jnp.bfloat16)
    values = [cache_buf[1, x] for x in range(n_ctx)] + [value]
    numer = sum(
        jnp.dot(w, v, preferred_element_type=jnp.float32) for w, v in zip(weights, values)
    )
    attention = (numer / denom).astype(jnp.bfloat16)
    for x in range(n_ctx):
        att_buf[c, x * rows_count : (x + 1) * rows_count, :] = attention[
            x * all_rows : x * all_rows + rows_count
        ]
    att_copy = remote(att_buf.at[c], att_buf.at[c], t_s.at[0], t_r.at[0], partner)
    att_copy.start()

    for x in range(n_ctx):
        last = slice(x * all_rows + rows_count, (x + 1) * all_rows)
        kv_buf[x, 0] = key[last]
        kv_buf[x, 1] = value[last]
    fin_copy = remote(kv_buf.at[other], fin_in, f_s.at[0], f_r.at[0], partner)
    fin_copy.start()
    nk_ref[:, own_lanes] = kv_buf[c, 0]
    nv_ref[:, own_lanes] = kv_buf[c, 1]

    loads[3].wait()
    att_copy.wait_recv()
    both = jnp.concatenate([att_buf[x] for x in range(n_ctx)], axis=1)
    y1 = []
    for tt in range(n_tp):
        for kk in range(per):
            start = (kk * n_tp + tt) * width
            piece = jnp.dot(
                both, wo_buf[:, start : start + width], preferred_element_type=jnp.float32
            )
            for x in range(n_ctx):
                half = piece[x * rows_count : (x + 1) * rows_count]
                y_part[kk, tt, x] = half
                y_send[kk, tt, x] = half.astype(jnp.bfloat16)
        copy = remote(y_send.at[1 - k, tt], y_in1.at[tt], y1_s.at[tt], y1_r.at[tt], sibling)
        copy.start()
        y1.append(copy)
    yv = []
    near = []
    for d in range(1, n_tp + 1):
        tt = (t + d) % n_tp
        remote(
            y_send.at[1 - k, tt], y_in1.at[tt], y1_s.at[tt], y1_r.at[tt], sibling
        ).wait_recv()
        for i, x in enumerate((other, c)):
            v_send[i, d - 1] = (y_part[k, tt, x] + y_in1[tt, x].astype(jnp.float32)).astype(
                jnp.bfloat16
            )
            copy = remote(
                v_send.at[i, d - 1],
                v_in.at[u, d - 1],
                yv_s.at[i * n_tp + d - 1],
                yv_r.at[u * n_tp + d - 1],
                (c * per + k, other, t) if i == 0 else beside,
            )
            if i == 0:
                copy.start()
                yv.append(copy)
            else:
                near.append(copy)
                pl.when(jnp.logical_not(at_home))(copy.start)
    fin_copy.wait_recv()
    nk_ref[:, other_lanes] = fin_in[0]
    nv_ref[:, other_lanes] = fin_in[1]
    y2 = []
    for d in range(1, n_tp + 1):

        @pl.when(at_home)
        def _():
            v_in[u, d - 1] = v_send[1, d - 1]

        for y in range(n_ctx):

            @pl.when(jnp.logical_not(jnp.logical_and(at_home, u == y)))
            def _():
                remote(
                    v_send.at[0, d - 1],
                    v_in.at[y, d - 1],
                    yv_s.at[d - 1],
                    yv_r.at[y * n_tp + d - 1],
                    partner,
                ).wait_recv()

        summed = v_in[0, d - 1].astype(jnp.float32) + v_in[1, d - 1].astype(jnp.float32)
        if d < n_tp:
            z_send[d - 1] = summed.astype(jnp.bfloat16)
            copy = remote(
                z_send.at[d - 1], z_in.at[d - 1], y2_s.at[d - 1], y2_r.at[d - 1], zpeer(d)
            )
            copy.start()
            y2.append(copy)
    for d in range(1, n_tp):
        y2[d - 1].wait_recv()
        summed = summed + z_in[d - 1].astype(jnp.float32)
    y_rows = summed
    ssy_buf[0] = row_squares(y_rows, lanes)[0:1]
    ssy_copies = exchange(ssy_buf, ssy_s, ssy_r)
    for copy in ssq_copies + cache_copies + stage_b + part_copies + y1 + yv + y2:
        copy.wait_send()
    for copy in [a_copy, att_copy, fin_copy]:
        copy.wait_send()

    @pl.when(jnp.logical_not(at_home))
    def _():
        for copy in near:
            copy.wait_send()

    for copy in ssy_copies:
        copy.wait_recv()
    total = ssy_buf[0]
    for d in range(1, members):
        total = total + ssy_buf[d]
    inverse = lax.rsqrt(jnp.transpose(jnp.broadcast_to(total, (8, lanes)))[:rows_count, 0:1] / D + epsilon)
    velocity = y_rows * inverse * og_ref[...].reshape(1, width)
    for f in range(flight):
        now = levels_ref[noise_ref[f]]
        after = levels_ref[noise_ref[f] + 1]
        out_ref[f] = state_ref[f] + (after - now) * velocity[f * ch : (f + 1) * ch]
    for copy in ssy_copies:
        copy.wait_send()


def write_out(*refs):
    sems = refs[6]
    copies = [pltpu.make_async_copy(refs[i], refs[3 + i], sems.at[i]) for i in range(3)]
    for copy in copies:
        copy.start()
    for copy in copies:
        copy.wait()


def fused(dims, *args):
    state, clean_tokens, w_query = args[0], args[1], args[2]
    w_out, cache_keys = args[5], args[6]
    n_grp, n_ctx, n_tp = dims
    per = n_grp // n_ctx
    members = n_grp * n_tp
    flight, ch, width = state.shape
    rows_count = flight * ch
    all_rows = rows_count + ch
    total = n_ctx * all_rows
    lanes = -(-all_rows // 128) * 128
    queries = n_ctx * rows_count
    cache_dev = cache_keys.shape[0]
    bf, fl = jnp.bfloat16, jnp.float32
    dma = pltpu.SemaphoreType.DMA
    vm = pl.BlockSpec(memory_space=pltpu.VMEM)
    hbm = pl.BlockSpec(memory_space=pltpu.HBM)

    def pair(count):
        return [dma((count,))] * 2

    scratch = [
        pltpu.VMEM(state.shape, fl),
        pltpu.VMEM(clean_tokens.shape, bf),
        pltpu.VMEM((width,), fl),
        pltpu.VMEM((width,), fl),
        pltpu.VMEM((width,), fl),
        *[pltpu.SMEM(a.shape, a.dtype) for a in args[11:]],
        pltpu.VMEM((3,) + w_query.shape, bf),
        pltpu.VMEM(w_out.shape, bf),
        pltpu.VMEM((2, n_ctx, cache_dev, HD), bf),
        pltpu.VMEM((n_ctx, 8, cache_dev), fl),
        pltpu.VMEM((members, 1, lanes), fl),
        pltpu.VMEM((members, 1, lanes), fl),
        pltpu.VMEM((all_rows, width), bf),
        pltpu.VMEM((per * n_tp, n_ctx, all_rows, width), bf),
        pltpu.VMEM((3, total, n_ctx * HD), fl),
        pltpu.VMEM((n_ctx, 3, total, HD), fl),
        pltpu.VMEM((3, total, HD), fl),
        pltpu.VMEM((n_ctx, 2, ch, HD), bf),
        pltpu.VMEM((2, ch, HD), bf),
        pltpu.VMEM((n_ctx, queries, HD), bf),
        pltpu.VMEM((per, n_tp, n_ctx, rows_count, width), fl),
        pltpu.VMEM((per, n_tp, n_ctx, rows_count, width), bf),
        pltpu.VMEM((n_tp, n_ctx, rows_count, width), bf),
        pltpu.VMEM((n_ctx, n_tp, rows_count, width), bf),
        pltpu.VMEM((n_ctx, n_tp, rows_count, width), bf),
        pltpu.VMEM((n_tp - 1, rows_count, width), bf),
        pltpu.VMEM((n_tp - 1, rows_count, width), bf),
        dma((15,)),
        *pair(3),
        *pair(members - 1),
        *pair(1),
        *pair(n_tp - 1),
        *pair(n_tp),
        *pair(2 * n_tp),
        *pair(3),
        *pair(1),
        *pair(1),
        *pair(n_tp),
        *pair(n_ctx * n_tp),
        *pair(n_tp - 1),
        *pair(members - 1),
    ]
    results = pl.pallas_call(
        functools.partial(kernel, dims),
        out_shape=(
            pltpu.VMEM(state.shape, fl),
            pltpu.VMEM((ch, cache_keys.shape[1]), bf),
            pltpu.VMEM((ch, cache_keys.shape[1]), bf),
        ),
        in_specs=[hbm] * 15,
        out_specs=(vm, vm, vm),
        scratch_shapes=scratch,
        compiler_params=pltpu.CompilerParams(
            collective_id=0, has_side_effects=True, vmem_limit_bytes=VMEM_LIMIT
        ),
    )(*args)
    return pl.pallas_call(
        write_out,
        out_shape=tuple(jax.ShapeDtypeStruct(r.shape, r.dtype) for r in results),
        in_specs=[vm] * 3,
        out_specs=(hbm,) * 3,
        scratch_shapes=[dma((3,))],
    )(*[pltpu.with_memory_space_constraint(r, pltpu.VMEM) for r in results])


def step(dims, *args):
    n_grp, n_ctx, n_tp = dims
    heads_dev = args[6].shape[1] // HD
    if n_ctx == heads_dev == 2 and n_grp == 2 * n_ctx and args[0].shape[0] <= 8:
        return fused(dims, *args)
    return local(*args)


def solution(mesh):
    dims = tuple(mesh.shape[name] for name in ("grp", "ctx", "tp"))
    return jax.shard_map(
        functools.partial(step, dims),
        mesh=mesh,
        in_specs=(
            P(None, "ctx", ("grp", "tp")),
            P("ctx", ("grp", "tp")),
            P("ctx", ("grp", "tp")),
            P("ctx", ("grp", "tp")),
            P("ctx", ("grp", "tp")),
            P(("grp", "tp"), "ctx"),
            P("ctx", ("grp", "tp")),
            P("ctx", ("grp", "tp")),
            P(("grp", "tp")),
            P(("grp", "tp")),
            P(("grp", "tp")),
            P(),
            P(),
            P("ctx"),
            P(),
        ),
        out_specs=(P(None, "ctx", ("grp", "tp")), P("ctx", ("grp", "tp")), P("ctx", ("grp", "tp"))),
        check_vma=False,
    )
```

```python
import functools
import math

import jax
import jax.numpy as jnp
from jax import lax
from jax.experimental import pallas as pl
from jax.experimental.pallas import tpu as pltpu
from jax.sharding import PartitionSpec as P

D = 5120
HD = 128
SLOT = 256


epsilon = 1e-06


def level_lookup(levels, indices):
    table = jnp.arange(levels.shape[0], dtype=jnp.int32)
    picked = (indices[:, None] == table[None, :]).astype(jnp.float32)
    return jnp.sum(picked * levels[None, :], axis=1)


def normalize_rows(rows, sigma_rows, norm_gain, mod_gain):
    squares = lax.psum(jnp.sum(rows * rows, axis=1), ("grp", "tp"))
    inverse = lax.rsqrt(squares / D + epsilon)
    scaled = (
        rows
        * inverse[:, None]
        * norm_gain[None, :]
        * (1.0 + sigma_rows[:, None] * mod_gain[None, :])
    )
    return lax.all_gather(scaled.astype(jnp.bfloat16), ("grp", "tp"), axis=1, tiled=True)


def local(
    state,
    clean_tokens,
    w_query,
    w_key,
    w_value,
    w_out,
    cache_keys,
    cache_values,
    norm_gain,
    mod_gain,
    out_gain,
    levels,
    noise_index,
    placement,
    group_mask,
):
    flight, ch_dev, local_width = state.shape
    ctx_count = lax.axis_size("ctx")
    group = ch_dev * ctx_count
    cache_dev = cache_keys.shape[0]
    slots_dev = cache_dev // SLOT
    heads_dev = cache_keys.shape[1] // HD
    rows_count = flight * ch_dev
    scale = 1.0 / math.sqrt(HD)
    wk_full, wv_full, wo_full = (
        lax.all_gather(w_key, "ctx", axis=0, tiled=True),
        lax.all_gather(w_value, "ctx", axis=0, tiled=True),
        lax.all_gather(w_out, "ctx", axis=1, tiled=True),
    )
    group_table = jnp.arange(group_mask.shape[1], dtype=jnp.int32)
    slot_onehot = (placement[:, None] == group_table[None, :]).astype(jnp.int32)
    slot_seen = jnp.sum(slot_onehot[None, :, :] * group_mask[:, None, :], axis=2) > 0
    cache_seen = slot_seen[:, None, None, :, None]
    own_group = jnp.arange(flight, dtype=jnp.int32)
    flight_seen = (own_group[None, :] <= own_group[:, None])[:, None, None, :, None]
    cache_k = cache_keys.reshape(slots_dev, SLOT, heads_dev, HD)
    cache_v = cache_values.reshape(slots_dev, SLOT, heads_dev, HD)
    finished_keys = None
    finished_values = None
    current = level_lookup(levels, noise_index + 0)
    following = level_lookup(levels, noise_index + 0 + 1)
    rows = state.reshape(rows_count, local_width)
    sigma_rows = jnp.repeat(current, ch_dev)
    rows = jnp.concatenate([rows, clean_tokens.astype(jnp.float32)], axis=0)
    sigma_rows = jnp.concatenate([sigma_rows, jnp.zeros((ch_dev,), jnp.float32)])
    features = normalize_rows(rows, sigma_rows, norm_gain, mod_gain)
    keys_new = jnp.dot(features, wk_full, preferred_element_type=jnp.float32).astype(jnp.bfloat16)
    values_new = jnp.dot(features, wv_full, preferred_element_type=jnp.float32).astype(jnp.bfloat16)
    finished_keys = keys_new[rows_count:]
    finished_values = values_new[rows_count:]
    keys_new = keys_new[:rows_count]
    values_new = values_new[:rows_count]
    noisy = features[:rows_count]
    pieces = lax.all_to_all(
        noisy.reshape(flight, ch_dev, -1), "ctx", split_axis=2, concat_axis=1, tiled=True
    )
    partial_q = jnp.einsum("fqd,de->fqe", pieces, w_query, preferred_element_type=jnp.float32)
    queries = lax.psum(partial_q, "ctx").astype(jnp.bfloat16)
    query_heads = queries.reshape(flight, group, heads_dev, HD)
    finished_k = finished_keys.reshape(ch_dev, heads_dev, HD)
    finished_v = finished_values.reshape(ch_dev, heads_dev, HD)
    flight_k = keys_new.reshape(flight, ch_dev, heads_dev, HD)
    flight_v = values_new.reshape(flight, ch_dev, heads_dev, HD)
    cache_scores = (
        jnp.einsum("fqhd,sthd->fqhst", query_heads, cache_k, preferred_element_type=jnp.float32)
        * scale
    )
    finished_scores = (
        jnp.einsum("fqhd,thd->fqht", query_heads, finished_k, preferred_element_type=jnp.float32)
        * scale
    )
    flight_scores = (
        jnp.einsum("fqhd,gthd->fqhgt", query_heads, flight_k, preferred_element_type=jnp.float32)
        * scale
    )
    peak = jnp.max(finished_scores, axis=3)
    peak = jnp.maximum(peak, jnp.max(jnp.where(cache_seen, cache_scores, -jnp.inf), axis=(3, 4)))
    peak = jnp.maximum(peak, jnp.max(jnp.where(flight_seen, flight_scores, -jnp.inf), axis=(3, 4)))
    peak = lax.pmax(peak, "ctx")
    cache_p = jnp.where(cache_seen, jnp.exp(cache_scores - peak[..., None, None]), 0.0).astype(
        jnp.bfloat16
    )
    finished_p = jnp.exp(finished_scores - peak[..., None]).astype(jnp.bfloat16)
    flight_p = jnp.where(flight_seen, jnp.exp(flight_scores - peak[..., None, None]), 0.0).astype(
        jnp.bfloat16
    )
    numer = jnp.einsum("fqhst,sthd->fqhd", cache_p, cache_v, preferred_element_type=jnp.float32)
    numer = numer + jnp.einsum(
        "fqht,thd->fqhd", finished_p, finished_v, preferred_element_type=jnp.float32
    )
    numer = numer + jnp.einsum(
        "fqhgt,gthd->fqhd", flight_p, flight_v, preferred_element_type=jnp.float32
    )
    denom = jnp.sum(cache_p, axis=(3, 4), dtype=jnp.float32)
    denom = denom + jnp.sum(finished_p, axis=3, dtype=jnp.float32)
    denom = denom + jnp.sum(flight_p, axis=(3, 4), dtype=jnp.float32)
    numer, denom = (
        lax.psum_scatter(
            numer.reshape(flight, group, heads_dev * HD), "ctx", scatter_dimension=1, tiled=True
        ),
        lax.psum_scatter(denom, "ctx", scatter_dimension=1, tiled=True),
    )
    attention = numer.reshape(flight, ch_dev, heads_dev, HD) / denom[..., None]
    attention = attention.astype(jnp.bfloat16).reshape(rows_count, heads_dev * HD)
    partial_y = jnp.dot(attention, wo_full, preferred_element_type=jnp.float32)
    y_rows = lax.psum_scatter(partial_y, ("grp", "tp"), scatter_dimension=1, tiled=True)
    y_squares = lax.psum(jnp.sum(y_rows * y_rows, axis=1), ("grp", "tp"))
    velocity = y_rows * lax.rsqrt(y_squares / D + epsilon)[:, None] * out_gain[None, :]
    state = state + (following - current)[:, None, None] * velocity.reshape(
        flight, ch_dev, local_width
    )
    return (state, finished_keys, finished_values)


MESH = pl.DeviceIdType.MESH
VMEM_LIMIT = 62 * 1024 * 1024


def remote(src, dst, send, recv, device):
    return pltpu.make_async_remote_copy(
        src_ref=src,
        dst_ref=dst,
        send_sem=send,
        recv_sem=recv,
        device_id=device,
        device_id_type=MESH,
    )


def row_squares(rows, lanes):
    squares = rows * rows
    count = squares.shape[0]
    if count < lanes:
        squares = jnp.concatenate(
            [squares, jnp.zeros((lanes - count, squares.shape[1]), jnp.float32)], axis=0
        )
    ones = jnp.ones((8, squares.shape[1]), jnp.float32)
    return lax.dot_general(
        ones,
        squares,
        (((1,), (1,)), ((), ())),
        precision=lax.Precision.HIGHEST,
        preferred_element_type=jnp.float32,
    )


def kernel(
    dims,
    state_hbm,
    clean_hbm,
    wq_hbm,
    wk_hbm,
    wv_hbm,
    wo_hbm,
    ck_hbm,
    cv_hbm,
    ng_hbm,
    mg_hbm,
    og_hbm,
    levels_hbm,
    noise_hbm,
    place_hbm,
    mask_hbm,
    out_ref,
    nk_ref,
    nv_ref,
    state_ref,
    clean_ref,
    ng_ref,
    mg_ref,
    og_ref,
    levels_ref,
    noise_ref,
    place_ref,
    mask_ref,
    w_buf,
    wo_buf,
    wo_cut,
    cache_buf,
    seen_buf,
    ssq_own,
    ssq_buf,
    ssy_buf,
    raw,
    raw_in,
    h_buf,
    acc,
    q_part,
    q_in,
    kv_part,
    kv_send,
    kv_in,
    kv_buf,
    fin_in,
    att_buf,
    y_part,
    y_send,
    y_in,
    near_a,
    far_a,
    cross_a,
    za_send,
    za_in,
    zb_send,
    zb_in,
    near_b,
    far_b,
    cross_b,
    local_sem,
    cache_s,
    cache_r,
    ssq_s,
    ssq_r,
    a_s,
    a_r,
    b_s,
    b_r,
    n_s,
    n_r,
    c_s,
    c_r,
    p_s,
    p_r,
    f_s,
    f_r,
    t_s,
    t_r,
    y1_s,
    y1_r,
    fa_s,
    na_s,
    xa_r,
    za_s,
    za_r,
    zb_s,
    zb_r,
    fb_s,
    nb_s,
    xb_r,
    ssy_s,
    ssy_r,
):
    n_grp, n_ctx, n_tp = dims
    per = n_grp // n_ctx
    members = n_grp * n_tp
    flight, ch, width = state_hbm.shape
    rows_count = flight * ch
    half = rows_count // 2
    all_rows = rows_count + ch
    cache_dev = ck_hbm.shape[0]
    lanes = ssq_buf.shape[2]
    total_rows = n_ctx * all_rows
    queries = n_ctx * rows_count
    g, c, t = lax.axis_index("grp"), lax.axis_index("ctx"), lax.axis_index("tp")
    u, k = g // per, g % per
    j = g * n_tp + t
    other = 1 - c
    partner = (g, other, t)
    sibling = (u * per + (1 - k), c, t)
    beside = ((1 - u) * per + k, c, t)
    held = 1 - u
    at_home = u == c
    owner = (c * per + k, other, t)

    def member(index):
        return (index // n_tp, c, index % n_tp)

    side = t // (n_tp // 2)
    inner = t + side * (n_tp - 1 - 2 * t)
    peers = []
    for i in range(n_tp - 1):
        v = n_tp - 1 - i
        p = v - (inner - v + n_tp) // n_tp
        peers.append(p + side * (n_tp - 1 - 2 * p))
    places = [t] + peers

    def zpeer(tt):
        return (g, c, tt)

    barrier = pltpu.get_barrier_semaphore()
    for dg in range(n_grp):
        for dc in range(n_ctx):
            for dt in range(n_tp):
                if dg + dc + dt > 0:
                    pl.semaphore_signal(
                        barrier,
                        inc=1,
                        device_id=((g + dg) % n_grp, (c + dc) % n_ctx, (t + dt) % n_tp),
                        device_id_type=MESH,
                    )

    loads = [
        pltpu.make_async_copy(wq_hbm, w_buf.at[0], local_sem.at[0]),
        pltpu.make_async_copy(wk_hbm, w_buf.at[1], local_sem.at[1]),
        pltpu.make_async_copy(wv_hbm, w_buf.at[2], local_sem.at[2]),
        pltpu.make_async_copy(wo_hbm, wo_buf, local_sem.at[3]),
    ]
    own_lanes = pl.ds(pl.multiple_of(c * HD, HD), HD)
    other_lanes = pl.ds(pl.multiple_of(other * HD, HD), HD)
    cache_loads = [
        pltpu.make_async_copy(ck_hbm.at[:, own_lanes], cache_buf.at[0, c], local_sem.at[4]),
        pltpu.make_async_copy(cv_hbm.at[:, own_lanes], cache_buf.at[1, c], local_sem.at[5]),
    ]
    small = [
        pltpu.make_async_copy(src, dst, local_sem.at[6 + i])
        for i, (src, dst) in enumerate(
            [
                (state_hbm, state_ref),
                (clean_hbm, clean_ref),
                (ng_hbm, ng_ref),
                (mg_hbm, mg_ref),
                (og_hbm, og_ref),
                (levels_hbm, levels_ref),
                (noise_hbm, noise_ref),
                (place_hbm, place_ref),
                (mask_hbm, mask_ref),
            ]
        )
    ]
    for copy in small + loads + cache_loads:
        copy.start()
    for copy in small:
        copy.wait()

    rows = jnp.concatenate(
        [state_ref[...].reshape(rows_count, width), clean_ref[...].astype(jnp.float32)], axis=0
    )
    ssq_own[...] = row_squares(rows, lanes)[0:1]

    @pl.when(c == held)
    def _():
        ssq_buf[j] = ssq_own[...]

    modulation = mg_ref[...].reshape(1, width)
    gained = rows * ng_ref[...].reshape(1, width)
    for f in range(flight):
        sigma = levels_ref[noise_ref[f]]
        raw[f * ch : (f + 1) * ch] = gained[f * ch : (f + 1) * ch] * (1.0 + sigma * modulation)
    raw[rows_count:] = gained[rows_count:]
    line = lax.broadcasted_iota(jnp.int32, (8, SLOT), 0)
    for s in range(cache_dev // SLOT):
        block = jnp.zeros((8, SLOT), jnp.float32)
        for f in range(flight):
            hidden = jnp.where(mask_ref[f, place_ref[s]] != 0, 0.0, -jnp.inf)
            block = jnp.where(line == f, hidden, block)
        seen_buf[c, :, s * SLOT : (s + 1) * SLOT] = block
    pl.semaphore_wait(barrier, n_grp * n_ctx * n_tp - 1)

    ssq_copies = []
    for dk in range(per):
        for dc in range(n_ctx):
            for dt in range(n_tp):
                copy = remote(
                    ssq_own,
                    ssq_buf.at[j],
                    ssq_s.at[len(ssq_copies)],
                    ssq_r.at[j],
                    ((1 - c) * per + (k + dk) % per, (c + dc) % n_ctx, (t + dt) % n_tp),
                )
                if ssq_copies:
                    copy.start()
                else:
                    pl.when(c != held)(copy.start)
                ssq_copies.append(copy)
    a_copy = remote(raw, raw_in, a_s.at[0], a_r.at[0], ((1 - c) * per + k, u, t))
    a_copy.start()
    cache_copies = [
        remote(seen_buf.at[c], seen_buf.at[c], cache_s.at[0], cache_r.at[0], partner),
        remote(
            ck_hbm.at[:, other_lanes], cache_buf.at[0, c], cache_s.at[1], cache_r.at[1], partner
        ),
        remote(
            cv_hbm.at[:, other_lanes], cache_buf.at[1, c], cache_s.at[2], cache_r.at[2], partner
        ),
    ]
    for copy in cache_copies:
        copy.start()

    def ssq_arrival(a, b):
        source = (g + a) % n_grp * n_tp + (t + b) % n_tp
        return remote(ssq_own, ssq_buf.at[source], ssq_s.at[0], ssq_r.at[source], partner)

    for a in range(n_grp):
        for b in range(n_tp):
            if a + b > 0:
                ssq_arrival(a, b).wait_recv()
            else:
                pl.when(c != held)(ssq_arrival(a, b).wait_recv)

    total = ssq_buf[0]
    for d in range(1, members):
        total = total + ssq_buf[d]
    inverse = lax.rsqrt(jnp.transpose(jnp.broadcast_to(total, (8, lanes)))[:all_rows, 0:1] / D + epsilon)
    a_copy.wait_recv()
    mine = k * n_tp + t
    h_buf[mine, held] = (raw_in[...] * inverse).astype(jnp.bfloat16)

    stage_b = []

    def forward(x, index, send, recv, out, into, device):
        copy = remote(h_buf.at[index, x], h_buf.at[index, x], send.at[out], recv.at[into], device)
        copy.start()
        stage_b.append(copy)

    def arrived(x, index, send, recv, into, device):
        remote(
            h_buf.at[index, x], h_buf.at[index, x], send.at[0], recv.at[into], device
        ).wait_recv()

    for i, tt in enumerate(peers):
        forward(held, mine, b_s, b_r, i, t, zpeer(tt))
    forward(held, mine, n_s, n_r, 0, t, beside)
    forward(held, mine, c_s, c_r, 0, t, sibling)

    loads[3].wait()
    for block in range(per * n_tp):
        wo_cut[block] = wo_buf[:, block * width : (block + 1) * width]
    for i, tt in enumerate(peers):
        arrived(held, k * n_tp + tt, b_s, b_r, tt, zpeer(tt))
        forward(held, k * n_tp + tt, n_s, n_r, i + 1, tt, beside)
        forward(held, k * n_tp + tt, c_s, c_r, i + 1, tt, sibling)

    for copy in loads[:3]:
        copy.wait()

    def project(slot, i):
        lhs = h_buf[slot].reshape(total_rows, width)
        depth = pl.ds(pl.multiple_of(slot * width, 64), width)
        return jnp.dot(lhs, w_buf[i, depth, :], preferred_element_type=jnp.float32)

    def own_slot(i):
        tt = places[i]
        slot = k * n_tp + tt
        arrived(u, slot, n_s, n_r, tt, beside)
        forward(u, slot, c_s, c_r, n_tp + i, n_tp + tt, sibling)
        for w in range(3):
            acc[w] = project(slot, w) if i == 0 else acc[w] + project(slot, w)

    part_copies = []

    def sibling_slot(i):
        tt = places[i]
        slot = (1 - k) * n_tp + tt
        arrived(held, slot, c_s, c_r, tt, sibling)
        arrived(u, slot, c_s, c_r, n_tp + tt, sibling)
        for w in range(3):
            if i < n_tp - 1:
                acc[w] = acc[w] + project(slot, w)
                continue
            whole = acc[w] + project(slot, w)
            for head in range(n_ctx):
                piece = whole[:, head * HD : (head + 1) * HD]
                if w == 0:
                    for x in range(n_ctx):
                        q_part[head, x * rows_count : (x + 1) * rows_count] = piece[
                            x * all_rows : x * all_rows + rows_count
                        ]
                else:
                    kv_part[head, w - 1] = piece
                    kv_send[head, w - 1] = piece.astype(jnp.bfloat16)
            if w == 0:
                copy = remote(q_part.at[other], q_in, p_s.at[0], p_r.at[0], partner)
            else:
                copy = remote(
                    kv_send.at[other, w - 1], kv_in.at[w - 1], p_s.at[w], p_r.at[w], partner
                )
            copy.start()
            part_copies.append(copy)

    for i in range(n_tp):
        own_slot(i)
        if i > 0:
            sibling_slot(i - 1)
    sibling_slot(n_tp - 1)
    for copy in cache_loads:
        copy.wait()
    for copy in cache_copies:
        copy.wait_recv()
    query_group = (lax.broadcasted_iota(jnp.int32, (queries, total_rows), 0) % rows_count) // ch
    key_group = (lax.broadcasted_iota(jnp.int32, (queries, total_rows), 1) % all_rows) // ch
    flight_seen = jnp.logical_or(key_group == flight, key_group <= query_group)

    part_copies[0].wait_recv()
    q = (q_part[c] + q_in[...]).astype(jnp.bfloat16)
    scale = 1.0 / math.sqrt(HD)

    def score(keys):
        return (
            lax.dot_general(q, keys, (((1,), (1,)), ((), ())), preferred_element_type=jnp.float32)
            * scale
        )

    scores = []
    for x in range(n_ctx):
        plain = score(cache_buf[0, x])
        scores.append(
            jnp.concatenate(
                [
                    plain[b * ch : (b + 1) * ch] + seen_buf[x, b % flight : b % flight + 1]
                    for b in range(n_ctx * flight)
                ],
                axis=0,
            )
        )
    peak = jnp.max(jnp.maximum(scores[0], scores[1]), axis=1, keepdims=True)
    part_copies[1].wait_recv()
    key = (kv_part[c, 0] + kv_in[0].astype(jnp.float32)).astype(jnp.bfloat16)
    scores.append(jnp.where(flight_seen, score(key), -jnp.inf))
    peak = jnp.maximum(peak, jnp.max(scores[-1], axis=1, keepdims=True))
    weights = [jnp.exp(v - peak).astype(jnp.bfloat16) for v in scores]
    denom = sum(jnp.sum(w.astype(jnp.float32), axis=1, keepdims=True) for w in weights)
    numer = sum(
        jnp.dot(weights[x], cache_buf[1, x], preferred_element_type=jnp.float32)
        for x in range(n_ctx)
    )
    part_copies[2].wait_recv()
    value = (kv_part[c, 1] + kv_in[1].astype(jnp.float32)).astype(jnp.bfloat16)
    numer = numer + jnp.dot(weights[-1], value, preferred_element_type=jnp.float32)
    attention = (numer / denom).astype(jnp.bfloat16)
    att_buf[c] = attention
    att_copy = remote(att_buf.at[c], att_buf.at[c], t_s.at[0], t_r.at[0], partner)
    att_copy.start()

    for x in range(n_ctx):
        last = slice(x * all_rows + rows_count, (x + 1) * all_rows)
        kv_buf[x, 0] = key[last]
        kv_buf[x, 1] = value[last]
    fin_copy = remote(kv_buf.at[other], fin_in, f_s.at[0], f_r.at[0], partner)
    fin_copy.start()
    nk_ref[:, own_lanes] = kv_buf[c, 0]
    nv_ref[:, own_lanes] = kv_buf[c, 1]

    own_depth = pl.ds(pl.multiple_of(c * HD, HD), HD)
    other_depth = pl.ds(pl.multiple_of(other * HD, HD), HD)
    blocks = [(1 - k) * n_tp + tt for tt in peers + [t]] + [k * n_tp + tt for tt in peers + [t]]
    for block in blocks:
        y_part[block] = jnp.dot(
            attention, wo_cut[block, own_depth, :], preferred_element_type=jnp.float32
        )
    att_copy.wait_recv()
    theirs = att_buf[other]
    y1 = []
    for i, block in enumerate(blocks):
        piece = y_part[block] + jnp.dot(
            theirs, wo_cut[block, other_depth, :], preferred_element_type=jnp.float32
        )
        if i >= n_tp:
            y_part[block] = piece
            continue
        tt = (peers + [t])[i]
        y_send[i] = piece.astype(jnp.bfloat16)
        copy = remote(y_send.at[i], y_in.at[tt], y1_s.at[i], y1_r.at[tt], sibling)
        copy.start()
        y1.append(copy)
    far, near, zb = [], [], []
    for i, tt in enumerate(peers + [t]):
        remote(y_send.at[i], y_in.at[tt], y1_s.at[i], y1_r.at[tt], sibling).wait_recv()
        block = k * n_tp + tt

        def chunk(x, start):
            at = pl.ds(pl.multiple_of(x * rows_count + start, half), half)
            return y_part[block, at, :] + y_in[tt, at, :].astype(jnp.float32)

        far_a[i] = chunk(other, 0).astype(jnp.bfloat16)
        copy = remote(far_a.at[i], cross_a.at[u, tt], fa_s.at[i], xa_r.at[u, tt], owner)
        copy.start()
        far.append(copy)
        near_a[i] = chunk(c, 0).astype(jnp.bfloat16)
        copy = remote(near_a.at[i], cross_a.at[u, tt], na_s.at[i], xa_r.at[u, tt], beside)
        near.append(copy)
        pl.when(jnp.logical_not(at_home))(copy.start)

        if i < n_tp - 1:
            for x in range(n_ctx):
                zb_send[i, x] = chunk(x, half).astype(jnp.bfloat16)
            copy = remote(zb_send.at[i], zb_in.at[t], zb_s.at[i], zb_r.at[t], zpeer(tt))
            copy.start()
            zb.append(copy)

    fin_copy.wait_recv()
    nk_ref[:, other_lanes] = fin_in[0]
    nv_ref[:, other_lanes] = fin_in[1]
    za = []
    for i, tt in enumerate(peers + [t]):

        @pl.when(at_home)
        def _():
            cross_a[u, tt] = near_a[i]

        for y in range(n_ctx):

            @pl.when(jnp.logical_not(jnp.logical_and(at_home, u == y)))
            def _():
                remote(far_a.at[i], cross_a.at[y, tt], fa_s.at[i], xa_r.at[y, tt], partner).wait_recv()

        summed_a = cross_a[0, tt].astype(jnp.float32) + cross_a[1, tt].astype(jnp.float32)
        if i < n_tp - 1:
            za_send[i] = summed_a.astype(jnp.bfloat16)
            copy = remote(za_send.at[i], za_in.at[t], za_s.at[i], za_r.at[t], zpeer(tt))
            copy.start()
            za.append(copy)

    for i, tt in enumerate(peers):
        remote(zb_send.at[i], zb_in.at[tt], zb_s.at[i], zb_r.at[tt], zpeer(tt)).wait_recv()

    def gathered(x):
        at = pl.ds(pl.multiple_of(x * rows_count + half, half), half)
        block = k * n_tp + t
        result = y_part[block, at, :] + y_in[t, at, :].astype(jnp.float32)
        for tt in peers:
            result = result + zb_in[tt, x].astype(jnp.float32)
        return result.astype(jnp.bfloat16)

    far_b[...] = gathered(other)
    far_copy = remote(far_b, cross_b.at[u], fb_s.at[0], xb_r.at[u], owner)
    far_copy.start()
    near_b[...] = gathered(c)
    near_copy = remote(near_b, cross_b.at[u], nb_s.at[0], xb_r.at[u], beside)
    pl.when(jnp.logical_not(at_home))(near_copy.start)

    for i, tt in enumerate(peers):
        remote(za_send.at[i], za_in.at[tt], za_s.at[i], za_r.at[tt], zpeer(tt)).wait_recv()
        summed_a = summed_a + za_in[tt].astype(jnp.float32)

    @pl.when(at_home)
    def _():
        cross_b[u] = near_b[...]

    for y in range(n_ctx):

        @pl.when(jnp.logical_not(jnp.logical_and(at_home, u == y)))
        def _():
            remote(far_b, cross_b.at[y], fb_s.at[0], xb_r.at[y], partner).wait_recv()

    summed_b = cross_b[0].astype(jnp.float32) + cross_b[1].astype(jnp.float32)
    y_rows = jnp.concatenate([summed_a, summed_b], axis=0)
    ssy_buf[0] = row_squares(y_rows, lanes)[0:1]
    ssy_copies = [
        remote(
            ssy_buf.at[0], ssy_buf.at[d], ssy_s.at[d - 1], ssy_r.at[d - 1], member((j + d) % members)
        )
        for d in range(1, members)
    ]
    for copy in ssy_copies:
        copy.start()
    pl.when(c != held)(ssq_copies[0].wait_send)
    for copy in ssq_copies[1:] + cache_copies + stage_b + part_copies + y1 + far + zb + za:
        copy.wait_send()
    for copy in [a_copy, att_copy, fin_copy, far_copy]:
        copy.wait_send()

    @pl.when(jnp.logical_not(at_home))
    def _():
        for copy in near + [near_copy]:
            copy.wait_send()

    for copy in ssy_copies:
        copy.wait_recv()
    total = ssy_buf[0]
    for d in range(1, members):
        total = total + ssy_buf[d]
    inverse = lax.rsqrt(jnp.transpose(jnp.broadcast_to(total, (8, lanes)))[:rows_count, 0:1] / D + epsilon)
    velocity = y_rows * inverse * og_ref[...].reshape(1, width)
    for f in range(flight):
        now = levels_ref[noise_ref[f]]
        after = levels_ref[noise_ref[f] + 1]
        out_ref[f] = state_ref[f] + (after - now) * velocity[f * ch : (f + 1) * ch]
    for copy in ssy_copies:
        copy.wait_send()


def write_out(*refs):
    sems = refs[6]
    copies = [pltpu.make_async_copy(refs[i], refs[3 + i], sems.at[i]) for i in range(3)]
    for copy in copies:
        copy.start()
    for copy in copies:
        copy.wait()


def fused(dims, *args):
    state, clean_tokens, w_query = args[0], args[1], args[2]
    w_out, cache_keys = args[5], args[6]
    n_grp, n_ctx, n_tp = dims
    per = n_grp // n_ctx
    members = n_grp * n_tp
    flight, ch, width = state.shape
    rows_count = flight * ch
    half = rows_count // 2
    all_rows = rows_count + ch
    total = n_ctx * all_rows
    lanes = -(-all_rows // 128) * 128
    queries = n_ctx * rows_count
    cache_dev = cache_keys.shape[0]
    bf, fl = jnp.bfloat16, jnp.float32
    dma = pltpu.SemaphoreType.DMA
    vm = pl.BlockSpec(memory_space=pltpu.VMEM)
    hbm = pl.BlockSpec(memory_space=pltpu.HBM)

    def pair(count):
        return [dma((count,))] * 2

    scratch = [
        pltpu.VMEM(state.shape, fl),
        pltpu.VMEM(clean_tokens.shape, bf),
        pltpu.VMEM((width,), fl),
        pltpu.VMEM((width,), fl),
        pltpu.VMEM((width,), fl),
        *[pltpu.SMEM(a.shape, a.dtype) for a in args[11:]],
        pltpu.VMEM((3,) + w_query.shape, bf),
        pltpu.VMEM(w_out.shape, bf),
        pltpu.VMEM((per * n_tp, w_out.shape[0], width), bf),
        pltpu.VMEM((2, n_ctx, cache_dev, HD), bf),
        pltpu.VMEM((n_ctx, 8, cache_dev), fl),
        pltpu.VMEM((1, lanes), fl),
        pltpu.VMEM((members, 1, lanes), fl),
        pltpu.VMEM((members, 1, lanes), fl),
        pltpu.VMEM((all_rows, width), fl),
        pltpu.VMEM((all_rows, width), fl),
        pltpu.VMEM((per * n_tp, n_ctx, all_rows, width), bf),
        pltpu.VMEM((3, total, n_ctx * HD), fl),
        pltpu.VMEM((n_ctx, queries, HD), fl),
        pltpu.VMEM((queries, HD), fl),
        pltpu.VMEM((n_ctx, 2, total, HD), fl),
        pltpu.VMEM((n_ctx, 2, total, HD), bf),
        pltpu.VMEM((2, total, HD), bf),
        pltpu.VMEM((n_ctx, 2, ch, HD), bf),
        pltpu.VMEM((2, ch, HD), bf),
        pltpu.VMEM((n_ctx, queries, HD), bf),
        pltpu.VMEM((per * n_tp, queries, width), fl),
        pltpu.VMEM((n_tp, queries, width), bf),
        pltpu.VMEM((n_tp, queries, width), bf),
        pltpu.VMEM((n_tp, half, width), bf),
        pltpu.VMEM((n_tp, half, width), bf),
        pltpu.VMEM((n_ctx, n_tp, half, width), bf),
        pltpu.VMEM((n_tp - 1, half, width), bf),
        pltpu.VMEM((n_tp, half, width), bf),
        pltpu.VMEM((n_tp - 1, n_ctx, half, width), bf),
        pltpu.VMEM((n_tp, n_ctx, half, width), bf),
        pltpu.VMEM((half, width), bf),
        pltpu.VMEM((half, width), bf),
        pltpu.VMEM((n_ctx, half, width), bf),
        dma((15,)),
        *pair(3),
        *pair(members),
        *pair(1),
        *pair(n_tp),
        *pair(n_tp),
        *pair(2 * n_tp),
        *pair(3),
        *pair(1),
        *pair(1),
        *pair(n_tp),
        dma((n_tp,)),
        dma((n_tp,)),
        dma((n_ctx, n_tp)),
        *pair(n_tp),
        *pair(n_tp),
        dma((1,)),
        dma((1,)),
        dma((n_ctx,)),
        *pair(members - 1),
    ]
    results = pl.pallas_call(
        functools.partial(kernel, dims),
        out_shape=(
            pltpu.VMEM(state.shape, fl),
            pltpu.VMEM((ch, cache_keys.shape[1]), bf),
            pltpu.VMEM((ch, cache_keys.shape[1]), bf),
        ),
        in_specs=[hbm] * 15,
        out_specs=(vm, vm, vm),
        scratch_shapes=scratch,
        compiler_params=pltpu.CompilerParams(
            collective_id=0, has_side_effects=True, vmem_limit_bytes=VMEM_LIMIT
        ),
    )(*args)
    return pl.pallas_call(
        write_out,
        out_shape=tuple(jax.ShapeDtypeStruct(r.shape, r.dtype) for r in results),
        in_specs=[vm] * 3,
        out_specs=(hbm,) * 3,
        scratch_shapes=[dma((3,))],
    )(*[pltpu.with_memory_space_constraint(r, pltpu.VMEM) for r in results])


def step(dims, *args):
    n_grp, n_ctx, n_tp = dims
    heads_dev = args[6].shape[1] // HD
    if n_ctx == heads_dev == 2 and n_grp == 2 * n_ctx and args[0].shape[0] <= 8:
        return fused(dims, *args)
    return local(*args)


def solution(mesh):
    dims = tuple(mesh.shape[name] for name in ("grp", "ctx", "tp"))
    return jax.shard_map(
        functools.partial(step, dims),
        mesh=mesh,
        in_specs=(
            P(None, "ctx", ("grp", "tp")),
            P("ctx", ("grp", "tp")),
            P("ctx", ("grp", "tp")),
            P("ctx", ("grp", "tp")),
            P("ctx", ("grp", "tp")),
            P(("grp", "tp"), "ctx"),
            P("ctx", ("grp", "tp")),
            P("ctx", ("grp", "tp")),
            P(("grp", "tp")),
            P(("grp", "tp")),
            P(("grp", "tp")),
            P(),
            P(),
            P("ctx"),
            P(),
        ),
        out_specs=(P(None, "ctx", ("grp", "tp")), P("ctx", ("grp", "tp")), P("ctx", ("grp", "tp"))),
        check_vma=False,
    )
```

```python
import functools
import math

import jax
import jax.numpy as jnp
from jax import lax
from jax.experimental import pallas as pl
from jax.experimental.pallas import tpu as pltpu
from jax.sharding import PartitionSpec as P

D = 5120
HD = 128
SLOT = 256


epsilon = 1e-06


def level_lookup(levels, indices):
    table = jnp.arange(levels.shape[0], dtype=jnp.int32)
    picked = (indices[:, None] == table[None, :]).astype(jnp.float32)
    return jnp.sum(picked * levels[None, :], axis=1)


def normalize_rows(rows, sigma_rows, norm_gain, mod_gain):
    squares = lax.psum(jnp.sum(rows * rows, axis=1), ("grp", "tp"))
    inverse = lax.rsqrt(squares / D + epsilon)
    scaled = (
        rows
        * inverse[:, None]
        * norm_gain[None, :]
        * (1.0 + sigma_rows[:, None] * mod_gain[None, :])
    )
    return lax.all_gather(scaled.astype(jnp.bfloat16), ("grp", "tp"), axis=1, tiled=True)


def local(
    state,
    clean_tokens,
    w_query,
    w_key,
    w_value,
    w_out,
    cache_keys,
    cache_values,
    norm_gain,
    mod_gain,
    out_gain,
    levels,
    noise_index,
    placement,
    group_mask,
):
    flight, ch_dev, local_width = state.shape
    ctx_count = lax.axis_size("ctx")
    group = ch_dev * ctx_count
    cache_dev = cache_keys.shape[0]
    slots_dev = cache_dev // SLOT
    heads_dev = cache_keys.shape[1] // HD
    rows_count = flight * ch_dev
    scale = 1.0 / math.sqrt(HD)
    wk_full, wv_full, wo_full = (
        lax.all_gather(w_key, "ctx", axis=0, tiled=True),
        lax.all_gather(w_value, "ctx", axis=0, tiled=True),
        lax.all_gather(w_out, "ctx", axis=1, tiled=True),
    )
    group_table = jnp.arange(group_mask.shape[1], dtype=jnp.int32)
    slot_onehot = (placement[:, None] == group_table[None, :]).astype(jnp.int32)
    slot_seen = jnp.sum(slot_onehot[None, :, :] * group_mask[:, None, :], axis=2) > 0
    cache_seen = slot_seen[:, None, None, :, None]
    own_group = jnp.arange(flight, dtype=jnp.int32)
    flight_seen = (own_group[None, :] <= own_group[:, None])[:, None, None, :, None]
    cache_k = cache_keys.reshape(slots_dev, SLOT, heads_dev, HD)
    cache_v = cache_values.reshape(slots_dev, SLOT, heads_dev, HD)
    finished_keys = None
    finished_values = None
    current = level_lookup(levels, noise_index + 0)
    following = level_lookup(levels, noise_index + 0 + 1)
    rows = state.reshape(rows_count, local_width)
    sigma_rows = jnp.repeat(current, ch_dev)
    rows = jnp.concatenate([rows, clean_tokens.astype(jnp.float32)], axis=0)
    sigma_rows = jnp.concatenate([sigma_rows, jnp.zeros((ch_dev,), jnp.float32)])
    features = normalize_rows(rows, sigma_rows, norm_gain, mod_gain)
    keys_new = jnp.dot(features, wk_full, preferred_element_type=jnp.float32).astype(jnp.bfloat16)
    values_new = jnp.dot(features, wv_full, preferred_element_type=jnp.float32).astype(jnp.bfloat16)
    finished_keys = keys_new[rows_count:]
    finished_values = values_new[rows_count:]
    keys_new = keys_new[:rows_count]
    values_new = values_new[:rows_count]
    noisy = features[:rows_count]
    pieces = lax.all_to_all(
        noisy.reshape(flight, ch_dev, -1), "ctx", split_axis=2, concat_axis=1, tiled=True
    )
    partial_q = jnp.einsum("fqd,de->fqe", pieces, w_query, preferred_element_type=jnp.float32)
    queries = lax.psum(partial_q, "ctx").astype(jnp.bfloat16)
    query_heads = queries.reshape(flight, group, heads_dev, HD)
    finished_k = finished_keys.reshape(ch_dev, heads_dev, HD)
    finished_v = finished_values.reshape(ch_dev, heads_dev, HD)
    flight_k = keys_new.reshape(flight, ch_dev, heads_dev, HD)
    flight_v = values_new.reshape(flight, ch_dev, heads_dev, HD)
    cache_scores = (
        jnp.einsum("fqhd,sthd->fqhst", query_heads, cache_k, preferred_element_type=jnp.float32)
        * scale
    )
    finished_scores = (
        jnp.einsum("fqhd,thd->fqht", query_heads, finished_k, preferred_element_type=jnp.float32)
        * scale
    )
    flight_scores = (
        jnp.einsum("fqhd,gthd->fqhgt", query_heads, flight_k, preferred_element_type=jnp.float32)
        * scale
    )
    peak = jnp.max(finished_scores, axis=3)
    peak = jnp.maximum(peak, jnp.max(jnp.where(cache_seen, cache_scores, -jnp.inf), axis=(3, 4)))
    peak = jnp.maximum(peak, jnp.max(jnp.where(flight_seen, flight_scores, -jnp.inf), axis=(3, 4)))
    peak = lax.pmax(peak, "ctx")
    cache_p = jnp.where(cache_seen, jnp.exp(cache_scores - peak[..., None, None]), 0.0).astype(
        jnp.bfloat16
    )
    finished_p = jnp.exp(finished_scores - peak[..., None]).astype(jnp.bfloat16)
    flight_p = jnp.where(flight_seen, jnp.exp(flight_scores - peak[..., None, None]), 0.0).astype(
        jnp.bfloat16
    )
    numer = jnp.einsum("fqhst,sthd->fqhd", cache_p, cache_v, preferred_element_type=jnp.float32)
    numer = numer + jnp.einsum(
        "fqht,thd->fqhd", finished_p, finished_v, preferred_element_type=jnp.float32
    )
    numer = numer + jnp.einsum(
        "fqhgt,gthd->fqhd", flight_p, flight_v, preferred_element_type=jnp.float32
    )
    denom = jnp.sum(cache_p, axis=(3, 4), dtype=jnp.float32)
    denom = denom + jnp.sum(finished_p, axis=3, dtype=jnp.float32)
    denom = denom + jnp.sum(flight_p, axis=(3, 4), dtype=jnp.float32)
    numer, denom = (
        lax.psum_scatter(
            numer.reshape(flight, group, heads_dev * HD), "ctx", scatter_dimension=1, tiled=True
        ),
        lax.psum_scatter(denom, "ctx", scatter_dimension=1, tiled=True),
    )
    attention = numer.reshape(flight, ch_dev, heads_dev, HD) / denom[..., None]
    attention = attention.astype(jnp.bfloat16).reshape(rows_count, heads_dev * HD)
    partial_y = jnp.dot(attention, wo_full, preferred_element_type=jnp.float32)
    y_rows = lax.psum_scatter(partial_y, ("grp", "tp"), scatter_dimension=1, tiled=True)
    y_squares = lax.psum(jnp.sum(y_rows * y_rows, axis=1), ("grp", "tp"))
    velocity = y_rows * lax.rsqrt(y_squares / D + epsilon)[:, None] * out_gain[None, :]
    state = state + (following - current)[:, None, None] * velocity.reshape(
        flight, ch_dev, local_width
    )
    return (state, finished_keys, finished_values)


MESH = pl.DeviceIdType.MESH
VMEM_LIMIT = 62 * 1024 * 1024


def remote(src, dst, send, recv, device):
    return pltpu.make_async_remote_copy(
        src_ref=src,
        dst_ref=dst,
        send_sem=send,
        recv_sem=recv,
        device_id=device,
        device_id_type=MESH,
    )


def row_squares(rows, lanes):
    squares = rows * rows
    count = squares.shape[0]
    if count < lanes:
        squares = jnp.concatenate(
            [squares, jnp.zeros((lanes - count, squares.shape[1]), jnp.float32)], axis=0
        )
    ones = jnp.ones((8, squares.shape[1]), jnp.float32)
    return lax.dot_general(
        ones,
        squares,
        (((1,), (1,)), ((), ())),
        precision=lax.Precision.HIGHEST,
        preferred_element_type=jnp.float32,
    )


def kernel(
    dims,
    state_hbm,
    clean_hbm,
    wq_hbm,
    wk_hbm,
    wv_hbm,
    wo_hbm,
    ck_hbm,
    cv_hbm,
    ng_hbm,
    mg_hbm,
    og_hbm,
    levels_hbm,
    noise_hbm,
    place_hbm,
    mask_hbm,
    out_ref,
    nk_ref,
    nv_ref,
    state_ref,
    clean_ref,
    ng_ref,
    mg_ref,
    og_ref,
    levels_ref,
    noise_ref,
    place_ref,
    mask_ref,
    w_buf,
    wo_buf,
    wo_cut,
    cache_buf,
    seen_buf,
    ssq_own,
    ssq_buf,
    ssy_buf,
    raw,
    raw_in,
    h_buf,
    acc,
    q_part,
    q_in,
    kv_part,
    kv_send,
    kv_in,
    kv_buf,
    fin_in,
    att_buf,
    y_part,
    y_send,
    y_in,
    near_a,
    far_a,
    cross_a,
    za_send,
    za_in,
    zb_send,
    zb_in,
    near_b,
    far_b,
    cross_b,
    local_sem,
    cache_s,
    cache_r,
    ssq_s,
    ssq_r,
    a_s,
    a_r,
    b_s,
    b_r,
    n_s,
    n_r,
    c_s,
    c_r,
    p_s,
    p_r,
    f_s,
    f_r,
    t_s,
    t_r,
    y1_s,
    y1_r,
    fa_s,
    na_s,
    xa_r,
    za_s,
    za_r,
    zb_s,
    zb_r,
    fb_s,
    nb_s,
    xb_r,
    ssy_s,
    ssy_r,
):
    n_grp, n_ctx, n_tp = dims
    per = n_grp // n_ctx
    members = n_grp * n_tp
    flight, ch, width = state_hbm.shape
    rows_count = flight * ch
    first = y_rows_first(rows_count)
    late = rows_count - first
    all_rows = rows_count + ch
    cache_dev = ck_hbm.shape[0]
    lanes = ssq_buf.shape[2]
    total_rows = n_ctx * all_rows
    queries = n_ctx * rows_count
    g, c, t = lax.axis_index("grp"), lax.axis_index("ctx"), lax.axis_index("tp")
    u, k = g // per, g % per
    j = g * n_tp + t
    other = 1 - c
    partner = (g, other, t)
    sibling = (u * per + (1 - k), c, t)
    beside = ((1 - u) * per + k, c, t)
    held = 1 - u
    at_home = u == c
    owner = (c * per + k, other, t)

    def member(index):
        return (index // n_tp, c, index % n_tp)

    side = t // (n_tp // 2)
    inner = t + side * (n_tp - 1 - 2 * t)
    peers = []
    for i in range(n_tp - 1):
        v = n_tp - 1 - i
        p = v - (inner - v + n_tp) // n_tp
        peers.append(p + side * (n_tp - 1 - 2 * p))
    places = [t] + peers

    def zpeer(tt):
        return (g, c, tt)

    barrier = pltpu.get_barrier_semaphore()
    for dg in range(n_grp):
        for dc in range(n_ctx):
            for dt in range(n_tp):
                if dg + dc + dt > 0:
                    pl.semaphore_signal(
                        barrier,
                        inc=1,
                        device_id=((g + dg) % n_grp, (c + dc) % n_ctx, (t + dt) % n_tp),
                        device_id_type=MESH,
                    )

    loads = [
        pltpu.make_async_copy(src, w_buf.at[i], local_sem.at[0])
        for i, src in enumerate((wq_hbm, wk_hbm, wv_hbm))
    ]
    wo_load = pltpu.make_async_copy(wo_hbm, wo_buf, local_sem.at[1])
    own_lanes = pl.ds(pl.multiple_of(c * HD, HD), HD)
    other_lanes = pl.ds(pl.multiple_of(other * HD, HD), HD)
    cache_loads = [
        pltpu.make_async_copy(src.at[:, own_lanes], cache_buf.at[c, i], local_sem.at[2])
        for i, src in enumerate((ck_hbm, cv_hbm))
    ]
    small = [
        pltpu.make_async_copy(src, dst, local_sem.at[3 + i])
        for i, (src, dst) in enumerate(
            [
                (state_hbm, state_ref),
                (clean_hbm, clean_ref),
                (ng_hbm, ng_ref),
                (mg_hbm, mg_ref),
                (og_hbm, og_ref),
                (levels_hbm, levels_ref),
                (noise_hbm, noise_ref),
                (place_hbm, place_ref),
                (mask_hbm, mask_ref),
            ]
        )
    ]
    for copy in small + [wo_load] + loads + cache_loads:
        copy.start()
    for copy in small:
        copy.wait()

    rows = jnp.concatenate(
        [state_ref[...].reshape(rows_count, width), clean_ref[...].astype(jnp.float32)], axis=0
    )
    ssq_own[...] = row_squares(rows, lanes)[0:1]

    @pl.when(c == held)
    def _():
        ssq_buf[j] = ssq_own[...]

    modulation = mg_ref[...].reshape(1, width)
    gained = rows * ng_ref[...].reshape(1, width)
    for f in range(flight):
        sigma = levels_ref[noise_ref[f]]
        raw[f * ch : (f + 1) * ch] = gained[f * ch : (f + 1) * ch] * (1.0 + sigma * modulation)
    raw[rows_count:] = gained[rows_count:]
    line = lax.broadcasted_iota(jnp.int32, (8, SLOT), 0)
    for s in range(cache_dev // SLOT):
        block = jnp.zeros((8, SLOT), jnp.float32)
        for f in range(flight):
            hidden = jnp.where(mask_ref[f, place_ref[s]] != 0, 0.0, -jnp.inf)
            block = jnp.where(line == f, hidden, block)
        seen_buf[c, :, s * SLOT : (s + 1) * SLOT] = block
    pl.semaphore_wait(barrier, n_grp * n_ctx * n_tp - 1)

    def ssq_copy(target):
        return remote(ssq_own, ssq_buf.at[j], ssq_s.at[0], ssq_r.at[0], target)

    for dk in range(per):
        for dc in range(n_ctx):
            for dt in range(n_tp):
                copy = ssq_copy(
                    ((1 - c) * per + (k + dk) % per, (c + dc) % n_ctx, (t + dt) % n_tp)
                )
                if dk + dc + dt > 0:
                    copy.start()
                else:
                    pl.when(c != held)(copy.start)
    a_copy = remote(raw, raw_in, a_s.at[0], a_r.at[0], ((1 - c) * per + k, u, t))
    a_copy.start()
    wo_load.wait()
    for block in range(per * n_tp):
        wo_cut[block] = wo_buf[:, block * width : (block + 1) * width]

    def ssq_wait(finish):
        @pl.when(c == held)
        def _():
            most = ssq_buf.at[: members - 1]
            finish(remote(most, most, ssq_s.at[0], ssq_r.at[0], partner))

        @pl.when(c != held)
        def _():
            finish(remote(ssq_buf, ssq_buf, ssq_s.at[0], ssq_r.at[0], partner))

    ssq_wait(lambda copy: copy.wait_recv())
    total = ssq_buf[0]
    for d in range(1, members):
        total = total + ssq_buf[d]
    inverse = lax.rsqrt(jnp.transpose(jnp.broadcast_to(total, (8, lanes)))[:all_rows, 0:1] / D + epsilon)
    a_copy.wait_recv()
    mine = k * n_tp + t
    h_buf[mine, held] = (raw_in[...] * inverse).astype(jnp.bfloat16)

    def slot_of(core, tt):
        return core * n_tp + tt

    def link(ref, send, recv, device):
        return remote(ref, ref, send, recv, device)

    def to_beside(x, tt):
        link(h_buf.at[slot_of(k, tt), x], n_s.at[0], n_r.at[tt], beside).start()

    def to_sibling(x, tt):
        link(h_buf.at[slot_of(k, tt), x], c_s.at[0], c_r.at[tt], sibling).start()

    for tt in peers:
        link(h_buf.at[mine, held], b_s.at[0], b_r.at[t], zpeer(tt)).start()
    to_beside(held, t)
    to_sibling(held, t)

    cache_copies = [
        remote(seen_buf.at[c], seen_buf.at[c], cache_s.at[0], cache_r.at[0], partner)
    ] + [
        remote(
            src.at[:, other_lanes], cache_buf.at[c, i], cache_s.at[1], cache_r.at[1], partner
        )
        for i, src in enumerate((ck_hbm, cv_hbm))
    ]
    for copy in cache_copies:
        copy.start()

    pltpu.make_async_copy(w_buf, w_buf, local_sem.at[0]).wait()

    def project(slots, w):
        total = None
        for slot in slots:
            lhs = h_buf[slot].reshape(total_rows, width)
            depth = pl.ds(pl.multiple_of(slot * width, 64), width)
            product = jnp.dot(lhs, w_buf[w, depth, :], preferred_element_type=jnp.float32)
            total = product if total is None else total + product
        return total

    def from_line(i):
        tt = places[i]
        link(h_buf.at[slot_of(k, tt), held], b_s.at[0], b_r.at[tt], zpeer(tt)).wait_recv()
        to_beside(held, tt)
        to_sibling(held, tt)

    def from_beside(i):
        tt = places[i]
        link(h_buf.at[slot_of(k, tt), u], n_s.at[0], n_r.at[tt], beside).wait_recv()
        to_sibling(u, tt)

    def from_sibling(i):
        tt = places[i]
        link(h_buf.at[slot_of(1 - k, tt)], c_s.at[0], c_r.at[tt], sibling).wait_recv()

    def add(slots, fresh=False):
        for w in range(3):
            acc[w] = project(slots, w) if fresh else acc[w] + project(slots, w)

    from_beside(0)
    from_line(1)
    from_sibling(0)
    add([slot_of(k, t), slot_of(1 - k, t)], True)
    from_line(2)
    from_line(3)
    from_beside(1)
    from_beside(2)
    from_sibling(1)
    add([slot_of(k, places[1]), slot_of(1 - k, places[1])])
    from_beside(3)
    add([slot_of(k, places[2]), slot_of(k, places[3])])
    from_sibling(2)
    from_sibling(n_tp - 1)
    part_copies = []
    for w in range(3):
        whole = acc[w] + project([slot_of(1 - k, tt) for tt in places[n_tp - 2 :]], w)
        for head in range(n_ctx):
            piece = whole[:, head * HD : (head + 1) * HD]
            if w == 0:
                for x in range(n_ctx):
                    q_part[head, x * rows_count : (x + 1) * rows_count] = piece[
                        x * all_rows : x * all_rows + rows_count
                    ]
            else:
                kv_part[head, w - 1] = piece
                kv_send[head, w - 1] = piece.astype(jnp.bfloat16)
        if w == 0:
            copy = remote(q_part.at[other], q_in, p_s.at[0], p_r.at[0], partner)
        else:
            copy = remote(
                kv_send.at[other, w - 1], kv_in.at[w - 1], p_s.at[1], p_r.at[w], partner
            )
        copy.start()
        part_copies.append(copy)
    pltpu.make_async_copy(cache_buf.at[0], cache_buf.at[0], local_sem.at[2]).wait()
    cache_copies[0].wait_recv()
    both_caches = remote(
        cache_buf.at[0], cache_buf.at[0], cache_s.at[1], cache_r.at[1], partner
    )
    both_caches.wait_recv()
    query_group = (lax.broadcasted_iota(jnp.int32, (queries, total_rows), 0) % rows_count) // ch
    key_group = (lax.broadcasted_iota(jnp.int32, (queries, total_rows), 1) % all_rows) // ch
    flight_seen = jnp.logical_or(key_group == flight, key_group <= query_group)

    part_copies[0].wait_recv()
    q = (q_part[c] + q_in[...]).astype(jnp.bfloat16)
    scale = 1.0 / math.sqrt(HD)

    def score(keys):
        return (
            lax.dot_general(q, keys, (((1,), (1,)), ((), ())), preferred_element_type=jnp.float32)
            * scale
        )

    scores = []
    for x in range(n_ctx):
        plain = score(cache_buf[x, 0])
        scores.append(
            jnp.concatenate(
                [
                    plain[b * ch : (b + 1) * ch] + seen_buf[x, b % flight : b % flight + 1]
                    for b in range(n_ctx * flight)
                ],
                axis=0,
            )
        )
    peak = jnp.max(jnp.maximum(scores[0], scores[1]), axis=1, keepdims=True)
    part_copies[1].wait_recv()
    key = (kv_part[c, 0] + kv_in[0].astype(jnp.float32)).astype(jnp.bfloat16)
    scores.append(jnp.where(flight_seen, score(key), -jnp.inf))
    peak = jnp.maximum(peak, jnp.max(scores[-1], axis=1, keepdims=True))
    weights = [jnp.exp(v - peak).astype(jnp.bfloat16) for v in scores]
    denom = sum(jnp.sum(w.astype(jnp.float32), axis=1, keepdims=True) for w in weights)
    numer = sum(
        jnp.dot(weights[x], cache_buf[x, 1], preferred_element_type=jnp.float32)
        for x in range(n_ctx)
    )
    part_copies[2].wait_recv()
    value = (kv_part[c, 1] + kv_in[1].astype(jnp.float32)).astype(jnp.bfloat16)
    numer = numer + jnp.dot(weights[-1], value, preferred_element_type=jnp.float32)
    attention = (numer / denom).astype(jnp.bfloat16)
    att_buf[c] = attention
    att_copy = remote(att_buf.at[c], att_buf.at[c], t_s.at[0], t_r.at[0], partner)
    att_copy.start()

    for x in range(n_ctx):
        last = slice(x * all_rows + rows_count, (x + 1) * all_rows)
        kv_buf[x, 0] = key[last]
        kv_buf[x, 1] = value[last]
    fin_copy = remote(kv_buf.at[other], fin_in, f_s.at[0], f_r.at[0], partner)
    fin_copy.start()
    nk_ref[:, own_lanes] = kv_buf[c, 0]
    nv_ref[:, own_lanes] = kv_buf[c, 1]

    att_copy.wait_recv()
    both = jnp.concatenate([att_buf[x] for x in range(n_ctx)], axis=1)
    order = peers + [t]
    for start in range(0, n_tp, 2):
        for i in (start, start + 1):
            piece = jnp.dot(
                both, wo_cut[slot_of(1 - k, order[i])], preferred_element_type=jnp.float32
            )
            y_send[i] = piece.astype(jnp.bfloat16)
        for i in (start, start + 1):
            remote(
                y_send.at[i], y_in.at[order[i]], y1_s.at[0], y1_r.at[order[i]], sibling
            ).start()
    for tt in order:
        y_part[tt] = jnp.dot(both, wo_cut[slot_of(k, tt)], preferred_element_type=jnp.float32)
    for i, tt in enumerate(order):
        remote(y_send.at[i], y_in.at[tt], y1_s.at[0], y1_r.at[tt], sibling).wait_recv()

        def chunk(x, start, size):
            at = pl.ds(pl.multiple_of(x * rows_count + start, ch), size)
            return y_part[tt, at, :] + y_in[tt, at, :].astype(jnp.float32)

        far_a[i] = chunk(other, 0, first).astype(jnp.bfloat16)
        remote(far_a.at[i], cross_a.at[tt, u], fa_s.at[0], xa_r.at[tt], owner).start()
        near_a[i] = chunk(c, 0, first).astype(jnp.bfloat16)
        near = remote(near_a.at[i], cross_a.at[tt, u], na_s.at[0], xa_r.at[tt], beside)
        pl.when(jnp.logical_not(at_home))(near.start)

        if i < n_tp - 1:
            for x in range(n_ctx):
                zb_send[i, x] = chunk(x, first, late).astype(jnp.bfloat16)
            remote(zb_send.at[i], zb_in.at[t], zb_s.at[0], zb_r.at[0], zpeer(tt)).start()

    fin_copy.wait_recv()
    nk_ref[:, other_lanes] = fin_in[0]
    nv_ref[:, other_lanes] = fin_in[1]

    def both_sources(ref, send, recv):
        @pl.when(at_home)
        def _():
            remote(ref.at[0], ref.at[0], send, recv, partner).wait_recv()

        @pl.when(jnp.logical_not(at_home))
        def _():
            remote(ref, ref, send, recv, partner).wait_recv()

    for i, tt in enumerate(order):

        @pl.when(at_home)
        def _():
            cross_a[tt, u] = near_a[i]

        both_sources(cross_a.at[tt], fa_s.at[0], xa_r.at[tt])
        summed_a = cross_a[tt, 0].astype(jnp.float32) + cross_a[tt, 1].astype(jnp.float32)
        if i < n_tp - 1:
            za_send[i] = summed_a.astype(jnp.bfloat16)
            remote(za_send.at[i], za_in.at[t], za_s.at[0], za_r.at[0], zpeer(tt)).start()

    link(zb_send, zb_s.at[0], zb_r.at[0], partner).wait_recv()

    def gathered(x):
        at = pl.ds(pl.multiple_of(x * rows_count + first, ch), late)
        result = y_part[t, at, :] + y_in[t, at, :].astype(jnp.float32)
        for tt in peers:
            result = result + zb_in[tt, x].astype(jnp.float32)
        return result.astype(jnp.bfloat16)

    far_b[...] = gathered(other)
    far_copy = remote(far_b, cross_b.at[u], fb_s.at[0], xb_r.at[0], owner)
    far_copy.start()
    near_b[...] = gathered(c)
    near_copy = remote(near_b, cross_b.at[u], nb_s.at[0], xb_r.at[0], beside)
    pl.when(jnp.logical_not(at_home))(near_copy.start)

    link(za_send, za_s.at[0], za_r.at[0], partner).wait_recv()
    for tt in peers:
        summed_a = summed_a + za_in[tt].astype(jnp.float32)

    @pl.when(at_home)
    def _():
        cross_b[u] = near_b[...]

    both_sources(cross_b, fb_s.at[0], xb_r.at[0])
    summed_b = cross_b[0].astype(jnp.float32) + cross_b[1].astype(jnp.float32)
    y_rows = jnp.concatenate([summed_a, summed_b], axis=0)
    ssy_buf[0] = row_squares(y_rows, lanes)[0:1]
    for d in range(1, members):
        remote(
            ssy_buf.at[0], ssy_buf.at[d], ssy_s.at[0], ssy_r.at[0], member((j + d) % members)
        ).start()
    ssq_wait(lambda copy: copy.wait_send())
    slots = n_tp - 1
    for ref, send in (
        (h_buf.at[:slots, 0], b_s),
        (h_buf.at[: n_tp // n_ctx], n_s),
        (h_buf.at[:n_tp], c_s),
        (kv_send.at[0], p_s.at[1:]),
        (y_send, y1_s),
        (far_a, fa_s),
        (za_send, za_s),
        (zb_send, zb_s),
    ):
        link(ref, send.at[0], send.at[0], partner).wait_send()
    for copy in [a_copy, cache_copies[0], both_caches, part_copies[0], att_copy, fin_copy, far_copy]:
        copy.wait_send()

    @pl.when(jnp.logical_not(at_home))
    def _():
        link(near_a, na_s.at[0], na_s.at[0], partner).wait_send()
        near_copy.wait_send()

    rest = ssy_buf.at[1:]
    ssy_all = remote(rest, rest, ssy_s.at[0], ssy_r.at[0], partner)
    ssy_all.wait_recv()
    total = ssy_buf[0]
    for d in range(1, members):
        total = total + ssy_buf[d]
    inverse = lax.rsqrt(jnp.transpose(jnp.broadcast_to(total, (8, lanes)))[:rows_count, 0:1] / D + epsilon)
    velocity = y_rows * inverse * og_ref[...].reshape(1, width)
    for f in range(flight):
        now = levels_ref[noise_ref[f]]
        after = levels_ref[noise_ref[f] + 1]
        out_ref[f] = state_ref[f] + (after - now) * velocity[f * ch : (f + 1) * ch]
    ssy_all.wait_send()


def y_rows_first(rows_count):
    return 3 * (rows_count // 4)


def write_out(*refs):
    sems = refs[6]
    copies = [pltpu.make_async_copy(refs[i], refs[3 + i], sems.at[i]) for i in range(3)]
    for copy in copies:
        copy.start()
    for copy in copies:
        copy.wait()


def fused(dims, *args):
    state, clean_tokens, w_query = args[0], args[1], args[2]
    w_out, cache_keys = args[5], args[6]
    n_grp, n_ctx, n_tp = dims
    per = n_grp // n_ctx
    members = n_grp * n_tp
    flight, ch, width = state.shape
    rows_count = flight * ch
    first = y_rows_first(rows_count)
    late = rows_count - first
    all_rows = rows_count + ch
    total = n_ctx * all_rows
    lanes = -(-all_rows // 128) * 128
    queries = n_ctx * rows_count
    cache_dev = cache_keys.shape[0]
    bf, fl = jnp.bfloat16, jnp.float32
    dma = pltpu.SemaphoreType.DMA
    vm = pl.BlockSpec(memory_space=pltpu.VMEM)
    hbm = pl.BlockSpec(memory_space=pltpu.HBM)

    def pair(count):
        return [dma((count,))] * 2

    scratch = [
        pltpu.VMEM(state.shape, fl),
        pltpu.VMEM(clean_tokens.shape, bf),
        pltpu.VMEM((width,), fl),
        pltpu.VMEM((width,), fl),
        pltpu.VMEM((width,), fl),
        *[pltpu.SMEM(a.shape, a.dtype) for a in args[11:]],
        pltpu.VMEM((3,) + w_query.shape, bf),
        pltpu.VMEM(w_out.shape, bf),
        pltpu.VMEM((per * n_tp, w_out.shape[0], width), bf),
        pltpu.VMEM((n_ctx, 2, cache_dev, HD), bf),
        pltpu.VMEM((n_ctx, 8, cache_dev), fl),
        pltpu.VMEM((1, lanes), fl),
        pltpu.VMEM((members, 1, lanes), fl),
        pltpu.VMEM((members, 1, lanes), fl),
        pltpu.VMEM((all_rows, width), fl),
        pltpu.VMEM((all_rows, width), fl),
        pltpu.VMEM((per * n_tp, n_ctx, all_rows, width), bf),
        pltpu.VMEM((3, total, n_ctx * HD), fl),
        pltpu.VMEM((n_ctx, queries, HD), fl),
        pltpu.VMEM((queries, HD), fl),
        pltpu.VMEM((n_ctx, 2, total, HD), fl),
        pltpu.VMEM((n_ctx, 2, total, HD), bf),
        pltpu.VMEM((2, total, HD), bf),
        pltpu.VMEM((n_ctx, 2, ch, HD), bf),
        pltpu.VMEM((2, ch, HD), bf),
        pltpu.VMEM((n_ctx, queries, HD), bf),
        pltpu.VMEM((n_tp, queries, width), fl),
        pltpu.VMEM((n_tp, queries, width), bf),
        pltpu.VMEM((n_tp, queries, width), bf),
        pltpu.VMEM((n_tp, first, width), bf),
        pltpu.VMEM((n_tp, first, width), bf),
        pltpu.VMEM((n_tp, n_ctx, first, width), bf),
        pltpu.VMEM((n_tp - 1, first, width), bf),
        pltpu.VMEM((n_tp, first, width), bf),
        pltpu.VMEM((n_tp - 1, n_ctx, late, width), bf),
        pltpu.VMEM((n_tp, n_ctx, late, width), bf),
        pltpu.VMEM((late, width), bf),
        pltpu.VMEM((late, width), bf),
        pltpu.VMEM((n_ctx, late, width), bf),
        dma((12,)),
        *pair(2),
        *pair(1),
        *pair(1),
        dma((1,)),
        dma((n_tp,)),
        dma((1,)),
        dma((n_tp,)),
        dma((1,)),
        dma((n_tp,)),
        dma((2,)),
        dma((3,)),
        *pair(1),
        *pair(1),
        dma((1,)),
        dma((n_tp,)),
        dma((1,)),
        dma((1,)),
        dma((n_tp,)),
        *pair(1),
        *pair(1),
        dma((1,)),
        dma((1,)),
        dma((1,)),
        *pair(1),
    ]
    results = pl.pallas_call(
        functools.partial(kernel, dims),
        out_shape=(
            pltpu.VMEM(state.shape, fl),
            pltpu.VMEM((ch, cache_keys.shape[1]), bf),
            pltpu.VMEM((ch, cache_keys.shape[1]), bf),
        ),
        in_specs=[hbm] * 15,
        out_specs=(vm, vm, vm),
        scratch_shapes=scratch,
        compiler_params=pltpu.CompilerParams(
            collective_id=0, has_side_effects=True, vmem_limit_bytes=VMEM_LIMIT
        ),
    )(*args)
    return pl.pallas_call(
        write_out,
        out_shape=tuple(jax.ShapeDtypeStruct(r.shape, r.dtype) for r in results),
        in_specs=[vm] * 3,
        out_specs=(hbm,) * 3,
        scratch_shapes=[dma((3,))],
    )(*[pltpu.with_memory_space_constraint(r, pltpu.VMEM) for r in results])


def step(dims, *args):
    n_grp, n_ctx, n_tp = dims
    heads_dev = args[6].shape[1] // HD
    if n_ctx == heads_dev == 2 and n_grp == 2 * n_ctx and args[0].shape[0] <= 8:
        return fused(dims, *args)
    return local(*args)


def solution(mesh):
    dims = tuple(mesh.shape[name] for name in ("grp", "ctx", "tp"))
    return jax.shard_map(
        functools.partial(step, dims),
        mesh=mesh,
        in_specs=(
            P(None, "ctx", ("grp", "tp")),
            P("ctx", ("grp", "tp")),
            P("ctx", ("grp", "tp")),
            P("ctx", ("grp", "tp")),
            P("ctx", ("grp", "tp")),
            P(("grp", "tp"), "ctx"),
            P("ctx", ("grp", "tp")),
            P("ctx", ("grp", "tp")),
            P(("grp", "tp")),
            P(("grp", "tp")),
            P(("grp", "tp")),
            P(),
            P(),
            P("ctx"),
            P(),
        ),
        out_specs=(P(None, "ctx", ("grp", "tp")), P("ctx", ("grp", "tp")), P("ctx", ("grp", "tp"))),
        check_vma=False,
    )
```

```python
import functools
import math

import jax
import jax.numpy as jnp
from jax import lax
from jax.experimental import pallas as pl
from jax.experimental.pallas import tpu as pltpu
from jax.sharding import PartitionSpec as P

D = 5120
HD = 128
SLOT = 256


epsilon = 1e-06


def level_lookup(levels, indices):
    table = jnp.arange(levels.shape[0], dtype=jnp.int32)
    picked = (indices[:, None] == table[None, :]).astype(jnp.float32)
    return jnp.sum(picked * levels[None, :], axis=1)


def normalize_rows(rows, sigma_rows, norm_gain, mod_gain):
    squares = lax.psum(jnp.sum(rows * rows, axis=1), ("grp", "tp"))
    inverse = lax.rsqrt(squares / D + epsilon)
    scaled = (
        rows
        * inverse[:, None]
        * norm_gain[None, :]
        * (1.0 + sigma_rows[:, None] * mod_gain[None, :])
    )
    return lax.all_gather(scaled.astype(jnp.bfloat16), ("grp", "tp"), axis=1, tiled=True)


def local(
    state,
    clean_tokens,
    w_query,
    w_key,
    w_value,
    w_out,
    cache_keys,
    cache_values,
    norm_gain,
    mod_gain,
    out_gain,
    levels,
    noise_index,
    placement,
    group_mask,
):
    flight, ch_dev, local_width = state.shape
    ctx_count = lax.axis_size("ctx")
    group = ch_dev * ctx_count
    cache_dev = cache_keys.shape[0]
    slots_dev = cache_dev // SLOT
    heads_dev = cache_keys.shape[1] // HD
    rows_count = flight * ch_dev
    scale = 1.0 / math.sqrt(HD)
    wk_full, wv_full, wo_full = (
        lax.all_gather(w_key, "ctx", axis=0, tiled=True),
        lax.all_gather(w_value, "ctx", axis=0, tiled=True),
        lax.all_gather(w_out, "ctx", axis=1, tiled=True),
    )
    group_table = jnp.arange(group_mask.shape[1], dtype=jnp.int32)
    slot_onehot = (placement[:, None] == group_table[None, :]).astype(jnp.int32)
    slot_seen = jnp.sum(slot_onehot[None, :, :] * group_mask[:, None, :], axis=2) > 0
    cache_seen = slot_seen[:, None, None, :, None]
    own_group = jnp.arange(flight, dtype=jnp.int32)
    flight_seen = (own_group[None, :] <= own_group[:, None])[:, None, None, :, None]
    cache_k = cache_keys.reshape(slots_dev, SLOT, heads_dev, HD)
    cache_v = cache_values.reshape(slots_dev, SLOT, heads_dev, HD)
    finished_keys = None
    finished_values = None
    current = level_lookup(levels, noise_index + 0)
    following = level_lookup(levels, noise_index + 0 + 1)
    rows = state.reshape(rows_count, local_width)
    sigma_rows = jnp.repeat(current, ch_dev)
    rows = jnp.concatenate([rows, clean_tokens.astype(jnp.float32)], axis=0)
    sigma_rows = jnp.concatenate([sigma_rows, jnp.zeros((ch_dev,), jnp.float32)])
    features = normalize_rows(rows, sigma_rows, norm_gain, mod_gain)
    keys_new = jnp.dot(features, wk_full, preferred_element_type=jnp.float32).astype(jnp.bfloat16)
    values_new = jnp.dot(features, wv_full, preferred_element_type=jnp.float32).astype(jnp.bfloat16)
    finished_keys = keys_new[rows_count:]
    finished_values = values_new[rows_count:]
    keys_new = keys_new[:rows_count]
    values_new = values_new[:rows_count]
    noisy = features[:rows_count]
    pieces = lax.all_to_all(
        noisy.reshape(flight, ch_dev, -1), "ctx", split_axis=2, concat_axis=1, tiled=True
    )
    partial_q = jnp.einsum("fqd,de->fqe", pieces, w_query, preferred_element_type=jnp.float32)
    queries = lax.psum(partial_q, "ctx").astype(jnp.bfloat16)
    query_heads = queries.reshape(flight, group, heads_dev, HD)
    finished_k = finished_keys.reshape(ch_dev, heads_dev, HD)
    finished_v = finished_values.reshape(ch_dev, heads_dev, HD)
    flight_k = keys_new.reshape(flight, ch_dev, heads_dev, HD)
    flight_v = values_new.reshape(flight, ch_dev, heads_dev, HD)
    cache_scores = (
        jnp.einsum("fqhd,sthd->fqhst", query_heads, cache_k, preferred_element_type=jnp.float32)
        * scale
    )
    finished_scores = (
        jnp.einsum("fqhd,thd->fqht", query_heads, finished_k, preferred_element_type=jnp.float32)
        * scale
    )
    flight_scores = (
        jnp.einsum("fqhd,gthd->fqhgt", query_heads, flight_k, preferred_element_type=jnp.float32)
        * scale
    )
    peak = jnp.max(finished_scores, axis=3)
    peak = jnp.maximum(peak, jnp.max(jnp.where(cache_seen, cache_scores, -jnp.inf), axis=(3, 4)))
    peak = jnp.maximum(peak, jnp.max(jnp.where(flight_seen, flight_scores, -jnp.inf), axis=(3, 4)))
    peak = lax.pmax(peak, "ctx")
    cache_p = jnp.where(cache_seen, jnp.exp(cache_scores - peak[..., None, None]), 0.0).astype(
        jnp.bfloat16
    )
    finished_p = jnp.exp(finished_scores - peak[..., None]).astype(jnp.bfloat16)
    flight_p = jnp.where(flight_seen, jnp.exp(flight_scores - peak[..., None, None]), 0.0).astype(
        jnp.bfloat16
    )
    numer = jnp.einsum("fqhst,sthd->fqhd", cache_p, cache_v, preferred_element_type=jnp.float32)
    numer = numer + jnp.einsum(
        "fqht,thd->fqhd", finished_p, finished_v, preferred_element_type=jnp.float32
    )
    numer = numer + jnp.einsum(
        "fqhgt,gthd->fqhd", flight_p, flight_v, preferred_element_type=jnp.float32
    )
    denom = jnp.sum(cache_p, axis=(3, 4), dtype=jnp.float32)
    denom = denom + jnp.sum(finished_p, axis=3, dtype=jnp.float32)
    denom = denom + jnp.sum(flight_p, axis=(3, 4), dtype=jnp.float32)
    numer, denom = (
        lax.psum_scatter(
            numer.reshape(flight, group, heads_dev * HD), "ctx", scatter_dimension=1, tiled=True
        ),
        lax.psum_scatter(denom, "ctx", scatter_dimension=1, tiled=True),
    )
    attention = numer.reshape(flight, ch_dev, heads_dev, HD) / denom[..., None]
    attention = attention.astype(jnp.bfloat16).reshape(rows_count, heads_dev * HD)
    partial_y = jnp.dot(attention, wo_full, preferred_element_type=jnp.float32)
    y_rows = lax.psum_scatter(partial_y, ("grp", "tp"), scatter_dimension=1, tiled=True)
    y_squares = lax.psum(jnp.sum(y_rows * y_rows, axis=1), ("grp", "tp"))
    velocity = y_rows * lax.rsqrt(y_squares / D + epsilon)[:, None] * out_gain[None, :]
    state = state + (following - current)[:, None, None] * velocity.reshape(
        flight, ch_dev, local_width
    )
    return (state, finished_keys, finished_values)


MESH = pl.DeviceIdType.MESH
VMEM_LIMIT = 62 * 1024 * 1024


def remote(src, dst, send, recv, device):
    return pltpu.make_async_remote_copy(
        src_ref=src,
        dst_ref=dst,
        send_sem=send,
        recv_sem=recv,
        device_id=device,
        device_id_type=MESH,
    )


def row_squares(rows, lanes):
    squares = rows * rows
    count = squares.shape[0]
    if count < lanes:
        squares = jnp.concatenate(
            [squares, jnp.zeros((lanes - count, squares.shape[1]), jnp.float32)], axis=0
        )
    ones = jnp.ones((8, squares.shape[1]), jnp.float32)
    return lax.dot_general(
        ones,
        squares,
        (((1,), (1,)), ((), ())),
        precision=lax.Precision.HIGHEST,
        preferred_element_type=jnp.float32,
    )


def kernel(
    dims,
    state_hbm,
    clean_hbm,
    wq_hbm,
    wk_hbm,
    wv_hbm,
    wo_hbm,
    ck_hbm,
    cv_hbm,
    ng_hbm,
    mg_hbm,
    og_hbm,
    levels_hbm,
    noise_hbm,
    place_hbm,
    mask_hbm,
    out_ref,
    nk_ref,
    nv_ref,
    state_ref,
    clean_ref,
    ng_ref,
    mg_ref,
    og_ref,
    levels_ref,
    noise_ref,
    place_ref,
    mask_ref,
    w_buf,
    wo_buf,
    wo_cut,
    wo_sib,
    cache_buf,
    seen_buf,
    ssq_own,
    ssq_buf,
    ssy_buf,
    raw,
    raw_in,
    h_buf,
    acc,
    q_part,
    q_in,
    kv_part,
    kv_send,
    kv_in,
    kv_buf,
    fin_in,
    att_buf,
    y_part,
    near_a,
    far_a,
    cross_a,
    za_send,
    za_in,
    zb_send,
    zb_in,
    near_b,
    far_b,
    cross_b,
    local_sem,
    cache_s,
    cache_r,
    ssq_s,
    ssq_r,
    a_s,
    a_r,
    b_s,
    b_r,
    n_s,
    n_r,
    c_s,
    c_r,
    p_s,
    p_r,
    f_s,
    f_r,
    t_s,
    t_r,
    wo_s,
    wo_r,
    fa_s,
    na_s,
    xa_r,
    za_s,
    za_r,
    zb_s,
    zb_r,
    fb_s,
    nb_s,
    xb_r,
    ssy_s,
    ssy_r,
):
    n_grp, n_ctx, n_tp = dims
    per = n_grp // n_ctx
    members = n_grp * n_tp
    flight, ch, width = state_hbm.shape
    rows_count = flight * ch
    first = y_rows_first(rows_count)
    late = rows_count - first
    all_rows = rows_count + ch
    cache_dev = ck_hbm.shape[0]
    lanes = ssq_buf.shape[2]
    total_rows = n_ctx * all_rows
    queries = n_ctx * rows_count
    g, c, t = lax.axis_index("grp"), lax.axis_index("ctx"), lax.axis_index("tp")
    u, k = g // per, g % per
    j = g * n_tp + t
    other = 1 - c
    partner = (g, other, t)
    sibling = (u * per + (1 - k), c, t)
    beside = ((1 - u) * per + k, c, t)
    held = 1 - u
    at_home = u == c
    owner = (c * per + k, other, t)

    def member(index):
        return (index // n_tp, c, index % n_tp)

    side = t // (n_tp // 2)
    inner = t + side * (n_tp - 1 - 2 * t)
    peers = []
    for i in range(n_tp - 1):
        v = n_tp - 1 - i
        p = v - (inner - v + n_tp) // n_tp
        peers.append(p + side * (n_tp - 1 - 2 * p))
    pair = t + 1 - 2 * (t % 2)
    span = n_tp // 2
    across = (t + span) % n_tp
    diagonal = (pair + span) % n_tp
    places = [t, pair, across, diagonal]

    def zpeer(tt):
        return (g, c, tt)

    barrier = pltpu.get_barrier_semaphore()
    for dg in range(n_grp):
        for dc in range(n_ctx):
            for dt in range(n_tp):
                if dg + dc + dt > 0:
                    pl.semaphore_signal(
                        barrier,
                        inc=1,
                        device_id=((g + dg) % n_grp, (c + dc) % n_ctx, (t + dt) % n_tp),
                        device_id_type=MESH,
                    )

    loads = [
        pltpu.make_async_copy(src, w_buf.at[i], local_sem.at[0])
        for i, src in enumerate((wq_hbm, wk_hbm, wv_hbm))
    ]
    wo_load = pltpu.make_async_copy(wo_hbm, wo_buf, local_sem.at[1])
    own_lanes = pl.ds(pl.multiple_of(c * HD, HD), HD)
    other_lanes = pl.ds(pl.multiple_of(other * HD, HD), HD)
    cache_loads = [
        pltpu.make_async_copy(src.at[:, own_lanes], cache_buf.at[c, i], local_sem.at[2])
        for i, src in enumerate((ck_hbm, cv_hbm))
    ]
    small = [
        pltpu.make_async_copy(src, dst, local_sem.at[3 + i])
        for i, (src, dst) in enumerate(
            [
                (state_hbm, state_ref),
                (clean_hbm, clean_ref),
                (ng_hbm, ng_ref),
                (mg_hbm, mg_ref),
                (og_hbm, og_ref),
                (levels_hbm, levels_ref),
                (noise_hbm, noise_ref),
                (place_hbm, place_ref),
                (mask_hbm, mask_ref),
            ]
        )
    ]
    for copy in small + [wo_load] + loads + cache_loads:
        copy.start()
    for copy in small:
        copy.wait()

    rows = jnp.concatenate(
        [state_ref[...].reshape(rows_count, width), clean_ref[...].astype(jnp.float32)], axis=0
    )
    ssq_own[...] = row_squares(rows, lanes)[0:1]

    @pl.when(c == held)
    def _():
        ssq_buf[j] = ssq_own[...]

    modulation = mg_ref[...].reshape(1, width)
    gained = rows * ng_ref[...].reshape(1, width)
    for f in range(flight):
        sigma = levels_ref[noise_ref[f]]
        raw[f * ch : (f + 1) * ch] = gained[f * ch : (f + 1) * ch] * (1.0 + sigma * modulation)
    raw[rows_count:] = gained[rows_count:]
    line = lax.broadcasted_iota(jnp.int32, (8, SLOT), 0)
    for s in range(cache_dev // SLOT):
        block = jnp.zeros((8, SLOT), jnp.float32)
        for f in range(flight):
            hidden = jnp.where(mask_ref[f, place_ref[s]] != 0, 0.0, -jnp.inf)
            block = jnp.where(line == f, hidden, block)
        seen_buf[c, :, s * SLOT : (s + 1) * SLOT] = block
    pl.semaphore_wait(barrier, n_grp * n_ctx * n_tp - 1)

    def ssq_copy(target):
        return remote(ssq_own, ssq_buf.at[j], ssq_s.at[0], ssq_r.at[0], target)

    for dk in range(per):
        for dc in range(n_ctx):
            for dt in range(n_tp):
                copy = ssq_copy(
                    ((1 - c) * per + (k + dk) % per, (c + dc) % n_ctx, (t + dt) % n_tp)
                )
                if dk + dc + dt > 0:
                    copy.start()
                else:
                    pl.when(c != held)(copy.start)
    a_copy = remote(raw, raw_in, a_s.at[0], a_r.at[0], ((1 - c) * per + k, u, t))
    a_copy.start()
    wo_load.wait()
    for block in range(per * n_tp):
        wo_cut[block] = wo_buf[:, block * width : (block + 1) * width]
    wo_copy = remote(
        wo_cut.at[pl.ds((1 - k) * n_tp, n_tp)], wo_sib, wo_s.at[0], wo_r.at[0], sibling
    )
    wo_copy.start()

    def ssq_wait(finish):
        @pl.when(c == held)
        def _():
            most = ssq_buf.at[: members - 1]
            finish(remote(most, most, ssq_s.at[0], ssq_r.at[0], partner))

        @pl.when(c != held)
        def _():
            finish(remote(ssq_buf, ssq_buf, ssq_s.at[0], ssq_r.at[0], partner))

    ssq_wait(lambda copy: copy.wait_recv())
    total = ssq_buf[0]
    for d in range(1, members):
        total = total + ssq_buf[d]
    inverse = lax.rsqrt(jnp.transpose(jnp.broadcast_to(total, (8, lanes)))[:all_rows, 0:1] / D + epsilon)
    a_copy.wait_recv()
    mine = k * n_tp + t
    h_buf[mine, held] = (raw_in[...] * inverse).astype(jnp.bfloat16)

    def slot_of(core, tt):
        return core * n_tp + tt

    def link(ref, send, recv, device):
        return remote(ref, ref, send, recv, device)

    def to_beside(x, tt):
        link(h_buf.at[slot_of(k, tt), x], n_s.at[0], n_r.at[tt], beside).start()

    def to_sibling(x, tt):
        link(h_buf.at[slot_of(k, tt), x], c_s.at[0], c_r.at[tt], sibling).start()

    def to_line(tt, device):
        link(h_buf.at[slot_of(k, tt), held], b_s.at[0], b_r.at[tt], device).start()

    to_line(t, zpeer(across))
    to_line(t, zpeer(pair))
    to_beside(held, t)
    to_sibling(held, t)

    cache_copies = [
        remote(seen_buf.at[c], seen_buf.at[c], cache_s.at[0], cache_r.at[0], partner)
    ] + [
        remote(
            src.at[:, other_lanes], cache_buf.at[c, i], cache_s.at[1], cache_r.at[1], partner
        )
        for i, src in enumerate((ck_hbm, cv_hbm))
    ]
    for copy in cache_copies:
        copy.start()

    pltpu.make_async_copy(w_buf, w_buf, local_sem.at[0]).wait()

    def project(slots, w):
        total = None
        for slot in slots:
            lhs = h_buf[slot].reshape(total_rows, width)
            depth = pl.ds(pl.multiple_of(slot * width, 64), width)
            product = jnp.dot(lhs, w_buf[w, depth, :], preferred_element_type=jnp.float32)
            total = product if total is None else total + product
        return total

    def from_line(i):
        tt = places[i]
        link(h_buf.at[slot_of(k, tt), held], b_s.at[0], b_r.at[tt], partner).wait_recv()
        if i == 1:
            to_beside(held, tt)
        if i == 2:
            to_line(tt, zpeer(pair))
        to_sibling(held, tt)

    def from_beside(i):
        tt = places[i]
        link(h_buf.at[slot_of(k, tt), u], n_s.at[0], n_r.at[tt], beside).wait_recv()
        if i in (0, 2):
            device = zpeer(across if i == 0 else pair)
            link(h_buf.at[slot_of(k, tt), u], n_s.at[0], n_r.at[tt], device).start()
        to_sibling(u, tt)

    def from_sibling(i):
        tt = places[i]
        link(h_buf.at[slot_of(1 - k, tt)], c_s.at[0], c_r.at[tt], sibling).wait_recv()

    def add(slots, fresh=False):
        for w in range(3):
            acc[w] = project(slots, w) if fresh else acc[w] + project(slots, w)

    from_beside(0)
    from_line(1)
    from_line(2)
    from_sibling(0)
    add([slot_of(k, t), slot_of(1 - k, t)], True)
    from_beside(2)
    from_beside(1)
    from_line(3)
    from_sibling(1)
    add([slot_of(k, pair), slot_of(1 - k, pair)])
    from_beside(3)
    from_sibling(2)
    add([slot_of(k, across), slot_of(1 - k, across), slot_of(k, diagonal)])
    from_sibling(n_tp - 1)
    part_copies = []
    for w in range(3):
        whole = acc[w] + project([slot_of(1 - k, diagonal)], w)
        for head in range(n_ctx):
            piece = whole[:, head * HD : (head + 1) * HD]
            if w == 0:
                for x in range(n_ctx):
                    q_part[head, x * rows_count : (x + 1) * rows_count] = piece[
                        x * all_rows : x * all_rows + rows_count
                    ]
            else:
                kv_part[head, w - 1] = piece
                kv_send[head, w - 1] = piece.astype(jnp.bfloat16)
        if w == 0:
            copy = remote(q_part.at[other], q_in, p_s.at[0], p_r.at[0], partner)
        else:
            copy = remote(
                kv_send.at[other, w - 1], kv_in.at[w - 1], p_s.at[1], p_r.at[w], partner
            )
        copy.start()
        part_copies.append(copy)
    pltpu.make_async_copy(cache_buf.at[0], cache_buf.at[0], local_sem.at[2]).wait()
    cache_copies[0].wait_recv()
    both_caches = remote(
        cache_buf.at[0], cache_buf.at[0], cache_s.at[1], cache_r.at[1], partner
    )
    both_caches.wait_recv()
    query_group = (lax.broadcasted_iota(jnp.int32, (queries, total_rows), 0) % rows_count) // ch
    key_group = (lax.broadcasted_iota(jnp.int32, (queries, total_rows), 1) % all_rows) // ch
    flight_seen = jnp.logical_or(key_group == flight, key_group <= query_group)

    part_copies[0].wait_recv()
    q = (q_part[c] + q_in[...]).astype(jnp.bfloat16)
    scale = 1.0 / math.sqrt(HD)

    def score(keys):
        return (
            lax.dot_general(q, keys, (((1,), (1,)), ((), ())), preferred_element_type=jnp.float32)
            * scale
        )

    scores = []
    for x in range(n_ctx):
        plain = score(cache_buf[x, 0])
        scores.append(
            jnp.concatenate(
                [
                    plain[b * ch : (b + 1) * ch] + seen_buf[x, b % flight : b % flight + 1]
                    for b in range(n_ctx * flight)
                ],
                axis=0,
            )
        )
    peak = jnp.max(jnp.maximum(scores[0], scores[1]), axis=1, keepdims=True)
    part_copies[1].wait_recv()
    key = (kv_part[c, 0] + kv_in[0].astype(jnp.float32)).astype(jnp.bfloat16)
    scores.append(jnp.where(flight_seen, score(key), -jnp.inf))
    peak = jnp.maximum(peak, jnp.max(scores[-1], axis=1, keepdims=True))
    weights = [jnp.exp(v - peak).astype(jnp.bfloat16) for v in scores]
    denom = sum(jnp.sum(w.astype(jnp.float32), axis=1, keepdims=True) for w in weights)
    numer = sum(
        jnp.dot(weights[x], cache_buf[x, 1], preferred_element_type=jnp.float32)
        for x in range(n_ctx)
    )
    part_copies[2].wait_recv()
    value = (kv_part[c, 1] + kv_in[1].astype(jnp.float32)).astype(jnp.bfloat16)
    numer = numer + jnp.dot(weights[-1], value, preferred_element_type=jnp.float32)
    attention = (numer / denom).astype(jnp.bfloat16)
    att_buf[k * n_ctx + c] = attention
    for device in (partner, (u * per + (1 - k), other, t), sibling):
        link(att_buf.at[k * n_ctx + c], t_s.at[0], t_r.at[0], device).start()

    for x in range(n_ctx):
        last = slice(x * all_rows + rows_count, (x + 1) * all_rows)
        kv_buf[x, 0] = key[last]
        kv_buf[x, 1] = value[last]
    fin_copy = remote(kv_buf.at[other], fin_in, f_s.at[0], f_r.at[0], partner)
    fin_copy.start()
    nk_ref[:, own_lanes] = kv_buf[c, 0]
    nv_ref[:, own_lanes] = kv_buf[c, 1]

    wo_copy.wait_recv()
    shared = att_buf.at[: per * n_ctx - 1]
    att_all = link(shared, t_s.at[0], t_r.at[0], partner)
    att_all.wait_recv()
    order = peers + [t]

    def heads_of(core):
        return jnp.concatenate([att_buf[core * n_ctx + x] for x in range(n_ctx)], axis=1)

    ours, theirs = heads_of(k), heads_of(1 - k)
    for i, tt in enumerate(order):
        y_part[i] = jnp.dot(
            ours, wo_cut[slot_of(k, tt)], preferred_element_type=jnp.float32
        ) + jnp.dot(theirs, wo_sib[tt], preferred_element_type=jnp.float32)

        def chunk(x, start, size):
            at = pl.ds(pl.multiple_of(x * rows_count + start, ch), size)
            return y_part[i, at, :]

        far_a[i] = chunk(other, 0, first).astype(jnp.bfloat16)
        remote(far_a.at[i], cross_a.at[tt, u], fa_s.at[0], xa_r.at[tt], owner).start()
        near_a[i] = chunk(c, 0, first).astype(jnp.bfloat16)
        near = remote(near_a.at[i], cross_a.at[tt, u], na_s.at[0], xa_r.at[tt], beside)
        pl.when(jnp.logical_not(at_home))(near.start)

        if i < n_tp - 1:
            for x in range(n_ctx):
                zb_send[i, x] = chunk(x, first, late).astype(jnp.bfloat16)
            remote(zb_send.at[i], zb_in.at[t], zb_s.at[0], zb_r.at[0], zpeer(tt)).start()

    fin_copy.wait_recv()
    nk_ref[:, other_lanes] = fin_in[0]
    nv_ref[:, other_lanes] = fin_in[1]

    def both_sources(ref, send, recv):
        @pl.when(at_home)
        def _():
            remote(ref.at[0], ref.at[0], send, recv, partner).wait_recv()

        @pl.when(jnp.logical_not(at_home))
        def _():
            remote(ref, ref, send, recv, partner).wait_recv()

    for i, tt in enumerate(order):

        @pl.when(at_home)
        def _():
            cross_a[tt, u] = near_a[i]

        both_sources(cross_a.at[tt], fa_s.at[0], xa_r.at[tt])
        summed_a = cross_a[tt, 0].astype(jnp.float32) + cross_a[tt, 1].astype(jnp.float32)
        if i < n_tp - 1:
            za_send[i] = summed_a.astype(jnp.bfloat16)
            remote(za_send.at[i], za_in.at[t], za_s.at[0], za_r.at[0], zpeer(tt)).start()

    link(zb_send, zb_s.at[0], zb_r.at[0], partner).wait_recv()

    def gathered(x):
        at = pl.ds(pl.multiple_of(x * rows_count + first, ch), late)
        result = y_part[n_tp - 1, at, :]
        for tt in peers:
            result = result + zb_in[tt, x].astype(jnp.float32)
        return result.astype(jnp.bfloat16)

    far_b[...] = gathered(other)
    far_copy = remote(far_b, cross_b.at[u], fb_s.at[0], xb_r.at[0], owner)
    far_copy.start()
    near_b[...] = gathered(c)
    near_copy = remote(near_b, cross_b.at[u], nb_s.at[0], xb_r.at[0], beside)
    pl.when(jnp.logical_not(at_home))(near_copy.start)

    link(za_send, za_s.at[0], za_r.at[0], partner).wait_recv()
    for tt in peers:
        summed_a = summed_a + za_in[tt].astype(jnp.float32)

    @pl.when(at_home)
    def _():
        cross_b[u] = near_b[...]

    both_sources(cross_b, fb_s.at[0], xb_r.at[0])
    summed_b = cross_b[0].astype(jnp.float32) + cross_b[1].astype(jnp.float32)
    y_rows = jnp.concatenate([summed_a, summed_b], axis=0)
    ssy_buf[0] = row_squares(y_rows, lanes)[0:1]
    for d in range(1, members):
        remote(
            ssy_buf.at[0], ssy_buf.at[d], ssy_s.at[0], ssy_r.at[0], member((j + d) % members)
        ).start()
    ssq_wait(lambda copy: copy.wait_send())
    slots = n_tp - 1
    for ref, send in (
        (h_buf.at[:slots, 0], b_s),
        (h_buf.at[: n_tp // n_ctx], n_s),
        (h_buf.at[:n_tp], c_s),
        (kv_send.at[0], p_s.at[1:]),
        (shared, t_s),
        (far_a, fa_s),
        (za_send, za_s),
        (zb_send, zb_s),
    ):
        link(ref, send.at[0], send.at[0], partner).wait_send()
    for copy in [a_copy, cache_copies[0], both_caches, part_copies[0], wo_copy, fin_copy, far_copy]:
        copy.wait_send()

    @pl.when(jnp.logical_not(at_home))
    def _():
        link(near_a, na_s.at[0], na_s.at[0], partner).wait_send()
        near_copy.wait_send()

    rest = ssy_buf.at[1:]
    ssy_all = remote(rest, rest, ssy_s.at[0], ssy_r.at[0], partner)
    ssy_all.wait_recv()
    total = ssy_buf[0]
    for d in range(1, members):
        total = total + ssy_buf[d]
    inverse = lax.rsqrt(jnp.transpose(jnp.broadcast_to(total, (8, lanes)))[:rows_count, 0:1] / D + epsilon)
    velocity = y_rows * inverse * og_ref[...].reshape(1, width)
    for f in range(flight):
        now = levels_ref[noise_ref[f]]
        after = levels_ref[noise_ref[f] + 1]
        out_ref[f] = state_ref[f] + (after - now) * velocity[f * ch : (f + 1) * ch]
    ssy_all.wait_send()


def y_rows_first(rows_count):
    return 3 * (rows_count // 4)


def write_out(*refs):
    sems = refs[6]
    copies = [pltpu.make_async_copy(refs[i], refs[3 + i], sems.at[i]) for i in range(3)]
    for copy in copies:
        copy.start()
    for copy in copies:
        copy.wait()


def fused(dims, *args):
    state, clean_tokens, w_query = args[0], args[1], args[2]
    w_out, cache_keys = args[5], args[6]
    n_grp, n_ctx, n_tp = dims
    per = n_grp // n_ctx
    members = n_grp * n_tp
    flight, ch, width = state.shape
    rows_count = flight * ch
    first = y_rows_first(rows_count)
    late = rows_count - first
    all_rows = rows_count + ch
    total = n_ctx * all_rows
    lanes = -(-all_rows // 128) * 128
    queries = n_ctx * rows_count
    cache_dev = cache_keys.shape[0]
    bf, fl = jnp.bfloat16, jnp.float32
    dma = pltpu.SemaphoreType.DMA
    vm = pl.BlockSpec(memory_space=pltpu.VMEM)
    hbm = pl.BlockSpec(memory_space=pltpu.HBM)

    def pair(count):
        return [dma((count,))] * 2

    scratch = [
        pltpu.VMEM(state.shape, fl),
        pltpu.VMEM(clean_tokens.shape, bf),
        pltpu.VMEM((width,), fl),
        pltpu.VMEM((width,), fl),
        pltpu.VMEM((width,), fl),
        *[pltpu.SMEM(a.shape, a.dtype) for a in args[11:]],
        pltpu.VMEM((3,) + w_query.shape, bf),
        pltpu.VMEM(w_out.shape, bf),
        pltpu.VMEM((per * n_tp, w_out.shape[0], width), bf),
        pltpu.VMEM((n_tp, w_out.shape[0], width), bf),
        pltpu.VMEM((n_ctx, 2, cache_dev, HD), bf),
        pltpu.VMEM((n_ctx, 8, cache_dev), fl),
        pltpu.VMEM((1, lanes), fl),
        pltpu.VMEM((members, 1, lanes), fl),
        pltpu.VMEM((members, 1, lanes), fl),
        pltpu.VMEM((all_rows, width), fl),
        pltpu.VMEM((all_rows, width), fl),
        pltpu.VMEM((per * n_tp, n_ctx, all_rows, width), bf),
        pltpu.VMEM((3, total, n_ctx * HD), fl),
        pltpu.VMEM((n_ctx, queries, HD), fl),
        pltpu.VMEM((queries, HD), fl),
        pltpu.VMEM((n_ctx, 2, total, HD), fl),
        pltpu.VMEM((n_ctx, 2, total, HD), bf),
        pltpu.VMEM((2, total, HD), bf),
        pltpu.VMEM((n_ctx, 2, ch, HD), bf),
        pltpu.VMEM((2, ch, HD), bf),
        pltpu.VMEM((per * n_ctx, queries, HD), bf),
        pltpu.VMEM((n_tp, queries, width), fl),
        pltpu.VMEM((n_tp, first, width), bf),
        pltpu.VMEM((n_tp, first, width), bf),
        pltpu.VMEM((n_tp, n_ctx, first, width), bf),
        pltpu.VMEM((n_tp - 1, first, width), bf),
        pltpu.VMEM((n_tp, first, width), bf),
        pltpu.VMEM((n_tp - 1, n_ctx, late, width), bf),
        pltpu.VMEM((n_tp, n_ctx, late, width), bf),
        pltpu.VMEM((late, width), bf),
        pltpu.VMEM((late, width), bf),
        pltpu.VMEM((n_ctx, late, width), bf),
        dma((12,)),
        *pair(2),
        *pair(1),
        *pair(1),
        dma((1,)),
        dma((n_tp,)),
        dma((1,)),
        dma((n_tp,)),
        dma((1,)),
        dma((n_tp,)),
        dma((2,)),
        dma((3,)),
        *pair(1),
        *pair(1),
        *pair(1),
        dma((1,)),
        dma((1,)),
        dma((n_tp,)),
        *pair(1),
        *pair(1),
        dma((1,)),
        dma((1,)),
        dma((1,)),
        *pair(1),
    ]
    results = pl.pallas_call(
        functools.partial(kernel, dims),
        out_shape=(
            pltpu.VMEM(state.shape, fl),
            pltpu.VMEM((ch, cache_keys.shape[1]), bf),
            pltpu.VMEM((ch, cache_keys.shape[1]), bf),
        ),
        in_specs=[hbm] * 15,
        out_specs=(vm, vm, vm),
        scratch_shapes=scratch,
        compiler_params=pltpu.CompilerParams(
            collective_id=0, has_side_effects=True, vmem_limit_bytes=VMEM_LIMIT
        ),
    )(*args)
    return pl.pallas_call(
        write_out,
        out_shape=tuple(jax.ShapeDtypeStruct(r.shape, r.dtype) for r in results),
        in_specs=[vm] * 3,
        out_specs=(hbm,) * 3,
        scratch_shapes=[dma((3,))],
    )(*[pltpu.with_memory_space_constraint(r, pltpu.VMEM) for r in results])


def step(dims, *args):
    n_grp, n_ctx, n_tp = dims
    heads_dev = args[6].shape[1] // HD
    if n_ctx == heads_dev == 2 and n_grp == n_tp == 4 and args[0].shape[0] == 4:
        return fused(dims, *args)
    return local(*args)


def solution(mesh):
    dims = tuple(mesh.shape[name] for name in ("grp", "ctx", "tp"))
    return jax.shard_map(
        functools.partial(step, dims),
        mesh=mesh,
        in_specs=(
            P(None, "ctx", ("grp", "tp")),
            P("ctx", ("grp", "tp")),
            P("ctx", ("grp", "tp")),
            P("ctx", ("grp", "tp")),
            P("ctx", ("grp", "tp")),
            P(("grp", "tp"), "ctx"),
            P("ctx", ("grp", "tp")),
            P("ctx", ("grp", "tp")),
            P(("grp", "tp")),
            P(("grp", "tp")),
            P(("grp", "tp")),
            P(),
            P(),
            P("ctx"),
            P(),
        ),
        out_specs=(P(None, "ctx", ("grp", "tp")), P("ctx", ("grp", "tp")), P("ctx", ("grp", "tp"))),
        check_vma=False,
    )
```

```python
import functools
import math

import jax
import jax.numpy as jnp
from jax import lax
from jax.experimental import pallas as pl
from jax.experimental.pallas import tpu as pltpu
from jax.sharding import PartitionSpec as P

D = 5120
HD = 128
SLOT = 256


epsilon = 1e-06


def level_lookup(levels, indices):
    table = jnp.arange(levels.shape[0], dtype=jnp.int32)
    picked = (indices[:, None] == table[None, :]).astype(jnp.float32)
    return jnp.sum(picked * levels[None, :], axis=1)


def normalize_rows(rows, sigma_rows, norm_gain, mod_gain):
    squares = lax.psum(jnp.sum(rows * rows, axis=1), ("grp", "tp"))
    inverse = lax.rsqrt(squares / D + epsilon)
    scaled = (
        rows
        * inverse[:, None]
        * norm_gain[None, :]
        * (1.0 + sigma_rows[:, None] * mod_gain[None, :])
    )
    return lax.all_gather(scaled.astype(jnp.bfloat16), ("grp", "tp"), axis=1, tiled=True)


def local(
    state,
    clean_tokens,
    w_query,
    w_key,
    w_value,
    w_out,
    cache_keys,
    cache_values,
    norm_gain,
    mod_gain,
    out_gain,
    levels,
    noise_index,
    placement,
    group_mask,
):
    flight, ch_dev, local_width = state.shape
    ctx_count = lax.axis_size("ctx")
    group = ch_dev * ctx_count
    cache_dev = cache_keys.shape[0]
    slots_dev = cache_dev // SLOT
    heads_dev = cache_keys.shape[1] // HD
    rows_count = flight * ch_dev
    scale = 1.0 / math.sqrt(HD)
    wk_full, wv_full, wo_full = (
        lax.all_gather(w_key, "ctx", axis=0, tiled=True),
        lax.all_gather(w_value, "ctx", axis=0, tiled=True),
        lax.all_gather(w_out, "ctx", axis=1, tiled=True),
    )
    group_table = jnp.arange(group_mask.shape[1], dtype=jnp.int32)
    slot_onehot = (placement[:, None] == group_table[None, :]).astype(jnp.int32)
    slot_seen = jnp.sum(slot_onehot[None, :, :] * group_mask[:, None, :], axis=2) > 0
    cache_seen = slot_seen[:, None, None, :, None]
    own_group = jnp.arange(flight, dtype=jnp.int32)
    flight_seen = (own_group[None, :] <= own_group[:, None])[:, None, None, :, None]
    cache_k = cache_keys.reshape(slots_dev, SLOT, heads_dev, HD)
    cache_v = cache_values.reshape(slots_dev, SLOT, heads_dev, HD)
    finished_keys = None
    finished_values = None
    current = level_lookup(levels, noise_index + 0)
    following = level_lookup(levels, noise_index + 0 + 1)
    rows = state.reshape(rows_count, local_width)
    sigma_rows = jnp.repeat(current, ch_dev)
    rows = jnp.concatenate([rows, clean_tokens.astype(jnp.float32)], axis=0)
    sigma_rows = jnp.concatenate([sigma_rows, jnp.zeros((ch_dev,), jnp.float32)])
    features = normalize_rows(rows, sigma_rows, norm_gain, mod_gain)
    keys_new = jnp.dot(features, wk_full, preferred_element_type=jnp.float32).astype(jnp.bfloat16)
    values_new = jnp.dot(features, wv_full, preferred_element_type=jnp.float32).astype(jnp.bfloat16)
    finished_keys = keys_new[rows_count:]
    finished_values = values_new[rows_count:]
    keys_new = keys_new[:rows_count]
    values_new = values_new[:rows_count]
    noisy = features[:rows_count]
    pieces = lax.all_to_all(
        noisy.reshape(flight, ch_dev, -1), "ctx", split_axis=2, concat_axis=1, tiled=True
    )
    partial_q = jnp.einsum("fqd,de->fqe", pieces, w_query, preferred_element_type=jnp.float32)
    queries = lax.psum(partial_q, "ctx").astype(jnp.bfloat16)
    query_heads = queries.reshape(flight, group, heads_dev, HD)
    finished_k = finished_keys.reshape(ch_dev, heads_dev, HD)
    finished_v = finished_values.reshape(ch_dev, heads_dev, HD)
    flight_k = keys_new.reshape(flight, ch_dev, heads_dev, HD)
    flight_v = values_new.reshape(flight, ch_dev, heads_dev, HD)
    cache_scores = (
        jnp.einsum("fqhd,sthd->fqhst", query_heads, cache_k, preferred_element_type=jnp.float32)
        * scale
    )
    finished_scores = (
        jnp.einsum("fqhd,thd->fqht", query_heads, finished_k, preferred_element_type=jnp.float32)
        * scale
    )
    flight_scores = (
        jnp.einsum("fqhd,gthd->fqhgt", query_heads, flight_k, preferred_element_type=jnp.float32)
        * scale
    )
    peak = jnp.max(finished_scores, axis=3)
    peak = jnp.maximum(peak, jnp.max(jnp.where(cache_seen, cache_scores, -jnp.inf), axis=(3, 4)))
    peak = jnp.maximum(peak, jnp.max(jnp.where(flight_seen, flight_scores, -jnp.inf), axis=(3, 4)))
    peak = lax.pmax(peak, "ctx")
    cache_p = jnp.where(cache_seen, jnp.exp(cache_scores - peak[..., None, None]), 0.0).astype(
        jnp.bfloat16
    )
    finished_p = jnp.exp(finished_scores - peak[..., None]).astype(jnp.bfloat16)
    flight_p = jnp.where(flight_seen, jnp.exp(flight_scores - peak[..., None, None]), 0.0).astype(
        jnp.bfloat16
    )
    numer = jnp.einsum("fqhst,sthd->fqhd", cache_p, cache_v, preferred_element_type=jnp.float32)
    numer = numer + jnp.einsum(
        "fqht,thd->fqhd", finished_p, finished_v, preferred_element_type=jnp.float32
    )
    numer = numer + jnp.einsum(
        "fqhgt,gthd->fqhd", flight_p, flight_v, preferred_element_type=jnp.float32
    )
    denom = jnp.sum(cache_p, axis=(3, 4), dtype=jnp.float32)
    denom = denom + jnp.sum(finished_p, axis=3, dtype=jnp.float32)
    denom = denom + jnp.sum(flight_p, axis=(3, 4), dtype=jnp.float32)
    numer, denom = (
        lax.psum_scatter(
            numer.reshape(flight, group, heads_dev * HD), "ctx", scatter_dimension=1, tiled=True
        ),
        lax.psum_scatter(denom, "ctx", scatter_dimension=1, tiled=True),
    )
    attention = numer.reshape(flight, ch_dev, heads_dev, HD) / denom[..., None]
    attention = attention.astype(jnp.bfloat16).reshape(rows_count, heads_dev * HD)
    partial_y = jnp.dot(attention, wo_full, preferred_element_type=jnp.float32)
    y_rows = lax.psum_scatter(partial_y, ("grp", "tp"), scatter_dimension=1, tiled=True)
    y_squares = lax.psum(jnp.sum(y_rows * y_rows, axis=1), ("grp", "tp"))
    velocity = y_rows * lax.rsqrt(y_squares / D + epsilon)[:, None] * out_gain[None, :]
    state = state + (following - current)[:, None, None] * velocity.reshape(
        flight, ch_dev, local_width
    )
    return (state, finished_keys, finished_values)


MESH = pl.DeviceIdType.MESH
VMEM_LIMIT = 62 * 1024 * 1024


def remote(src, dst, send, recv, device):
    return pltpu.make_async_remote_copy(
        src_ref=src,
        dst_ref=dst,
        send_sem=send,
        recv_sem=recv,
        device_id=device,
        device_id_type=MESH,
    )


def row_squares(rows, lanes):
    squares = rows * rows
    count = squares.shape[0]
    if count < lanes:
        squares = jnp.concatenate(
            [squares, jnp.zeros((lanes - count, squares.shape[1]), jnp.float32)], axis=0
        )
    pad = -squares.shape[1] % 128
    if pad:
        squares = jnp.concatenate(
            [squares, jnp.zeros((squares.shape[0], pad), jnp.float32)], axis=1
        )
    folded = squares[:, :128]
    for start in range(128, squares.shape[1], 128):
        folded = folded + squares[:, start : start + 128]
    return jnp.sum(jnp.transpose(folded), axis=0, keepdims=True)


def kernel(
    dims,
    state_hbm,
    clean_hbm,
    wq_hbm,
    wk_hbm,
    wv_hbm,
    wo_hbm,
    ck_hbm,
    cv_hbm,
    ng_hbm,
    mg_hbm,
    og_hbm,
    levels_hbm,
    noise_hbm,
    place_hbm,
    mask_hbm,
    out_ref,
    nk_ref,
    nv_ref,
    state_ref,
    clean_ref,
    ng_ref,
    mg_ref,
    og_ref,
    levels_ref,
    noise_ref,
    place_ref,
    mask_ref,
    w_buf,
    wo_buf,
    wo_cut,
    wo_sib,
    cache_buf,
    seen_buf,
    ssq_own,
    ssq_buf,
    ssy_buf,
    raw,
    raw_in,
    h_buf,
    acc,
    q_part,
    q_in,
    kv_part,
    kv_send,
    kv_in,
    kv_buf,
    fin_in,
    att_buf,
    y_part,
    near_a,
    far_a,
    cross_a,
    za_send,
    za_in,
    zb_send,
    zb_in,
    near_b,
    far_b,
    cross_b,
    local_sem,
    cache_s,
    cache_r,
    ssq_s,
    ssq_r,
    a_s,
    a_r,
    b_s,
    b_r,
    n_s,
    n_r,
    c_s,
    c_r,
    p_s,
    p_r,
    f_s,
    f_r,
    t_s,
    t_r,
    wo_s,
    wo_r,
    fa_s,
    na_s,
    xa_r,
    za_s,
    za_r,
    zb_s,
    zb_r,
    fb_s,
    nb_s,
    xb_r,
    ssy_s,
    ssy_r,
):
    n_grp, n_ctx, n_tp = dims
    per = n_grp // n_ctx
    members = n_grp * n_tp
    flight, ch, width = state_hbm.shape
    rows_count = flight * ch
    first = y_rows_first(rows_count)
    late = rows_count - first
    all_rows = rows_count + ch
    cache_dev = ck_hbm.shape[0]
    lanes = ssq_buf.shape[2]
    total_rows = n_ctx * all_rows
    queries = n_ctx * rows_count
    g, c, t = lax.axis_index("grp"), lax.axis_index("ctx"), lax.axis_index("tp")
    u, k = g // per, g % per
    j = g * n_tp + t
    other = 1 - c
    partner = (g, other, t)
    sibling = (u * per + (1 - k), c, t)
    beside = ((1 - u) * per + k, c, t)
    held = 1 - u
    at_home = u == c
    owner = (c * per + k, other, t)

    def member(index):
        return (index // n_tp, c, index % n_tp)

    side = t // (n_tp // 2)
    inner = t + side * (n_tp - 1 - 2 * t)
    peers = []
    for i in range(n_tp - 1):
        v = n_tp - 1 - i
        p = v - (inner - v + n_tp) // n_tp
        peers.append(p + side * (n_tp - 1 - 2 * p))
    pair = t + 1 - 2 * (t % 2)
    span = n_tp // 2
    across = (t + span) % n_tp
    diagonal = (pair + span) % n_tp
    places = [t, pair, across, diagonal]

    def zpeer(tt):
        return (g, c, tt)

    own_pair, far_pair = u * per, (1 - u) * per
    barrier = pltpu.get_barrier_semaphore()
    for tt in peers + [t]:
        for dc in reversed(range(n_ctx)):
            for core in (far_pair, own_pair):
                for dk in reversed(range(per)):
                    if tt is t and dc + dk == 0 and core is own_pair:
                        continue
                    pl.semaphore_signal(
                        barrier,
                        inc=1,
                        device_id=(core + (k + dk) % per, (c + dc) % n_ctx, tt),
                        device_id_type=MESH,
                    )

    loads = [
        pltpu.make_async_copy(src, w_buf.at[i], local_sem.at[0])
        for i, src in enumerate((wq_hbm, wk_hbm, wv_hbm))
    ]
    wo_load = pltpu.make_async_copy(wo_hbm, wo_buf, local_sem.at[1])
    own_lanes = pl.ds(pl.multiple_of(c * HD, HD), HD)
    other_lanes = pl.ds(pl.multiple_of(other * HD, HD), HD)
    cache_loads = [
        pltpu.make_async_copy(src.at[:, own_lanes], cache_buf.at[c, i], local_sem.at[2])
        for i, src in enumerate((ck_hbm, cv_hbm))
    ]
    small = [
        pltpu.make_async_copy(src, dst, local_sem.at[3 + i])
        for i, (src, dst) in enumerate(
            [
                (state_hbm, state_ref),
                (clean_hbm, clean_ref),
                (ng_hbm, ng_ref),
                (mg_hbm, mg_ref),
                (og_hbm, og_ref),
                (levels_hbm, levels_ref),
                (noise_hbm, noise_ref),
                (place_hbm, place_ref),
                (mask_hbm, mask_ref),
            ]
        )
    ]
    for copy in small + [wo_load] + loads + cache_loads:
        copy.start()
    for copy in small:
        copy.wait()

    rows = jnp.concatenate(
        [state_ref[...].reshape(rows_count, width), clean_ref[...].astype(jnp.float32)], axis=0
    )
    ssq_own[...] = row_squares(rows, lanes)

    @pl.when(c == held)
    def _():
        ssq_buf[j] = ssq_own[...]

    modulation = mg_ref[...].reshape(1, width)
    gained = rows * ng_ref[...].reshape(1, width)
    for f in range(flight):
        sigma = levels_ref[noise_ref[f]]
        raw[f * ch : (f + 1) * ch] = gained[f * ch : (f + 1) * ch] * (1.0 + sigma * modulation)
    raw[rows_count:] = gained[rows_count:]
    line = lax.broadcasted_iota(jnp.int32, (8, SLOT), 0)
    for s in range(cache_dev // SLOT):
        block = jnp.zeros((8, SLOT), jnp.float32)
        for f in range(flight):
            hidden = jnp.where(mask_ref[f, place_ref[s]] != 0, 0.0, -jnp.inf)
            block = jnp.where(line == f, hidden, block)
        seen_buf[c, :, s * SLOT : (s + 1) * SLOT] = block
    pl.semaphore_wait(barrier, n_grp * n_ctx * n_tp - 1)

    def ssq_copy(target):
        return remote(ssq_own, ssq_buf.at[j], ssq_s.at[0], ssq_r.at[0], target)

    for dk in range(per):
        for dc in range(n_ctx):
            for dt in range(n_tp):
                copy = ssq_copy(
                    ((1 - c) * per + (k + dk) % per, (c + dc) % n_ctx, (t + dt) % n_tp)
                )
                if dk + dc + dt > 0:
                    copy.start()
                else:
                    pl.when(c != held)(copy.start)
    a_copy = remote(raw, raw_in, a_s.at[0], a_r.at[0], ((1 - c) * per + k, u, t))
    a_copy.start()
    wo_load.wait()
    for block in range(per * n_tp):
        wo_cut[block] = wo_buf[:, block * width : (block + 1) * width]
    wo_copy = remote(
        wo_cut.at[pl.ds((1 - k) * n_tp, n_tp)], wo_sib, wo_s.at[0], wo_r.at[0], sibling
    )
    wo_copy.start()

    def ssq_wait(finish):
        @pl.when(c == held)
        def _():
            most = ssq_buf.at[: members - 1]
            finish(remote(most, most, ssq_s.at[0], ssq_r.at[0], partner))

        @pl.when(c != held)
        def _():
            finish(remote(ssq_buf, ssq_buf, ssq_s.at[0], ssq_r.at[0], partner))

    ssq_wait(lambda copy: copy.wait_recv())
    total = ssq_buf[0]
    for d in range(1, members):
        total = total + ssq_buf[d]
    inverse = lax.rsqrt(jnp.transpose(jnp.broadcast_to(total, (8, lanes)))[:all_rows, 0:1] / D + epsilon)
    a_copy.wait_recv()
    mine = k * n_tp + t
    h_buf[mine, held] = (raw_in[...] * inverse).astype(jnp.bfloat16)

    def slot_of(core, tt):
        return core * n_tp + tt

    def link(ref, send, recv, device):
        return remote(ref, ref, send, recv, device)

    def to_beside(x, tt):
        link(h_buf.at[slot_of(k, tt), x], n_s.at[0], n_r.at[tt], beside).start()

    def to_sibling(x, tt):
        link(h_buf.at[slot_of(k, tt), x], c_s.at[0], c_r.at[tt], sibling).start()

    def to_line(tt, device):
        link(h_buf.at[slot_of(k, tt), held], b_s.at[0], b_r.at[tt], device).start()

    for tt in (across, pair):
        to_line(t, zpeer(tt))
    to_beside(held, t)
    to_sibling(held, t)

    cache_copies = [
        remote(seen_buf.at[c], seen_buf.at[c], cache_s.at[0], cache_r.at[0], partner)
    ] + [
        remote(
            src.at[:, other_lanes], cache_buf.at[c, i], cache_s.at[1], cache_r.at[1], partner
        )
        for i, src in enumerate((ck_hbm, cv_hbm))
    ]
    for copy in cache_copies:
        copy.start()

    pltpu.make_async_copy(w_buf, w_buf, local_sem.at[0]).wait()

    def project(slots, w):
        total = None
        for slot in slots:
            lhs = h_buf[slot].reshape(total_rows, width)
            depth = pl.ds(pl.multiple_of(slot * width, 64), width)
            product = jnp.dot(lhs, w_buf[w, depth, :], preferred_element_type=jnp.float32)
            total = product if total is None else total + product
        return total

    def from_line(i):
        tt = places[i]
        link(h_buf.at[slot_of(k, tt), held], b_s.at[0], b_r.at[tt], partner).wait_recv()
        if i == 1:
            to_beside(held, tt)
        if i == 2:
            to_line(tt, zpeer(pair))
        to_sibling(held, tt)

    def from_beside(i):
        tt = places[i]
        link(h_buf.at[slot_of(k, tt), u], n_s.at[0], n_r.at[tt], beside).wait_recv()
        if i in (0, 2):
            place = across if i == 0 else pair
            link(h_buf.at[slot_of(k, tt), u], n_s.at[0], n_r.at[tt], zpeer(place)).start()
        to_sibling(u, tt)

    def from_sibling(i):
        tt = places[i]
        link(h_buf.at[slot_of(1 - k, tt)], c_s.at[0], c_r.at[tt], sibling).wait_recv()

    def add(slots, fresh=False):
        for w in range(3):
            acc[w] = project(slots, w) if fresh else acc[w] + project(slots, w)

    from_beside(0)
    from_line(1)
    from_line(2)
    from_sibling(0)
    add([slot_of(k, places[0]), slot_of(1 - k, places[0])], True)
    from_beside(2)
    from_beside(1)
    from_line(3)
    from_beside(3)
    from_sibling(1)
    from_sibling(2)
    add([slot_of(k, places[1]), slot_of(1 - k, places[1]), slot_of(k, places[2]), slot_of(1 - k, places[2]), slot_of(k, places[3])])
    from_sibling(3)
    part_copies = []
    for w in range(3):
        whole = acc[w] + project([slot_of(1 - k, places[3])], w)
        for head in range(n_ctx):
            piece = whole[:, head * HD : (head + 1) * HD]
            if w == 0:
                for x in range(n_ctx):
                    q_part[head, x * rows_count : (x + 1) * rows_count] = piece[
                        x * all_rows : x * all_rows + rows_count
                    ]
            else:
                kv_part[head, w - 1] = piece
                kv_send[head, w - 1] = piece.astype(jnp.bfloat16)
        if w == 0:
            copy = remote(q_part.at[other], q_in, p_s.at[0], p_r.at[0], partner)
        else:
            copy = remote(
                kv_send.at[other, w - 1], kv_in.at[w - 1], p_s.at[1], p_r.at[w], partner
            )
        copy.start()
        part_copies.append(copy)
    pltpu.make_async_copy(cache_buf.at[0], cache_buf.at[0], local_sem.at[2]).wait()
    cache_copies[0].wait_recv()
    both_caches = remote(
        cache_buf.at[0], cache_buf.at[0], cache_s.at[1], cache_r.at[1], partner
    )
    both_caches.wait_recv()
    query_group = (lax.broadcasted_iota(jnp.int32, (queries, total_rows), 0) % rows_count) // ch
    key_group = (lax.broadcasted_iota(jnp.int32, (queries, total_rows), 1) % all_rows) // ch
    flight_seen = jnp.logical_or(key_group == flight, key_group <= query_group)

    part_copies[0].wait_recv()
    q = (q_part[c] + q_in[...]).astype(jnp.bfloat16)
    scale = 1.0 / math.sqrt(HD)

    def score(keys):
        return (
            lax.dot_general(q, keys, (((1,), (1,)), ((), ())), preferred_element_type=jnp.float32)
            * scale
        )

    scores = []
    for x in range(n_ctx):
        plain = score(cache_buf[x, 0])
        scores.append(
            jnp.concatenate(
                [
                    plain[b * ch : (b + 1) * ch] + seen_buf[x, b % flight : b % flight + 1]
                    for b in range(n_ctx * flight)
                ],
                axis=0,
            )
        )
    peak = jnp.max(jnp.maximum(scores[0], scores[1]), axis=1, keepdims=True)
    part_copies[1].wait_recv()
    key = (kv_part[c, 0] + kv_in[0].astype(jnp.float32)).astype(jnp.bfloat16)
    scores.append(jnp.where(flight_seen, score(key), -jnp.inf))
    peak = jnp.maximum(peak, jnp.max(scores[-1], axis=1, keepdims=True))
    weights = [jnp.exp(v - peak).astype(jnp.bfloat16) for v in scores]
    denom = sum(jnp.sum(w.astype(jnp.float32), axis=1, keepdims=True) for w in weights)
    numer = sum(
        jnp.dot(weights[x], cache_buf[x, 1], preferred_element_type=jnp.float32)
        for x in range(n_ctx)
    )
    part_copies[2].wait_recv()
    value = (kv_part[c, 1] + kv_in[1].astype(jnp.float32)).astype(jnp.bfloat16)
    numer = numer + jnp.dot(weights[-1], value, preferred_element_type=jnp.float32)
    attention = (numer / denom).astype(jnp.bfloat16)
    att_buf[k * n_ctx + c] = attention
    for device in (partner, (u * per + (1 - k), other, t), sibling):
        link(att_buf.at[k * n_ctx + c], t_s.at[0], t_r.at[0], device).start()

    for x in range(n_ctx):
        last = slice(x * all_rows + rows_count, (x + 1) * all_rows)
        kv_buf[x, 0] = key[last]
        kv_buf[x, 1] = value[last]
    fin_copy = remote(kv_buf.at[other], fin_in, f_s.at[0], f_r.at[0], partner)
    fin_copy.start()
    nk_ref[:, own_lanes] = kv_buf[c, 0]
    nv_ref[:, own_lanes] = kv_buf[c, 1]

    wo_copy.wait_recv()
    shared = att_buf.at[: per * n_ctx - 1]
    att_all = link(shared, t_s.at[0], t_r.at[0], partner)
    att_all.wait_recv()
    order = peers + [t]

    def heads_of(core):
        return jnp.concatenate([att_buf[core * n_ctx + x] for x in range(n_ctx)], axis=1)

    ours, theirs = heads_of(k), heads_of(1 - k)
    for i, tt in enumerate(order):
        y_part[i] = jnp.dot(
            ours, wo_cut[slot_of(k, tt)], preferred_element_type=jnp.float32
        ) + jnp.dot(theirs, wo_sib[tt], preferred_element_type=jnp.float32)

        def chunk(x, start, size):
            at = pl.ds(pl.multiple_of(x * rows_count + start, ch), size)
            return y_part[i, at, :]

        far_a[i] = chunk(other, 0, first).astype(jnp.bfloat16)
        remote(far_a.at[i], cross_a.at[tt, u], fa_s.at[0], xa_r.at[tt], owner).start()
        near_a[i] = chunk(c, 0, first).astype(jnp.bfloat16)
        near = remote(near_a.at[i], cross_a.at[tt, u], na_s.at[0], xa_r.at[tt], beside)
        pl.when(jnp.logical_not(at_home))(near.start)

        if i < n_tp - 1:
            for x in range(n_ctx):
                zb_send[i, x] = chunk(x, first, late).astype(jnp.bfloat16)
            remote(zb_send.at[i], zb_in.at[t], zb_s.at[0], zb_r.at[0], zpeer(tt)).start()

    fin_copy.wait_recv()
    nk_ref[:, other_lanes] = fin_in[0]
    nv_ref[:, other_lanes] = fin_in[1]

    def both_sources(ref, send, recv):
        @pl.when(at_home)
        def _():
            remote(ref.at[0], ref.at[0], send, recv, partner).wait_recv()

        @pl.when(jnp.logical_not(at_home))
        def _():
            remote(ref, ref, send, recv, partner).wait_recv()

    for i, tt in enumerate(order):

        @pl.when(at_home)
        def _():
            cross_a[tt, u] = near_a[i]

        both_sources(cross_a.at[tt], fa_s.at[0], xa_r.at[tt])
        summed_a = cross_a[tt, 0].astype(jnp.float32) + cross_a[tt, 1].astype(jnp.float32)
        if i < n_tp - 1:
            za_send[i] = summed_a.astype(jnp.bfloat16)
            remote(za_send.at[i], za_in.at[t], za_s.at[0], za_r.at[0], zpeer(tt)).start()

    link(zb_send, zb_s.at[0], zb_r.at[0], partner).wait_recv()

    def gathered(x):
        at = pl.ds(pl.multiple_of(x * rows_count + first, ch), late)
        result = y_part[n_tp - 1, at, :]
        for tt in peers:
            result = result + zb_in[tt, x].astype(jnp.float32)
        return result.astype(jnp.bfloat16)

    far_b[...] = gathered(other)
    far_copy = remote(far_b, cross_b.at[u], fb_s.at[0], xb_r.at[0], owner)
    far_copy.start()
    near_b[...] = gathered(c)
    near_copy = remote(near_b, cross_b.at[u], nb_s.at[0], xb_r.at[0], beside)
    pl.when(jnp.logical_not(at_home))(near_copy.start)

    link(za_send, za_s.at[0], za_r.at[0], partner).wait_recv()
    for tt in peers:
        summed_a = summed_a + za_in[tt].astype(jnp.float32)

    @pl.when(at_home)
    def _():
        cross_b[u] = near_b[...]

    both_sources(cross_b, fb_s.at[0], xb_r.at[0])
    summed_b = cross_b[0].astype(jnp.float32) + cross_b[1].astype(jnp.float32)
    y_rows = jnp.concatenate([summed_a, summed_b], axis=0)
    ssy_buf[0] = row_squares(y_rows, lanes)
    for d in range(1, members):
        remote(
            ssy_buf.at[0], ssy_buf.at[d], ssy_s.at[0], ssy_r.at[0], member((j + d) % members)
        ).start()
    ssq_wait(lambda copy: copy.wait_send())
    slots = n_tp - 1
    for ref, send in (
        (h_buf.at[:slots, 0], b_s),
        (h_buf.at[: n_tp // n_ctx], n_s),
        (h_buf.at[:n_tp], c_s),
        (kv_send.at[0], p_s.at[1:]),
        (shared, t_s),
        (far_a, fa_s),
        (za_send, za_s),
        (zb_send, zb_s),
    ):
        link(ref, send.at[0], send.at[0], partner).wait_send()
    for copy in [a_copy, cache_copies[0], both_caches, part_copies[0], wo_copy, fin_copy, far_copy]:
        copy.wait_send()

    @pl.when(jnp.logical_not(at_home))
    def _():
        link(near_a, na_s.at[0], na_s.at[0], partner).wait_send()
        near_copy.wait_send()

    rest = ssy_buf.at[1:]
    ssy_all = remote(rest, rest, ssy_s.at[0], ssy_r.at[0], partner)
    ssy_all.wait_recv()
    total = ssy_buf[0]
    for d in range(1, members):
        total = total + ssy_buf[d]
    inverse = lax.rsqrt(jnp.transpose(jnp.broadcast_to(total, (8, lanes)))[:rows_count, 0:1] / D + epsilon)
    velocity = y_rows * inverse * og_ref[...].reshape(1, width)
    for f in range(flight):
        now = levels_ref[noise_ref[f]]
        after = levels_ref[noise_ref[f] + 1]
        out_ref[f] = state_ref[f] + (after - now) * velocity[f * ch : (f + 1) * ch]
    ssy_all.wait_send()


def y_rows_first(rows_count):
    return 3 * (rows_count // 4)


def write_out(*refs):
    sems = refs[6]
    copies = [pltpu.make_async_copy(refs[i], refs[3 + i], sems.at[i]) for i in range(3)]
    for copy in copies:
        copy.start()
    for copy in copies:
        copy.wait()


def fused(dims, *args):
    state, clean_tokens, w_query = args[0], args[1], args[2]
    w_out, cache_keys = args[5], args[6]
    n_grp, n_ctx, n_tp = dims
    per = n_grp // n_ctx
    members = n_grp * n_tp
    flight, ch, width = state.shape
    rows_count = flight * ch
    first = y_rows_first(rows_count)
    late = rows_count - first
    all_rows = rows_count + ch
    total = n_ctx * all_rows
    lanes = -(-all_rows // 128) * 128
    queries = n_ctx * rows_count
    cache_dev = cache_keys.shape[0]
    bf, fl = jnp.bfloat16, jnp.float32
    dma = pltpu.SemaphoreType.DMA
    vm = pl.BlockSpec(memory_space=pltpu.VMEM)
    hbm = pl.BlockSpec(memory_space=pltpu.HBM)

    def pair(count):
        return [dma((count,))] * 2

    scratch = [
        pltpu.VMEM(state.shape, fl),
        pltpu.VMEM(clean_tokens.shape, bf),
        pltpu.VMEM((width,), fl),
        pltpu.VMEM((width,), fl),
        pltpu.VMEM((width,), fl),
        *[pltpu.SMEM(a.shape, a.dtype) for a in args[11:]],
        pltpu.VMEM((3,) + w_query.shape, bf),
        pltpu.VMEM(w_out.shape, bf),
        pltpu.VMEM((per * n_tp, w_out.shape[0], width), bf),
        pltpu.VMEM((n_tp, w_out.shape[0], width), bf),
        pltpu.VMEM((n_ctx, 2, cache_dev, HD), bf),
        pltpu.VMEM((n_ctx, 8, cache_dev), fl),
        pltpu.VMEM((1, lanes), fl),
        pltpu.VMEM((members, 1, lanes), fl),
        pltpu.VMEM((members, 1, lanes), fl),
        pltpu.VMEM((all_rows, width), fl),
        pltpu.VMEM((all_rows, width), fl),
        pltpu.VMEM((per * n_tp, n_ctx, all_rows, width), bf),
        pltpu.VMEM((3, total, n_ctx * HD), fl),
        pltpu.VMEM((n_ctx, queries, HD), fl),
        pltpu.VMEM((queries, HD), fl),
        pltpu.VMEM((n_ctx, 2, total, HD), fl),
        pltpu.VMEM((n_ctx, 2, total, HD), bf),
        pltpu.VMEM((2, total, HD), bf),
        pltpu.VMEM((n_ctx, 2, ch, HD), bf),
        pltpu.VMEM((2, ch, HD), bf),
        pltpu.VMEM((per * n_ctx, queries, HD), bf),
        pltpu.VMEM((n_tp, queries, width), fl),
        pltpu.VMEM((n_tp, first, width), bf),
        pltpu.VMEM((n_tp, first, width), bf),
        pltpu.VMEM((n_tp, n_ctx, first, width), bf),
        pltpu.VMEM((n_tp - 1, first, width), bf),
        pltpu.VMEM((n_tp, first, width), bf),
        pltpu.VMEM((n_tp - 1, n_ctx, late, width), bf),
        pltpu.VMEM((n_tp, n_ctx, late, width), bf),
        pltpu.VMEM((late, width), bf),
        pltpu.VMEM((late, width), bf),
        pltpu.VMEM((n_ctx, late, width), bf),
        dma((12,)),
        *pair(2),
        *pair(1),
        *pair(1),
        dma((1,)),
        dma((n_tp,)),
        dma((1,)),
        dma((n_tp,)),
        dma((1,)),
        dma((n_tp,)),
        dma((2,)),
        dma((3,)),
        *pair(1),
        *pair(1),
        *pair(1),
        dma((1,)),
        dma((1,)),
        dma((n_tp,)),
        *pair(1),
        *pair(1),
        dma((1,)),
        dma((1,)),
        dma((1,)),
        *pair(1),
    ]
    results = pl.pallas_call(
        functools.partial(kernel, dims),
        out_shape=(
            pltpu.VMEM(state.shape, fl),
            pltpu.VMEM((ch, cache_keys.shape[1]), bf),
            pltpu.VMEM((ch, cache_keys.shape[1]), bf),
        ),
        in_specs=[hbm] * 15,
        out_specs=(vm, vm, vm),
        scratch_shapes=scratch,
        compiler_params=pltpu.CompilerParams(
            collective_id=0, has_side_effects=True, vmem_limit_bytes=VMEM_LIMIT
        ),
    )(*args)
    return pl.pallas_call(
        write_out,
        out_shape=tuple(jax.ShapeDtypeStruct(r.shape, r.dtype) for r in results),
        in_specs=[vm] * 3,
        out_specs=(hbm,) * 3,
        scratch_shapes=[dma((3,))],
    )(*[pltpu.with_memory_space_constraint(r, pltpu.VMEM) for r in results])


def step(dims, *args):
    n_grp, n_ctx, n_tp = dims
    heads_dev = args[6].shape[1] // HD
    if n_ctx == heads_dev == 2 and n_grp == n_tp == 4 and args[0].shape[0] == 4:
        return fused(dims, *args)
    return local(*args)


def solution(mesh):
    dims = tuple(mesh.shape[name] for name in ("grp", "ctx", "tp"))
    return jax.shard_map(
        functools.partial(step, dims),
        mesh=mesh,
        in_specs=(
            P(None, "ctx", ("grp", "tp")),
            P("ctx", ("grp", "tp")),
            P("ctx", ("grp", "tp")),
            P("ctx", ("grp", "tp")),
            P("ctx", ("grp", "tp")),
            P(("grp", "tp"), "ctx"),
            P("ctx", ("grp", "tp")),
            P("ctx", ("grp", "tp")),
            P(("grp", "tp")),
            P(("grp", "tp")),
            P(("grp", "tp")),
            P(),
            P(),
            P("ctx"),
            P(),
        ),
        out_specs=(P(None, "ctx", ("grp", "tp")), P("ctx", ("grp", "tp")), P("ctx", ("grp", "tp"))),
        check_vma=False,
    )
```

```python
import functools
import math

import jax
import jax.numpy as jnp
from jax import lax
from jax.experimental import pallas as pl
from jax.experimental.pallas import tpu as pltpu
from jax.sharding import PartitionSpec as P

D = 5120
HD = 128
SLOT = 256


epsilon = 1e-06


def level_lookup(levels, indices):
    table = jnp.arange(levels.shape[0], dtype=jnp.int32)
    picked = (indices[:, None] == table[None, :]).astype(jnp.float32)
    return jnp.sum(picked * levels[None, :], axis=1)


def normalize_rows(rows, sigma_rows, norm_gain, mod_gain):
    squares = lax.psum(jnp.sum(rows * rows, axis=1), ("grp", "tp"))
    inverse = lax.rsqrt(squares / D + epsilon)
    scaled = (
        rows
        * inverse[:, None]
        * norm_gain[None, :]
        * (1.0 + sigma_rows[:, None] * mod_gain[None, :])
    )
    return lax.all_gather(scaled.astype(jnp.bfloat16), ("grp", "tp"), axis=1, tiled=True)


def local(
    state,
    clean_tokens,
    w_query,
    w_key,
    w_value,
    w_out,
    cache_keys,
    cache_values,
    norm_gain,
    mod_gain,
    out_gain,
    levels,
    noise_index,
    placement,
    group_mask,
):
    flight, ch_dev, local_width = state.shape
    ctx_count = lax.axis_size("ctx")
    group = ch_dev * ctx_count
    cache_dev = cache_keys.shape[0]
    slots_dev = cache_dev // SLOT
    heads_dev = cache_keys.shape[1] // HD
    rows_count = flight * ch_dev
    scale = 1.0 / math.sqrt(HD)
    wk_full, wv_full, wo_full = (
        lax.all_gather(w_key, "ctx", axis=0, tiled=True),
        lax.all_gather(w_value, "ctx", axis=0, tiled=True),
        lax.all_gather(w_out, "ctx", axis=1, tiled=True),
    )
    group_table = jnp.arange(group_mask.shape[1], dtype=jnp.int32)
    slot_onehot = (placement[:, None] == group_table[None, :]).astype(jnp.int32)
    slot_seen = jnp.sum(slot_onehot[None, :, :] * group_mask[:, None, :], axis=2) > 0
    cache_seen = slot_seen[:, None, None, :, None]
    own_group = jnp.arange(flight, dtype=jnp.int32)
    flight_seen = (own_group[None, :] <= own_group[:, None])[:, None, None, :, None]
    cache_k = cache_keys.reshape(slots_dev, SLOT, heads_dev, HD)
    cache_v = cache_values.reshape(slots_dev, SLOT, heads_dev, HD)
    finished_keys = None
    finished_values = None
    current = level_lookup(levels, noise_index + 0)
    following = level_lookup(levels, noise_index + 0 + 1)
    rows = state.reshape(rows_count, local_width)
    sigma_rows = jnp.repeat(current, ch_dev)
    rows = jnp.concatenate([rows, clean_tokens.astype(jnp.float32)], axis=0)
    sigma_rows = jnp.concatenate([sigma_rows, jnp.zeros((ch_dev,), jnp.float32)])
    features = normalize_rows(rows, sigma_rows, norm_gain, mod_gain)
    keys_new = jnp.dot(features, wk_full, preferred_element_type=jnp.float32).astype(jnp.bfloat16)
    values_new = jnp.dot(features, wv_full, preferred_element_type=jnp.float32).astype(jnp.bfloat16)
    finished_keys = keys_new[rows_count:]
    finished_values = values_new[rows_count:]
    keys_new = keys_new[:rows_count]
    values_new = values_new[:rows_count]
    noisy = features[:rows_count]
    pieces = lax.all_to_all(
        noisy.reshape(flight, ch_dev, -1), "ctx", split_axis=2, concat_axis=1, tiled=True
    )
    partial_q = jnp.einsum("fqd,de->fqe", pieces, w_query, preferred_element_type=jnp.float32)
    queries = lax.psum(partial_q, "ctx").astype(jnp.bfloat16)
    query_heads = queries.reshape(flight, group, heads_dev, HD)
    finished_k = finished_keys.reshape(ch_dev, heads_dev, HD)
    finished_v = finished_values.reshape(ch_dev, heads_dev, HD)
    flight_k = keys_new.reshape(flight, ch_dev, heads_dev, HD)
    flight_v = values_new.reshape(flight, ch_dev, heads_dev, HD)
    cache_scores = (
        jnp.einsum("fqhd,sthd->fqhst", query_heads, cache_k, preferred_element_type=jnp.float32)
        * scale
    )
    finished_scores = (
        jnp.einsum("fqhd,thd->fqht", query_heads, finished_k, preferred_element_type=jnp.float32)
        * scale
    )
    flight_scores = (
        jnp.einsum("fqhd,gthd->fqhgt", query_heads, flight_k, preferred_element_type=jnp.float32)
        * scale
    )
    peak = jnp.max(finished_scores, axis=3)
    peak = jnp.maximum(peak, jnp.max(jnp.where(cache_seen, cache_scores, -jnp.inf), axis=(3, 4)))
    peak = jnp.maximum(peak, jnp.max(jnp.where(flight_seen, flight_scores, -jnp.inf), axis=(3, 4)))
    peak = lax.pmax(peak, "ctx")
    cache_p = jnp.where(cache_seen, jnp.exp(cache_scores - peak[..., None, None]), 0.0).astype(
        jnp.bfloat16
    )
    finished_p = jnp.exp(finished_scores - peak[..., None]).astype(jnp.bfloat16)
    flight_p = jnp.where(flight_seen, jnp.exp(flight_scores - peak[..., None, None]), 0.0).astype(
        jnp.bfloat16
    )
    numer = jnp.einsum("fqhst,sthd->fqhd", cache_p, cache_v, preferred_element_type=jnp.float32)
    numer = numer + jnp.einsum(
        "fqht,thd->fqhd", finished_p, finished_v, preferred_element_type=jnp.float32
    )
    numer = numer + jnp.einsum(
        "fqhgt,gthd->fqhd", flight_p, flight_v, preferred_element_type=jnp.float32
    )
    denom = jnp.sum(cache_p, axis=(3, 4), dtype=jnp.float32)
    denom = denom + jnp.sum(finished_p, axis=3, dtype=jnp.float32)
    denom = denom + jnp.sum(flight_p, axis=(3, 4), dtype=jnp.float32)
    numer, denom = (
        lax.psum_scatter(
            numer.reshape(flight, group, heads_dev * HD), "ctx", scatter_dimension=1, tiled=True
        ),
        lax.psum_scatter(denom, "ctx", scatter_dimension=1, tiled=True),
    )
    attention = numer.reshape(flight, ch_dev, heads_dev, HD) / denom[..., None]
    attention = attention.astype(jnp.bfloat16).reshape(rows_count, heads_dev * HD)
    partial_y = jnp.dot(attention, wo_full, preferred_element_type=jnp.float32)
    y_rows = lax.psum_scatter(partial_y, ("grp", "tp"), scatter_dimension=1, tiled=True)
    y_squares = lax.psum(jnp.sum(y_rows * y_rows, axis=1), ("grp", "tp"))
    velocity = y_rows * lax.rsqrt(y_squares / D + epsilon)[:, None] * out_gain[None, :]
    state = state + (following - current)[:, None, None] * velocity.reshape(
        flight, ch_dev, local_width
    )
    return (state, finished_keys, finished_values)


MESH = pl.DeviceIdType.MESH
VMEM_LIMIT = 62 * 1024 * 1024


def remote(src, dst, send, recv, device):
    return pltpu.make_async_remote_copy(
        src_ref=src,
        dst_ref=dst,
        send_sem=send,
        recv_sem=recv,
        device_id=device,
        device_id_type=MESH,
    )


def row_squares(rows, lanes):
    squares = rows * rows
    count = squares.shape[0]
    if count < lanes:
        squares = jnp.concatenate(
            [squares, jnp.zeros((lanes - count, squares.shape[1]), jnp.float32)], axis=0
        )
    pad = -squares.shape[1] % 128
    if pad:
        squares = jnp.concatenate(
            [squares, jnp.zeros((squares.shape[0], pad), jnp.float32)], axis=1
        )
    folded = squares[:, :128]
    for start in range(128, squares.shape[1], 128):
        folded = folded + squares[:, start : start + 128]
    return jnp.sum(jnp.transpose(folded), axis=0, keepdims=True)


def kernel(
    dims,
    state_hbm,
    clean_hbm,
    wq_hbm,
    wk_hbm,
    wv_hbm,
    wo_hbm,
    ck_hbm,
    cv_hbm,
    ng_hbm,
    mg_hbm,
    og_hbm,
    levels_hbm,
    noise_hbm,
    place_hbm,
    mask_hbm,
    out_ref,
    nk_ref,
    nv_ref,
    state_ref,
    clean_ref,
    ng_ref,
    mg_ref,
    og_ref,
    levels_ref,
    noise_ref,
    place_ref,
    mask_ref,
    w_buf,
    wo_buf,
    wo_cut,
    wo_sib,
    cache_buf,
    seen_buf,
    ssq_own,
    ssq_buf,
    ssy_buf,
    raw,
    raw_in,
    h_buf,
    acc,
    q_part,
    q_in,
    kv_part,
    kv_send,
    kv_in,
    kv_buf,
    fin_in,
    att_buf,
    y_part,
    near_a,
    far_a,
    cross_a,
    za_send,
    za_in,
    zb_send,
    zb_in,
    near_b,
    far_b,
    cross_b,
    local_sem,
    send,
    cache_r,
    ssq_r,
    a_r,
    b_r,
    n_r,
    c_r,
    p_r,
    f_r,
    t_r,
    wo_r,
    xa_r,
    za_r,
    zb_r,
    xb_r,
    ssy_r,
):
    n_grp, n_ctx, n_tp = dims
    per = n_grp // n_ctx
    members = n_grp * n_tp
    flight, ch, width = state_hbm.shape
    rows_count = flight * ch
    first = y_rows_first(rows_count)
    late = rows_count - first
    all_rows = rows_count + ch
    cache_dev = ck_hbm.shape[0]
    lanes = ssq_buf.shape[2]
    total_rows = n_ctx * all_rows
    queries = n_ctx * rows_count
    g, c, t = lax.axis_index("grp"), lax.axis_index("ctx"), lax.axis_index("tp")
    u, k = g // per, g % per
    j = g * n_tp + t
    other = 1 - c
    partner = (g, other, t)
    sibling = (u * per + (1 - k), c, t)
    beside = ((1 - u) * per + k, c, t)
    held = 1 - u
    at_home = u == c
    owner = (c * per + k, other, t)

    def member(index):
        return (index // n_tp, c, index % n_tp)

    side = t // (n_tp // 2)
    inner = t + side * (n_tp - 1 - 2 * t)
    peers = []
    for i in range(n_tp - 1):
        v = n_tp - 1 - i
        p = v - (inner - v + n_tp) // n_tp
        peers.append(p + side * (n_tp - 1 - 2 * p))
    pair = t + 1 - 2 * (t % 2)
    span = n_tp // 2
    across = (t + span) % n_tp
    diagonal = (pair + span) % n_tp
    places = [t, pair, across, diagonal]

    def zpeer(tt):
        return (g, c, tt)

    own_pair, far_pair = u * per, (1 - u) * per
    barrier = pltpu.get_barrier_semaphore()
    for tt in peers + [t]:
        for dc in reversed(range(n_ctx)):
            for core in (far_pair, own_pair):
                for dk in reversed(range(per)):
                    if tt is t and dc + dk == 0 and core is own_pair:
                        continue
                    pl.semaphore_signal(
                        barrier,
                        inc=1,
                        device_id=(core + (k + dk) % per, (c + dc) % n_ctx, tt),
                        device_id_type=MESH,
                    )

    loads = [
        pltpu.make_async_copy(src, w_buf.at[i], local_sem.at[0])
        for i, src in enumerate((wq_hbm, wk_hbm, wv_hbm))
    ]
    wo_load = pltpu.make_async_copy(wo_hbm, wo_buf, local_sem.at[1])
    own_lanes = pl.ds(pl.multiple_of(c * HD, HD), HD)
    other_lanes = pl.ds(pl.multiple_of(other * HD, HD), HD)
    cache_loads = [
        pltpu.make_async_copy(src.at[:, own_lanes], cache_buf.at[c, i], local_sem.at[2])
        for i, src in enumerate((ck_hbm, cv_hbm))
    ]
    small = [
        pltpu.make_async_copy(src, dst, local_sem.at[3])
        for i, (src, dst) in enumerate(
            [
                (state_hbm, state_ref),
                (clean_hbm, clean_ref),
                (ng_hbm, ng_ref),
                (mg_hbm, mg_ref),
                (og_hbm, og_ref),
                (levels_hbm, levels_ref),
                (noise_hbm, noise_ref),
                (place_hbm, place_ref),
                (mask_hbm, mask_ref),
            ]
        )
    ]
    for copy in small + [wo_load] + loads + cache_loads:
        copy.start()
    for copy in small:
        copy.wait()

    rows = jnp.concatenate(
        [state_ref[...].reshape(rows_count, width), clean_ref[...].astype(jnp.float32)], axis=0
    )
    ssq_own[...] = row_squares(rows, lanes)

    @pl.when(c == held)
    def _():
        ssq_buf[j] = ssq_own[...]

    modulation = mg_ref[...].reshape(1, width)
    gained = rows * ng_ref[...].reshape(1, width)
    for f in range(flight):
        sigma = levels_ref[noise_ref[f]]
        raw[f * ch : (f + 1) * ch] = gained[f * ch : (f + 1) * ch] * (1.0 + sigma * modulation)
    raw[rows_count:] = gained[rows_count:]
    line = lax.broadcasted_iota(jnp.int32, (8, SLOT), 0)
    for s in range(cache_dev // SLOT):
        block = jnp.zeros((8, SLOT), jnp.float32)
        for f in range(flight):
            hidden = jnp.where(mask_ref[f, place_ref[s]] != 0, 0.0, -jnp.inf)
            block = jnp.where(line == f, hidden, block)
        seen_buf[c, :, s * SLOT : (s + 1) * SLOT] = block
    pl.semaphore_wait(barrier, n_grp * n_ctx * n_tp - 1)

    def ssq_copy(target):
        return remote(ssq_own, ssq_buf.at[j], send.at[0], ssq_r.at[0], target)

    for dk in range(per):
        for dc in range(n_ctx):
            for dt in range(n_tp):
                copy = ssq_copy(
                    ((1 - c) * per + (k + dk) % per, (c + dc) % n_ctx, (t + dt) % n_tp)
                )
                if dk + dc + dt > 0:
                    copy.start()
                else:
                    pl.when(c != held)(copy.start)
    a_copy = remote(raw, raw_in, send.at[0], a_r.at[0], ((1 - c) * per + k, u, t))
    a_copy.start()
    wo_load.wait()
    for block in range(per * n_tp):
        wo_cut[block] = wo_buf[:, block * width : (block + 1) * width]
    wo_copy = remote(
        wo_cut.at[pl.ds((1 - k) * n_tp, n_tp)], wo_sib, send.at[0], wo_r.at[0], sibling
    )
    wo_copy.start()

    def ssq_wait(finish):
        @pl.when(c == held)
        def _():
            most = ssq_buf.at[: members - 1]
            finish(remote(most, most, send.at[0], ssq_r.at[0], partner))

        @pl.when(c != held)
        def _():
            finish(remote(ssq_buf, ssq_buf, send.at[0], ssq_r.at[0], partner))

    ssq_wait(lambda copy: copy.wait_recv())
    total = ssq_buf[0]
    for d in range(1, members):
        total = total + ssq_buf[d]
    inverse = lax.rsqrt(jnp.transpose(jnp.broadcast_to(total, (8, lanes)))[:all_rows, 0:1] / D + epsilon)
    a_copy.wait_recv()
    mine = k * n_tp + t
    h_buf[mine, held] = (raw_in[...] * inverse).astype(jnp.bfloat16)

    def slot_of(core, tt):
        return core * n_tp + tt

    def link(ref, send, recv, device):
        return remote(ref, ref, send, recv, device)

    def to_beside(x, tt):
        link(h_buf.at[slot_of(k, tt), x], send.at[0], n_r.at[tt], beside).start()

    def to_sibling(x, tt):
        link(h_buf.at[slot_of(k, tt), x], send.at[0], c_r.at[tt], sibling).start()

    def to_line(tt, device):
        link(h_buf.at[slot_of(k, tt), held], send.at[0], b_r.at[tt], device).start()

    for tt in (across, pair):
        to_line(t, zpeer(tt))
    to_beside(held, t)
    to_sibling(held, t)

    cache_copies = [
        remote(seen_buf.at[c], seen_buf.at[c], send.at[0], cache_r.at[0], partner)
    ] + [
        remote(
            src.at[:, other_lanes], cache_buf.at[c, i], send.at[0], cache_r.at[1], partner
        )
        for i, src in enumerate((ck_hbm, cv_hbm))
    ]
    for copy in cache_copies:
        copy.start()

    pltpu.make_async_copy(w_buf, w_buf, local_sem.at[0]).wait()

    def project(slots, w):
        total = None
        for slot in slots:
            lhs = h_buf[slot].reshape(total_rows, width)
            depth = pl.ds(pl.multiple_of(slot * width, 64), width)
            product = jnp.dot(lhs, w_buf[w, depth, :], preferred_element_type=jnp.float32)
            total = product if total is None else total + product
        return total

    def from_line(i):
        tt = places[i]
        link(h_buf.at[slot_of(k, tt), held], send.at[0], b_r.at[tt], partner).wait_recv()
        if i == 1:
            to_beside(held, tt)
        if i == 2:
            to_line(tt, zpeer(pair))
        to_sibling(held, tt)

    def from_beside(i):
        tt = places[i]
        link(h_buf.at[slot_of(k, tt), u], send.at[0], n_r.at[tt], beside).wait_recv()
        if i in (0, 2):
            place = across if i == 0 else pair
            link(h_buf.at[slot_of(k, tt), u], send.at[0], n_r.at[tt], zpeer(place)).start()
        to_sibling(u, tt)

    def from_sibling(i):
        tt = places[i]
        link(h_buf.at[slot_of(1 - k, tt)], send.at[0], c_r.at[tt], sibling).wait_recv()

    def add(slots, fresh=False):
        for w in range(3):
            acc[w] = project(slots, w) if fresh else acc[w] + project(slots, w)

    from_beside(0)
    from_line(1)
    from_line(2)
    from_sibling(0)
    add([slot_of(k, places[0]), slot_of(1 - k, places[0])], True)
    from_beside(2)
    from_beside(1)
    from_line(3)
    from_beside(3)
    from_sibling(1)
    from_sibling(2)
    add([slot_of(k, places[1]), slot_of(1 - k, places[1]), slot_of(k, places[2]), slot_of(1 - k, places[2]), slot_of(k, places[3])])
    from_sibling(3)
    part_copies = []
    for w in range(3):
        whole = acc[w] + project([slot_of(1 - k, places[3])], w)
        for head in range(n_ctx):
            piece = whole[:, head * HD : (head + 1) * HD]
            if w == 0:
                for x in range(n_ctx):
                    q_part[head, x * rows_count : (x + 1) * rows_count] = piece[
                        x * all_rows : x * all_rows + rows_count
                    ]
            else:
                kv_part[head, w - 1] = piece
                kv_send[head, w - 1] = piece.astype(jnp.bfloat16)
        if w == 0:
            copy = remote(q_part.at[other], q_in, send.at[0], p_r.at[0], partner)
        else:
            copy = remote(
                kv_send.at[other, w - 1], kv_in.at[w - 1], send.at[0], p_r.at[w], partner
            )
        copy.start()
        part_copies.append(copy)
    pltpu.make_async_copy(cache_buf.at[0], cache_buf.at[0], local_sem.at[2]).wait()
    cache_copies[0].wait_recv()
    both_caches = remote(
        cache_buf.at[0], cache_buf.at[0], send.at[0], cache_r.at[1], partner
    )
    both_caches.wait_recv()
    query_group = (lax.broadcasted_iota(jnp.int32, (queries, total_rows), 0) % rows_count) // ch
    key_group = (lax.broadcasted_iota(jnp.int32, (queries, total_rows), 1) % all_rows) // ch
    flight_seen = jnp.logical_or(key_group == flight, key_group <= query_group)

    part_copies[0].wait_recv()
    q = (q_part[c] + q_in[...]).astype(jnp.bfloat16)
    scale = 1.0 / math.sqrt(HD)

    def score(keys):
        return (
            lax.dot_general(q, keys, (((1,), (1,)), ((), ())), preferred_element_type=jnp.float32)
            * scale
        )

    scores = []
    for x in range(n_ctx):
        plain = score(cache_buf[x, 0])
        scores.append(
            jnp.concatenate(
                [
                    plain[b * ch : (b + 1) * ch] + seen_buf[x, b % flight : b % flight + 1]
                    for b in range(n_ctx * flight)
                ],
                axis=0,
            )
        )
    peak = jnp.max(jnp.maximum(scores[0], scores[1]), axis=1, keepdims=True)
    part_copies[1].wait_recv()
    key = (kv_part[c, 0] + kv_in[0].astype(jnp.float32)).astype(jnp.bfloat16)
    scores.append(jnp.where(flight_seen, score(key), -jnp.inf))
    peak = jnp.maximum(peak, jnp.max(scores[-1], axis=1, keepdims=True))
    weights = [jnp.exp(v - peak).astype(jnp.bfloat16) for v in scores]
    denom = sum(jnp.sum(w.astype(jnp.float32), axis=1, keepdims=True) for w in weights)
    numer = sum(
        jnp.dot(weights[x], cache_buf[x, 1], preferred_element_type=jnp.float32)
        for x in range(n_ctx)
    )
    part_copies[2].wait_recv()
    value = (kv_part[c, 1] + kv_in[1].astype(jnp.float32)).astype(jnp.bfloat16)
    numer = numer + jnp.dot(weights[-1], value, preferred_element_type=jnp.float32)
    attention = (numer / denom).astype(jnp.bfloat16)
    att_buf[k * n_ctx + c] = attention
    for device in (partner, (u * per + (1 - k), other, t), sibling):
        link(att_buf.at[k * n_ctx + c], send.at[0], t_r.at[0], device).start()

    for x in range(n_ctx):
        last = slice(x * all_rows + rows_count, (x + 1) * all_rows)
        kv_buf[x, 0] = key[last]
        kv_buf[x, 1] = value[last]
    fin_copy = remote(kv_buf.at[other], fin_in, send.at[0], f_r.at[0], partner)
    fin_copy.start()
    nk_ref[:, own_lanes] = kv_buf[c, 0]
    nv_ref[:, own_lanes] = kv_buf[c, 1]

    wo_copy.wait_recv()
    shared = att_buf.at[: per * n_ctx - 1]
    att_all = link(shared, send.at[0], t_r.at[0], partner)
    att_all.wait_recv()
    order = peers + [t]

    def heads_of(core):
        return jnp.concatenate([att_buf[core * n_ctx + x] for x in range(n_ctx)], axis=1)

    ours, theirs = heads_of(k), heads_of(1 - k)
    for i, tt in enumerate(order):
        y_part[i] = jnp.dot(
            ours, wo_cut[slot_of(k, tt)], preferred_element_type=jnp.float32
        ) + jnp.dot(theirs, wo_sib[tt], preferred_element_type=jnp.float32)

        def chunk(x, start, size):
            at = pl.ds(pl.multiple_of(x * rows_count + start, ch), size)
            return y_part[i, at, :]

        far_a[i] = chunk(other, 0, first).astype(jnp.bfloat16)
        remote(far_a.at[i], cross_a.at[tt, u], send.at[0], xa_r.at[tt], owner).start()
        near_a[i] = chunk(c, 0, first).astype(jnp.bfloat16)
        near = remote(near_a.at[i], cross_a.at[tt, u], send.at[0], xa_r.at[tt], beside)
        pl.when(jnp.logical_not(at_home))(near.start)

        if i < n_tp - 1:
            for x in range(n_ctx):
                zb_send[i, x] = chunk(x, first, late).astype(jnp.bfloat16)
            remote(zb_send.at[i], zb_in.at[t], send.at[0], zb_r.at[0], zpeer(tt)).start()

    fin_copy.wait_recv()
    nk_ref[:, other_lanes] = fin_in[0]
    nv_ref[:, other_lanes] = fin_in[1]

    def both_sources(ref, send, recv):
        @pl.when(at_home)
        def _():
            remote(ref.at[0], ref.at[0], send, recv, partner).wait_recv()

        @pl.when(jnp.logical_not(at_home))
        def _():
            remote(ref, ref, send, recv, partner).wait_recv()

    def from_across(i):
        tt = order[i]

        @pl.when(at_home)
        def _():
            cross_a[tt, u] = near_a[i]

        both_sources(cross_a.at[tt], send.at[0], xa_r.at[tt])
        return cross_a[tt, 0].astype(jnp.float32) + cross_a[tt, 1].astype(jnp.float32)

    for i in range(n_tp - 1):
        za_send[i] = from_across(i).astype(jnp.bfloat16)
        remote(za_send.at[i], za_in.at[t], send.at[0], za_r.at[0], zpeer(order[i])).start()

    link(zb_send, send.at[0], zb_r.at[0], partner).wait_recv()

    def gathered(x):
        at = pl.ds(pl.multiple_of(x * rows_count + first, ch), late)
        result = y_part[n_tp - 1, at, :]
        for tt in peers:
            result = result + zb_in[tt, x].astype(jnp.float32)
        return result.astype(jnp.bfloat16)

    far_b[...] = gathered(other)
    far_copy = remote(far_b, cross_b.at[u], send.at[0], xb_r.at[0], owner)
    far_copy.start()
    near_b[...] = gathered(c)
    near_copy = remote(near_b, cross_b.at[u], send.at[0], xb_r.at[0], beside)
    pl.when(jnp.logical_not(at_home))(near_copy.start)

    summed_a = from_across(n_tp - 1)
    link(za_send, send.at[0], za_r.at[0], partner).wait_recv()
    for tt in peers:
        summed_a = summed_a + za_in[tt].astype(jnp.float32)

    @pl.when(at_home)
    def _():
        cross_b[u] = near_b[...]

    both_sources(cross_b, send.at[0], xb_r.at[0])
    summed_b = cross_b[0].astype(jnp.float32) + cross_b[1].astype(jnp.float32)
    y_rows = jnp.concatenate([summed_a, summed_b], axis=0)
    ssy_buf[0] = row_squares(y_rows, lanes)
    for d in range(1, members):
        remote(
            ssy_buf.at[0], ssy_buf.at[d], send.at[0], ssy_r.at[0], member((j + d) % members)
        ).start()
    ssq_wait(lambda copy: copy.wait_send())
    slots = n_tp - 1
    for ref in (
        h_buf.at[:slots, 0],
        h_buf.at[: n_tp // n_ctx],
        h_buf.at[:n_tp],
        kv_send.at[0],
        shared,
        far_a,
        za_send,
        zb_send,
    ):
        link(ref, send.at[0], send.at[0], partner).wait_send()
    for copy in [a_copy, cache_copies[0], both_caches, part_copies[0], wo_copy, fin_copy, far_copy]:
        copy.wait_send()

    @pl.when(jnp.logical_not(at_home))
    def _():
        link(near_a, send.at[0], send.at[0], partner).wait_send()
        near_copy.wait_send()

    rest = ssy_buf.at[1:]
    ssy_all = remote(rest, rest, send.at[0], ssy_r.at[0], partner)
    ssy_all.wait_recv()
    total = ssy_buf[0]
    for d in range(1, members):
        total = total + ssy_buf[d]
    inverse = lax.rsqrt(jnp.transpose(jnp.broadcast_to(total, (8, lanes)))[:rows_count, 0:1] / D + epsilon)
    velocity = y_rows * inverse * og_ref[...].reshape(1, width)
    for f in range(flight):
        now = levels_ref[noise_ref[f]]
        after = levels_ref[noise_ref[f] + 1]
        out_ref[f] = state_ref[f] + (after - now) * velocity[f * ch : (f + 1) * ch]
    ssy_all.wait_send()


def y_rows_first(rows_count):
    return 3 * (rows_count // 4)


def write_out(*refs):
    sems = refs[6]
    copies = [pltpu.make_async_copy(refs[i], refs[3 + i], sems.at[i]) for i in range(3)]
    for copy in copies:
        copy.start()
    for copy in copies:
        copy.wait()


def fused(dims, *args):
    state, clean_tokens, w_query = args[0], args[1], args[2]
    w_out, cache_keys = args[5], args[6]
    n_grp, n_ctx, n_tp = dims
    per = n_grp // n_ctx
    members = n_grp * n_tp
    flight, ch, width = state.shape
    rows_count = flight * ch
    first = y_rows_first(rows_count)
    late = rows_count - first
    all_rows = rows_count + ch
    total = n_ctx * all_rows
    lanes = -(-all_rows // 128) * 128
    queries = n_ctx * rows_count
    cache_dev = cache_keys.shape[0]
    bf, fl = jnp.bfloat16, jnp.float32
    dma = pltpu.SemaphoreType.DMA
    vm = pl.BlockSpec(memory_space=pltpu.VMEM)
    hbm = pl.BlockSpec(memory_space=pltpu.HBM)

    scratch = [
        pltpu.VMEM(state.shape, fl),
        pltpu.VMEM(clean_tokens.shape, bf),
        pltpu.VMEM((width,), fl),
        pltpu.VMEM((width,), fl),
        pltpu.VMEM((width,), fl),
        *[pltpu.SMEM(a.shape, a.dtype) for a in args[11:]],
        pltpu.VMEM((3,) + w_query.shape, bf),
        pltpu.VMEM(w_out.shape, bf),
        pltpu.VMEM((per * n_tp, w_out.shape[0], width), bf),
        pltpu.VMEM((n_tp, w_out.shape[0], width), bf),
        pltpu.VMEM((n_ctx, 2, cache_dev, HD), bf),
        pltpu.VMEM((n_ctx, 8, cache_dev), fl),
        pltpu.VMEM((1, lanes), fl),
        pltpu.VMEM((members, 1, lanes), fl),
        pltpu.VMEM((members, 1, lanes), fl),
        pltpu.VMEM((all_rows, width), fl),
        pltpu.VMEM((all_rows, width), fl),
        pltpu.VMEM((per * n_tp, n_ctx, all_rows, width), bf),
        pltpu.VMEM((3, total, n_ctx * HD), fl),
        pltpu.VMEM((n_ctx, queries, HD), fl),
        pltpu.VMEM((queries, HD), fl),
        pltpu.VMEM((n_ctx, 2, total, HD), fl),
        pltpu.VMEM((n_ctx, 2, total, HD), bf),
        pltpu.VMEM((2, total, HD), bf),
        pltpu.VMEM((n_ctx, 2, ch, HD), bf),
        pltpu.VMEM((2, ch, HD), bf),
        pltpu.VMEM((per * n_ctx, queries, HD), bf),
        pltpu.VMEM((n_tp, queries, width), fl),
        pltpu.VMEM((n_tp, first, width), bf),
        pltpu.VMEM((n_tp, first, width), bf),
        pltpu.VMEM((n_tp, n_ctx, first, width), bf),
        pltpu.VMEM((n_tp - 1, first, width), bf),
        pltpu.VMEM((n_tp, first, width), bf),
        pltpu.VMEM((n_tp - 1, n_ctx, late, width), bf),
        pltpu.VMEM((n_tp, n_ctx, late, width), bf),
        pltpu.VMEM((late, width), bf),
        pltpu.VMEM((late, width), bf),
        pltpu.VMEM((n_ctx, late, width), bf),
        dma((4,)),
        dma((1,)),
        dma((2,)),
        dma((1,)),
        dma((1,)),
        dma((n_tp,)),
        dma((n_tp,)),
        dma((n_tp,)),
        dma((3,)),
        dma((1,)),
        dma((1,)),
        dma((1,)),
        dma((n_tp,)),
        dma((1,)),
        dma((1,)),
        dma((1,)),
        dma((1,)),
    ]
    results = pl.pallas_call(
        functools.partial(kernel, dims),
        out_shape=(
            pltpu.VMEM(state.shape, fl),
            pltpu.VMEM((ch, cache_keys.shape[1]), bf),
            pltpu.VMEM((ch, cache_keys.shape[1]), bf),
        ),
        in_specs=[hbm] * 15,
        out_specs=(vm, vm, vm),
        scratch_shapes=scratch,
        compiler_params=pltpu.CompilerParams(
            collective_id=0, has_side_effects=True, vmem_limit_bytes=VMEM_LIMIT
        ),
    )(*args)
    return pl.pallas_call(
        write_out,
        out_shape=tuple(jax.ShapeDtypeStruct(r.shape, r.dtype) for r in results),
        in_specs=[vm] * 3,
        out_specs=(hbm,) * 3,
        scratch_shapes=[dma((3,))],
    )(*[pltpu.with_memory_space_constraint(r, pltpu.VMEM) for r in results])


def step(dims, *args):
    n_grp, n_ctx, n_tp = dims
    heads_dev = args[6].shape[1] // HD
    if n_ctx == heads_dev == 2 and n_grp == n_tp == 4 and args[0].shape[0] == 4:
        return fused(dims, *args)
    return local(*args)


def solution(mesh):
    dims = tuple(mesh.shape[name] for name in ("grp", "ctx", "tp"))
    return jax.shard_map(
        functools.partial(step, dims),
        mesh=mesh,
        in_specs=(
            P(None, "ctx", ("grp", "tp")),
            P("ctx", ("grp", "tp")),
            P("ctx", ("grp", "tp")),
            P("ctx", ("grp", "tp")),
            P("ctx", ("grp", "tp")),
            P(("grp", "tp"), "ctx"),
            P("ctx", ("grp", "tp")),
            P("ctx", ("grp", "tp")),
            P(("grp", "tp")),
            P(("grp", "tp")),
            P(("grp", "tp")),
            P(),
            P(),
            P("ctx"),
            P(),
        ),
        out_specs=(P(None, "ctx", ("grp", "tp")), P("ctx", ("grp", "tp")), P("ctx", ("grp", "tp"))),
        check_vma=False,
    )
```

```python
import functools
import math

import jax
import jax.numpy as jnp
from jax import lax
from jax.experimental import pallas as pl
from jax.experimental.pallas import tpu as pltpu
from jax.sharding import PartitionSpec as P

D = 5120
HD = 128
SLOT = 256


epsilon = 1e-06


def level_lookup(levels, indices):
    table = jnp.arange(levels.shape[0], dtype=jnp.int32)
    picked = (indices[:, None] == table[None, :]).astype(jnp.float32)
    return jnp.sum(picked * levels[None, :], axis=1)


def normalize_rows(rows, sigma_rows, norm_gain, mod_gain):
    squares = lax.psum(jnp.sum(rows * rows, axis=1), ("grp", "tp"))
    inverse = lax.rsqrt(squares / D + epsilon)
    scaled = (
        rows
        * inverse[:, None]
        * norm_gain[None, :]
        * (1.0 + sigma_rows[:, None] * mod_gain[None, :])
    )
    return lax.all_gather(scaled.astype(jnp.bfloat16), ("grp", "tp"), axis=1, tiled=True)


def local(
    state,
    clean_tokens,
    w_query,
    w_key,
    w_value,
    w_out,
    cache_keys,
    cache_values,
    norm_gain,
    mod_gain,
    out_gain,
    levels,
    noise_index,
    placement,
    group_mask,
):
    flight, ch_dev, local_width = state.shape
    ctx_count = lax.axis_size("ctx")
    group = ch_dev * ctx_count
    cache_dev = cache_keys.shape[0]
    slots_dev = cache_dev // SLOT
    heads_dev = cache_keys.shape[1] // HD
    rows_count = flight * ch_dev
    scale = 1.0 / math.sqrt(HD)
    wk_full, wv_full, wo_full = (
        lax.all_gather(w_key, "ctx", axis=0, tiled=True),
        lax.all_gather(w_value, "ctx", axis=0, tiled=True),
        lax.all_gather(w_out, "ctx", axis=1, tiled=True),
    )
    group_table = jnp.arange(group_mask.shape[1], dtype=jnp.int32)
    slot_onehot = (placement[:, None] == group_table[None, :]).astype(jnp.int32)
    slot_seen = jnp.sum(slot_onehot[None, :, :] * group_mask[:, None, :], axis=2) > 0
    cache_seen = slot_seen[:, None, None, :, None]
    own_group = jnp.arange(flight, dtype=jnp.int32)
    flight_seen = (own_group[None, :] <= own_group[:, None])[:, None, None, :, None]
    cache_k = cache_keys.reshape(slots_dev, SLOT, heads_dev, HD)
    cache_v = cache_values.reshape(slots_dev, SLOT, heads_dev, HD)
    finished_keys = None
    finished_values = None
    current = level_lookup(levels, noise_index + 0)
    following = level_lookup(levels, noise_index + 0 + 1)
    rows = state.reshape(rows_count, local_width)
    sigma_rows = jnp.repeat(current, ch_dev)
    rows = jnp.concatenate([rows, clean_tokens.astype(jnp.float32)], axis=0)
    sigma_rows = jnp.concatenate([sigma_rows, jnp.zeros((ch_dev,), jnp.float32)])
    features = normalize_rows(rows, sigma_rows, norm_gain, mod_gain)
    keys_new = jnp.dot(features, wk_full, preferred_element_type=jnp.float32).astype(jnp.bfloat16)
    values_new = jnp.dot(features, wv_full, preferred_element_type=jnp.float32).astype(jnp.bfloat16)
    finished_keys = keys_new[rows_count:]
    finished_values = values_new[rows_count:]
    keys_new = keys_new[:rows_count]
    values_new = values_new[:rows_count]
    noisy = features[:rows_count]
    pieces = lax.all_to_all(
        noisy.reshape(flight, ch_dev, -1), "ctx", split_axis=2, concat_axis=1, tiled=True
    )
    partial_q = jnp.einsum("fqd,de->fqe", pieces, w_query, preferred_element_type=jnp.float32)
    queries = lax.psum(partial_q, "ctx").astype(jnp.bfloat16)
    query_heads = queries.reshape(flight, group, heads_dev, HD)
    finished_k = finished_keys.reshape(ch_dev, heads_dev, HD)
    finished_v = finished_values.reshape(ch_dev, heads_dev, HD)
    flight_k = keys_new.reshape(flight, ch_dev, heads_dev, HD)
    flight_v = values_new.reshape(flight, ch_dev, heads_dev, HD)
    cache_scores = (
        jnp.einsum("fqhd,sthd->fqhst", query_heads, cache_k, preferred_element_type=jnp.float32)
        * scale
    )
    finished_scores = (
        jnp.einsum("fqhd,thd->fqht", query_heads, finished_k, preferred_element_type=jnp.float32)
        * scale
    )
    flight_scores = (
        jnp.einsum("fqhd,gthd->fqhgt", query_heads, flight_k, preferred_element_type=jnp.float32)
        * scale
    )
    peak = jnp.max(finished_scores, axis=3)
    peak = jnp.maximum(peak, jnp.max(jnp.where(cache_seen, cache_scores, -jnp.inf), axis=(3, 4)))
    peak = jnp.maximum(peak, jnp.max(jnp.where(flight_seen, flight_scores, -jnp.inf), axis=(3, 4)))
    peak = lax.pmax(peak, "ctx")
    cache_p = jnp.where(cache_seen, jnp.exp(cache_scores - peak[..., None, None]), 0.0).astype(
        jnp.bfloat16
    )
    finished_p = jnp.exp(finished_scores - peak[..., None]).astype(jnp.bfloat16)
    flight_p = jnp.where(flight_seen, jnp.exp(flight_scores - peak[..., None, None]), 0.0).astype(
        jnp.bfloat16
    )
    numer = jnp.einsum("fqhst,sthd->fqhd", cache_p, cache_v, preferred_element_type=jnp.float32)
    numer = numer + jnp.einsum(
        "fqht,thd->fqhd", finished_p, finished_v, preferred_element_type=jnp.float32
    )
    numer = numer + jnp.einsum(
        "fqhgt,gthd->fqhd", flight_p, flight_v, preferred_element_type=jnp.float32
    )
    denom = jnp.sum(cache_p, axis=(3, 4), dtype=jnp.float32)
    denom = denom + jnp.sum(finished_p, axis=3, dtype=jnp.float32)
    denom = denom + jnp.sum(flight_p, axis=(3, 4), dtype=jnp.float32)
    numer, denom = (
        lax.psum_scatter(
            numer.reshape(flight, group, heads_dev * HD), "ctx", scatter_dimension=1, tiled=True
        ),
        lax.psum_scatter(denom, "ctx", scatter_dimension=1, tiled=True),
    )
    attention = numer.reshape(flight, ch_dev, heads_dev, HD) / denom[..., None]
    attention = attention.astype(jnp.bfloat16).reshape(rows_count, heads_dev * HD)
    partial_y = jnp.dot(attention, wo_full, preferred_element_type=jnp.float32)
    y_rows = lax.psum_scatter(partial_y, ("grp", "tp"), scatter_dimension=1, tiled=True)
    y_squares = lax.psum(jnp.sum(y_rows * y_rows, axis=1), ("grp", "tp"))
    velocity = y_rows * lax.rsqrt(y_squares / D + epsilon)[:, None] * out_gain[None, :]
    state = state + (following - current)[:, None, None] * velocity.reshape(
        flight, ch_dev, local_width
    )
    return (state, finished_keys, finished_values)


MESH = pl.DeviceIdType.MESH
VMEM_LIMIT = 62 * 1024 * 1024


def remote(src, dst, send, recv, device):
    return pltpu.make_async_remote_copy(
        src_ref=src,
        dst_ref=dst,
        send_sem=send,
        recv_sem=recv,
        device_id=device,
        device_id_type=MESH,
    )


def row_squares(rows, lanes):
    squares = rows * rows
    count = squares.shape[0]
    if count < lanes:
        squares = jnp.concatenate(
            [squares, jnp.zeros((lanes - count, squares.shape[1]), jnp.float32)], axis=0
        )
    pad = -squares.shape[1] % 128
    if pad:
        squares = jnp.concatenate(
            [squares, jnp.zeros((squares.shape[0], pad), jnp.float32)], axis=1
        )
    folded = squares[:, :128]
    for start in range(128, squares.shape[1], 128):
        folded = folded + squares[:, start : start + 128]
    return jnp.sum(jnp.transpose(folded), axis=0, keepdims=True)


def kernel(
    dims,
    state_hbm,
    clean_hbm,
    wq_hbm,
    wk_hbm,
    wv_hbm,
    wo_hbm,
    ck_hbm,
    cv_hbm,
    ng_hbm,
    mg_hbm,
    og_hbm,
    levels_hbm,
    noise_hbm,
    place_hbm,
    mask_hbm,
    out_ref,
    nk_ref,
    nv_ref,
    state_ref,
    clean_ref,
    ng_ref,
    mg_ref,
    og_ref,
    levels_ref,
    noise_ref,
    place_ref,
    mask_ref,
    w_buf,
    wo_buf,
    wo_cut,
    wo_sib,
    cache_buf,
    seen_buf,
    ssq_own,
    ssq_buf,
    ssy_buf,
    raw,
    raw_in,
    h_buf,
    acc,
    q_part,
    q_in,
    kv_part,
    kv_send,
    kv_in,
    kv_buf,
    fin_in,
    att_buf,
    y_part,
    near_a,
    far_a,
    cross_a,
    za_send,
    za_in,
    zb_send,
    zb_in,
    near_b,
    far_b,
    cross_b,
    local_sem,
    send,
    cache_r,
    ssq_r,
    a_r,
    b_r,
    n_r,
    c_r,
    p_r,
    f_r,
    t_r,
    wo_r,
    xa_r,
    za_r,
    zb_r,
    xb_r,
    ssy_r,
):
    n_grp, n_ctx, n_tp = dims
    per = n_grp // n_ctx
    members = n_grp * n_tp
    flight, ch, width = state_hbm.shape
    rows_count = flight * ch
    first = y_rows_first(rows_count)
    late = rows_count - first
    all_rows = rows_count + ch
    cache_dev = ck_hbm.shape[0]
    lanes = ssq_buf.shape[2]
    total_rows = n_ctx * all_rows
    queries = n_ctx * rows_count
    g, c, t = lax.axis_index("grp"), lax.axis_index("ctx"), lax.axis_index("tp")
    u, k = g // per, g % per
    j = g * n_tp + t
    other = 1 - c
    partner = (g, other, t)
    sibling = (u * per + (1 - k), c, t)
    beside = ((1 - u) * per + k, c, t)
    held = 1 - u
    at_home = u == c
    owner = (c * per + k, other, t)

    def member(index):
        return (index // n_tp, c, index % n_tp)

    side = t // (n_tp // 2)
    inner = t + side * (n_tp - 1 - 2 * t)
    peers = []
    for i in range(n_tp - 1):
        v = n_tp - 1 - i
        p = v - (inner - v + n_tp) // n_tp
        peers.append(p + side * (n_tp - 1 - 2 * p))
    pair = t + 1 - 2 * (t % 2)
    span = n_tp // 2
    across = (t + span) % n_tp
    diagonal = (pair + span) % n_tp
    places = [t, pair, across, diagonal]

    def zpeer(tt):
        return (g, c, tt)

    own_pair, far_pair = u * per, (1 - u) * per
    barrier = pltpu.get_barrier_semaphore()
    for tt in peers + [t]:
        for dc in reversed(range(n_ctx)):
            for core in (far_pair, own_pair):
                for dk in reversed(range(per)):
                    if tt is t and dc + dk == 0 and core is own_pair:
                        continue
                    pl.semaphore_signal(
                        barrier,
                        inc=1,
                        device_id=(core + (k + dk) % per, (c + dc) % n_ctx, tt),
                        device_id_type=MESH,
                    )

    loads = [
        pltpu.make_async_copy(src, w_buf.at[i], local_sem.at[0])
        for i, src in enumerate((wq_hbm, wk_hbm, wv_hbm))
    ]
    wo_load = pltpu.make_async_copy(wo_hbm, wo_buf, local_sem.at[1])
    own_lanes = pl.ds(pl.multiple_of(c * HD, HD), HD)
    other_lanes = pl.ds(pl.multiple_of(other * HD, HD), HD)
    cache_loads = [
        pltpu.make_async_copy(src.at[:, own_lanes], cache_buf.at[c, i], local_sem.at[2])
        for i, src in enumerate((ck_hbm, cv_hbm))
    ]
    small = [
        pltpu.make_async_copy(src, dst, local_sem.at[3])
        for i, (src, dst) in enumerate(
            [
                (state_hbm, state_ref),
                (clean_hbm, clean_ref),
                (ng_hbm, ng_ref),
                (mg_hbm, mg_ref),
                (og_hbm, og_ref),
                (levels_hbm, levels_ref),
                (noise_hbm, noise_ref),
                (place_hbm, place_ref),
                (mask_hbm, mask_ref),
            ]
        )
    ]
    for copy in small + [wo_load] + loads + cache_loads:
        copy.start()
    for copy in small:
        copy.wait()

    rows = jnp.concatenate(
        [state_ref[...].reshape(rows_count, width), clean_ref[...].astype(jnp.float32)], axis=0
    )
    ssq_own[...] = row_squares(rows, lanes)

    @pl.when(c == held)
    def _():
        ssq_buf[j] = ssq_own[...]

    modulation = mg_ref[...].reshape(1, width)
    gained = rows * ng_ref[...].reshape(1, width)
    for f in range(flight):
        sigma = levels_ref[noise_ref[f]]
        raw[f * ch : (f + 1) * ch] = gained[f * ch : (f + 1) * ch] * (1.0 + sigma * modulation)
    raw[rows_count:] = gained[rows_count:]
    line = lax.broadcasted_iota(jnp.int32, (8, SLOT), 0)
    for s in range(cache_dev // SLOT):
        block = jnp.zeros((8, SLOT), jnp.float32)
        for f in range(flight):
            hidden = jnp.where(mask_ref[f, place_ref[s]] != 0, 0.0, -jnp.inf)
            block = jnp.where(line == f, hidden, block)
        seen_buf[c, :, s * SLOT : (s + 1) * SLOT] = block
    pl.semaphore_wait(barrier, n_grp * n_ctx * n_tp - 1)

    def ssq_copy(target):
        return remote(ssq_own, ssq_buf.at[j], send.at[0], ssq_r.at[0], target)

    for dk in range(per):
        for dc in range(n_ctx):
            for dt in range(n_tp):
                copy = ssq_copy(
                    ((1 - c) * per + (k + dk) % per, (c + dc) % n_ctx, (t + dt) % n_tp)
                )
                if dk + dc + dt > 0:
                    copy.start()
                else:
                    pl.when(c != held)(copy.start)
    a_copy = remote(raw, raw_in, send.at[0], a_r.at[0], ((1 - c) * per + k, u, t))
    a_copy.start()
    wo_load.wait()
    for block in range(per * n_tp):
        wo_cut[block] = wo_buf[:, block * width : (block + 1) * width]
    wo_copy = remote(
        wo_cut.at[pl.ds((1 - k) * n_tp, n_tp)], wo_sib, send.at[0], wo_r.at[0], sibling
    )
    wo_copy.start()

    def ssq_wait(finish):
        @pl.when(c == held)
        def _():
            most = ssq_buf.at[: members - 1]
            finish(remote(most, most, send.at[0], ssq_r.at[0], partner))

        @pl.when(c != held)
        def _():
            finish(remote(ssq_buf, ssq_buf, send.at[0], ssq_r.at[0], partner))

    ssq_wait(lambda copy: copy.wait_recv())
    total = ssq_buf[0]
    for d in range(1, members):
        total = total + ssq_buf[d]
    inverse = lax.rsqrt(jnp.transpose(jnp.broadcast_to(total, (8, lanes)))[:all_rows, 0:1] / D + epsilon)
    a_copy.wait_recv()
    mine = k * n_tp + t
    h_buf[mine, held] = (raw_in[...] * inverse).astype(jnp.bfloat16)

    def slot_of(core, tt):
        return core * n_tp + tt

    def link(ref, send, recv, device):
        return remote(ref, ref, send, recv, device)

    def to_beside(x, tt):
        link(h_buf.at[slot_of(k, tt), x], send.at[0], n_r.at[tt], beside).start()

    def to_sibling(x, tt):
        link(h_buf.at[slot_of(k, tt), x], send.at[0], c_r.at[tt], sibling).start()

    def to_line(tt, device):
        link(h_buf.at[slot_of(k, tt), held], send.at[0], b_r.at[tt], device).start()

    to_beside(held, t)
    to_sibling(held, t)
    for tt in (across, pair):
        to_line(t, zpeer(tt))

    cache_copies = [
        remote(seen_buf.at[c], seen_buf.at[c], send.at[0], cache_r.at[0], partner)
    ] + [
        remote(
            src.at[:, other_lanes], cache_buf.at[c, i], send.at[0], cache_r.at[1], partner
        )
        for i, src in enumerate((ck_hbm, cv_hbm))
    ]
    for copy in cache_copies:
        copy.start()

    pltpu.make_async_copy(w_buf, w_buf, local_sem.at[0]).wait()

    def project(slots, w):
        total = None
        for slot in slots:
            lhs = h_buf[slot].reshape(total_rows, width)
            depth = pl.ds(pl.multiple_of(slot * width, 64), width)
            product = jnp.dot(lhs, w_buf[w, depth, :], preferred_element_type=jnp.float32)
            total = product if total is None else total + product
        return total

    def from_line(i):
        tt = places[i]
        link(h_buf.at[slot_of(k, tt), held], send.at[0], b_r.at[tt], partner).wait_recv()
        if i == 1:
            to_beside(held, tt)
        if i == 2:
            to_line(tt, zpeer(pair))
        to_sibling(held, tt)

    def from_beside(i):
        tt = places[i]
        link(h_buf.at[slot_of(k, tt), u], send.at[0], n_r.at[tt], beside).wait_recv()
        if i in (0, 2):
            place = across if i == 0 else pair
            link(h_buf.at[slot_of(k, tt), u], send.at[0], n_r.at[tt], zpeer(place)).start()
        to_sibling(u, tt)

    def from_sibling(i):
        tt = places[i]
        link(h_buf.at[slot_of(1 - k, tt)], send.at[0], c_r.at[tt], sibling).wait_recv()

    def add(slots, fresh=False):
        for w in range(3):
            acc[w] = project(slots, w) if fresh else acc[w] + project(slots, w)

    from_beside(0)
    from_line(2)
    from_line(1)
    from_sibling(0)
    add([slot_of(k, places[0]), slot_of(1 - k, places[0])], True)
    from_beside(2)
    from_beside(1)
    from_line(3)
    from_beside(3)
    from_sibling(1)
    from_sibling(2)
    add([slot_of(k, places[1]), slot_of(1 - k, places[1]), slot_of(k, places[2]), slot_of(1 - k, places[2]), slot_of(k, places[3])])
    from_sibling(3)
    part_copies = []
    for w in range(3):
        whole = acc[w] + project([slot_of(1 - k, places[3])], w)
        for head in range(n_ctx):
            piece = whole[:, head * HD : (head + 1) * HD]
            if w == 0:
                for x in range(n_ctx):
                    q_part[head, x * rows_count : (x + 1) * rows_count] = piece[
                        x * all_rows : x * all_rows + rows_count
                    ]
            else:
                kv_part[head, w - 1] = piece
                kv_send[head, w - 1] = piece.astype(jnp.bfloat16)
        if w == 0:
            copy = remote(q_part.at[other], q_in, send.at[0], p_r.at[0], partner)
        else:
            copy = remote(
                kv_send.at[other, w - 1], kv_in.at[w - 1], send.at[0], p_r.at[w], partner
            )
        copy.start()
        part_copies.append(copy)
    pltpu.make_async_copy(cache_buf.at[0], cache_buf.at[0], local_sem.at[2]).wait()
    cache_copies[0].wait_recv()
    both_caches = remote(
        cache_buf.at[0], cache_buf.at[0], send.at[0], cache_r.at[1], partner
    )
    both_caches.wait_recv()
    query_group = (lax.broadcasted_iota(jnp.int32, (queries, total_rows), 0) % rows_count) // ch
    key_group = (lax.broadcasted_iota(jnp.int32, (queries, total_rows), 1) % all_rows) // ch
    flight_seen = jnp.logical_or(key_group == flight, key_group <= query_group)

    part_copies[0].wait_recv()
    q = (q_part[c] + q_in[...]).astype(jnp.bfloat16)
    scale = 1.0 / math.sqrt(HD)

    def score(keys):
        return (
            lax.dot_general(q, keys, (((1,), (1,)), ((), ())), preferred_element_type=jnp.float32)
            * scale
        )

    scores = []
    for x in range(n_ctx):
        plain = score(cache_buf[x, 0])
        scores.append(
            jnp.concatenate(
                [
                    plain[b * ch : (b + 1) * ch] + seen_buf[x, b % flight : b % flight + 1]
                    for b in range(n_ctx * flight)
                ],
                axis=0,
            )
        )
    peak = jnp.max(jnp.maximum(scores[0], scores[1]), axis=1, keepdims=True)
    part_copies[1].wait_recv()
    key = (kv_part[c, 0] + kv_in[0].astype(jnp.float32)).astype(jnp.bfloat16)
    scores.append(jnp.where(flight_seen, score(key), -jnp.inf))
    peak = jnp.maximum(peak, jnp.max(scores[-1], axis=1, keepdims=True))
    weights = [jnp.exp(v - peak).astype(jnp.bfloat16) for v in scores]
    denom = sum(jnp.sum(w.astype(jnp.float32), axis=1, keepdims=True) for w in weights)
    numer = sum(
        jnp.dot(weights[x], cache_buf[x, 1], preferred_element_type=jnp.float32)
        for x in range(n_ctx)
    )
    part_copies[2].wait_recv()
    value = (kv_part[c, 1] + kv_in[1].astype(jnp.float32)).astype(jnp.bfloat16)
    numer = numer + jnp.dot(weights[-1], value, preferred_element_type=jnp.float32)
    attention = (numer / denom).astype(jnp.bfloat16)
    att_buf[k * n_ctx + c] = attention
    for device in (partner, (u * per + (1 - k), other, t), sibling):
        link(att_buf.at[k * n_ctx + c], send.at[0], t_r.at[0], device).start()

    for x in range(n_ctx):
        last = slice(x * all_rows + rows_count, (x + 1) * all_rows)
        kv_buf[x, 0] = key[last]
        kv_buf[x, 1] = value[last]
    fin_copy = remote(kv_buf.at[other], fin_in, send.at[0], f_r.at[0], partner)
    fin_copy.start()
    nk_ref[:, own_lanes] = kv_buf[c, 0]
    nv_ref[:, own_lanes] = kv_buf[c, 1]

    wo_copy.wait_recv()
    shared = att_buf.at[: per * n_ctx - 1]
    att_all = link(shared, send.at[0], t_r.at[0], partner)
    att_all.wait_recv()
    order = peers + [t]

    def heads_of(core):
        return jnp.concatenate([att_buf[core * n_ctx + x] for x in range(n_ctx)], axis=1)

    ours, theirs = heads_of(k), heads_of(1 - k)
    for i, tt in enumerate(order):
        y_part[i] = jnp.dot(
            ours, wo_cut[slot_of(k, tt)], preferred_element_type=jnp.float32
        ) + jnp.dot(theirs, wo_sib[tt], preferred_element_type=jnp.float32)

        def chunk(x, start, size):
            at = pl.ds(pl.multiple_of(x * rows_count + start, ch), size)
            return y_part[i, at, :]

        far_a[i] = chunk(other, 0, first).astype(jnp.bfloat16)
        remote(far_a.at[i], cross_a.at[tt, u], send.at[0], xa_r.at[tt], owner).start()
        near_a[i] = chunk(c, 0, first).astype(jnp.bfloat16)
        near = remote(near_a.at[i], cross_a.at[tt, u], send.at[0], xa_r.at[tt], beside)
        pl.when(jnp.logical_not(at_home))(near.start)

        if i < n_tp - 1:
            for x in range(n_ctx):
                zb_send[i, x] = chunk(x, first, late).astype(jnp.bfloat16)
            remote(zb_send.at[i], zb_in.at[t], send.at[0], zb_r.at[0], zpeer(tt)).start()

    fin_copy.wait_recv()
    nk_ref[:, other_lanes] = fin_in[0]
    nv_ref[:, other_lanes] = fin_in[1]

    def both_sources(ref, send, recv):
        @pl.when(at_home)
        def _():
            remote(ref.at[0], ref.at[0], send, recv, partner).wait_recv()

        @pl.when(jnp.logical_not(at_home))
        def _():
            remote(ref, ref, send, recv, partner).wait_recv()

    def from_across(i):
        tt = order[i]

        @pl.when(at_home)
        def _():
            cross_a[tt, u] = near_a[i]

        both_sources(cross_a.at[tt], send.at[0], xa_r.at[tt])
        return cross_a[tt, 0].astype(jnp.float32) + cross_a[tt, 1].astype(jnp.float32)

    for i in range(n_tp - 1):
        za_send[i] = from_across(i).astype(jnp.bfloat16)
        remote(za_send.at[i], za_in.at[t], send.at[0], za_r.at[0], zpeer(order[i])).start()

    link(zb_send, send.at[0], zb_r.at[0], partner).wait_recv()

    def gathered(x):
        at = pl.ds(pl.multiple_of(x * rows_count + first, ch), late)
        result = y_part[n_tp - 1, at, :]
        for tt in peers:
            result = result + zb_in[tt, x].astype(jnp.float32)
        return result.astype(jnp.bfloat16)

    far_b[...] = gathered(other)
    far_copy = remote(far_b, cross_b.at[u], send.at[0], xb_r.at[0], owner)
    far_copy.start()
    near_b[...] = gathered(c)
    near_copy = remote(near_b, cross_b.at[u], send.at[0], xb_r.at[0], beside)
    pl.when(jnp.logical_not(at_home))(near_copy.start)

    summed_a = from_across(n_tp - 1)
    link(za_send, send.at[0], za_r.at[0], partner).wait_recv()
    for tt in peers:
        summed_a = summed_a + za_in[tt].astype(jnp.float32)

    @pl.when(at_home)
    def _():
        cross_b[u] = near_b[...]

    both_sources(cross_b, send.at[0], xb_r.at[0])
    summed_b = cross_b[0].astype(jnp.float32) + cross_b[1].astype(jnp.float32)
    y_rows = jnp.concatenate([summed_a, summed_b], axis=0)
    ssy_buf[0] = row_squares(y_rows, lanes)
    for d in range(1, members):
        remote(
            ssy_buf.at[0], ssy_buf.at[d], send.at[0], ssy_r.at[0], member((j + d) % members)
        ).start()
    ssq_wait(lambda copy: copy.wait_send())
    slots = n_tp - 1
    for ref in (
        h_buf.at[:slots, 0],
        h_buf.at[: n_tp // n_ctx],
        h_buf.at[:n_tp],
        kv_send.at[0],
        shared,
        far_a,
        za_send,
        zb_send,
    ):
        link(ref, send.at[0], send.at[0], partner).wait_send()
    for copy in [a_copy, cache_copies[0], both_caches, part_copies[0], wo_copy, fin_copy, far_copy]:
        copy.wait_send()

    @pl.when(jnp.logical_not(at_home))
    def _():
        link(near_a, send.at[0], send.at[0], partner).wait_send()
        near_copy.wait_send()

    gained = y_rows * og_ref[...].reshape(1, width)
    moves = []
    for f in range(flight):
        now = levels_ref[noise_ref[f]]
        after = levels_ref[noise_ref[f] + 1]
        moves.append((after - now) * gained[f * ch : (f + 1) * ch])
    rest = ssy_buf.at[1:]
    ssy_all = remote(rest, rest, send.at[0], ssy_r.at[0], partner)
    ssy_all.wait_recv()
    total = ssy_buf[0]
    for d in range(1, members):
        total = total + ssy_buf[d]
    inverse = lax.rsqrt(jnp.transpose(jnp.broadcast_to(total, (8, lanes)))[:rows_count, 0:1] / D + epsilon)
    for f in range(flight):
        out_ref[f] = state_ref[f] + moves[f] * inverse[f * ch : (f + 1) * ch]
    ssy_all.wait_send()


def y_rows_first(rows_count):
    return 3 * (rows_count // 4)


def write_out(*refs):
    sems = refs[6]
    copies = [pltpu.make_async_copy(refs[i], refs[3 + i], sems.at[i]) for i in range(3)]
    for copy in copies:
        copy.start()
    for copy in copies:
        copy.wait()


def fused(dims, *args):
    state, clean_tokens, w_query = args[0], args[1], args[2]
    w_out, cache_keys = args[5], args[6]
    n_grp, n_ctx, n_tp = dims
    per = n_grp // n_ctx
    members = n_grp * n_tp
    flight, ch, width = state.shape
    rows_count = flight * ch
    first = y_rows_first(rows_count)
    late = rows_count - first
    all_rows = rows_count + ch
    total = n_ctx * all_rows
    lanes = -(-all_rows // 128) * 128
    queries = n_ctx * rows_count
    cache_dev = cache_keys.shape[0]
    bf, fl = jnp.bfloat16, jnp.float32
    dma = pltpu.SemaphoreType.DMA
    vm = pl.BlockSpec(memory_space=pltpu.VMEM)
    hbm = pl.BlockSpec(memory_space=pltpu.HBM)

    scratch = [
        pltpu.VMEM(state.shape, fl),
        pltpu.VMEM(clean_tokens.shape, bf),
        pltpu.VMEM((width,), fl),
        pltpu.VMEM((width,), fl),
        pltpu.VMEM((width,), fl),
        *[pltpu.SMEM(a.shape, a.dtype) for a in args[11:]],
        pltpu.VMEM((3,) + w_query.shape, bf),
        pltpu.VMEM(w_out.shape, bf),
        pltpu.VMEM((per * n_tp, w_out.shape[0], width), bf),
        pltpu.VMEM((n_tp, w_out.shape[0], width), bf),
        pltpu.VMEM((n_ctx, 2, cache_dev, HD), bf),
        pltpu.VMEM((n_ctx, 8, cache_dev), fl),
        pltpu.VMEM((1, lanes), fl),
        pltpu.VMEM((members, 1, lanes), fl),
        pltpu.VMEM((members, 1, lanes), fl),
        pltpu.VMEM((all_rows, width), fl),
        pltpu.VMEM((all_rows, width), fl),
        pltpu.VMEM((per * n_tp, n_ctx, all_rows, width), bf),
        pltpu.VMEM((3, total, n_ctx * HD), fl),
        pltpu.VMEM((n_ctx, queries, HD), fl),
        pltpu.VMEM((queries, HD), fl),
        pltpu.VMEM((n_ctx, 2, total, HD), fl),
        pltpu.VMEM((n_ctx, 2, total, HD), bf),
        pltpu.VMEM((2, total, HD), bf),
        pltpu.VMEM((n_ctx, 2, ch, HD), bf),
        pltpu.VMEM((2, ch, HD), bf),
        pltpu.VMEM((per * n_ctx, queries, HD), bf),
        pltpu.VMEM((n_tp, queries, width), fl),
        pltpu.VMEM((n_tp, first, width), bf),
        pltpu.VMEM((n_tp, first, width), bf),
        pltpu.VMEM((n_tp, n_ctx, first, width), bf),
        pltpu.VMEM((n_tp - 1, first, width), bf),
        pltpu.VMEM((n_tp, first, width), bf),
        pltpu.VMEM((n_tp - 1, n_ctx, late, width), bf),
        pltpu.VMEM((n_tp, n_ctx, late, width), bf),
        pltpu.VMEM((late, width), bf),
        pltpu.VMEM((late, width), bf),
        pltpu.VMEM((n_ctx, late, width), bf),
        dma((4,)),
        dma((1,)),
        dma((2,)),
        dma((1,)),
        dma((1,)),
        dma((n_tp,)),
        dma((n_tp,)),
        dma((n_tp,)),
        dma((3,)),
        dma((1,)),
        dma((1,)),
        dma((1,)),
        dma((n_tp,)),
        dma((1,)),
        dma((1,)),
        dma((1,)),
        dma((1,)),
    ]
    results = pl.pallas_call(
        functools.partial(kernel, dims),
        out_shape=(
            pltpu.VMEM(state.shape, fl),
            pltpu.VMEM((ch, cache_keys.shape[1]), bf),
            pltpu.VMEM((ch, cache_keys.shape[1]), bf),
        ),
        in_specs=[hbm] * 15,
        out_specs=(vm, vm, vm),
        scratch_shapes=scratch,
        compiler_params=pltpu.CompilerParams(
            collective_id=0, has_side_effects=True, vmem_limit_bytes=VMEM_LIMIT
        ),
    )(*args)
    return pl.pallas_call(
        write_out,
        out_shape=tuple(jax.ShapeDtypeStruct(r.shape, r.dtype) for r in results),
        in_specs=[vm] * 3,
        out_specs=(hbm,) * 3,
        scratch_shapes=[dma((3,))],
    )(*[pltpu.with_memory_space_constraint(r, pltpu.VMEM) for r in results])


def step(dims, *args):
    n_grp, n_ctx, n_tp = dims
    heads_dev = args[6].shape[1] // HD
    if n_ctx == heads_dev == 2 and n_grp == n_tp == 4 and args[0].shape[0] == 4:
        return fused(dims, *args)
    return local(*args)


def solution(mesh):
    dims = tuple(mesh.shape[name] for name in ("grp", "ctx", "tp"))
    return jax.shard_map(
        functools.partial(step, dims),
        mesh=mesh,
        in_specs=(
            P(None, "ctx", ("grp", "tp")),
            P("ctx", ("grp", "tp")),
            P("ctx", ("grp", "tp")),
            P("ctx", ("grp", "tp")),
            P("ctx", ("grp", "tp")),
            P(("grp", "tp"), "ctx"),
            P("ctx", ("grp", "tp")),
            P("ctx", ("grp", "tp")),
            P(("grp", "tp")),
            P(("grp", "tp")),
            P(("grp", "tp")),
            P(),
            P(),
            P("ctx"),
            P(),
        ),
        out_specs=(P(None, "ctx", ("grp", "tp")), P("ctx", ("grp", "tp")), P("ctx", ("grp", "tp"))),
        check_vma=False,
    )
```
